32 devices in a mesh: wide: 16 (over z, y, core), narrow: 2 (over x).
Axes of the slice: x: 2, y: 2, z: 4, core: 2. Of those that a mesh axis runs over, the one named last changes fastest.
Arguments:
- inputs: bfloat16 [18464, 1024], P('wide', 'narrow'), may hold values from -6 to 6
- counts: int32 [16], P('wide'), may hold values from 1 to 2, as said below
- ln1_gain: float32 [1024], P('narrow'), may hold values from 0.5 to 1.5
- ln1_bias: float32 [1024], P('narrow'), may hold values from -3 to 3
- w_qkv: bfloat16 [1024, 3072], P('wide', 'narrow'), may hold values from -2 to 2
- qv_bias: float32 [2048], P('narrow'), may hold values from -3 to 3
- w_proj: bfloat16 [1024, 1024], P('narrow', 'wide'), may hold values from -1.5 to 1.5
- proj_bias: float32 [1024], P('narrow'), may hold values from -3 to 3
- ln2_gain: float32 [1024], P('narrow'), may hold values from 0.5 to 1.5
- ln2_bias: float32 [1024], P('narrow'), may hold values from -3 to 3
- w_fc1: bfloat16 [1024, 4096], P('wide', 'narrow'), may hold values from -0.1875 to 0.1875
- fc1_bias: float32 [4096], P('narrow'), may hold values from -3 to 3
- w_fc2: bfloat16 [4096, 1024], P('narrow', 'wide'), may hold values from -0.09375 to 0.09375
- fc2_bias: float32 [1024], P('narrow'), may hold values from -3 to 3
- cotangent: bfloat16 [18464, 1024], P('wide', 'narrow'), may hold values from -6 to 6
Outputs:
- output: bfloat16 [18464, 1024], P('wide', 'narrow')
- grad_in: bfloat16 [18464, 1024], P('wide', 'narrow')
- grad_ln1_gain: float32 [1024], P('narrow')
- grad_ln1_bias: float32 [1024], P('narrow')
- grad_w_qkv: float32 [1024, 3072], P('wide', 'narrow')
- grad_qv_bias: float32 [2048], P('narrow')
- grad_w_proj: float32 [1024, 1024], P('narrow', 'wide')
- grad_proj_bias: float32 [1024], P('narrow')
- grad_ln2_gain: float32 [1024], P('narrow')
- grad_ln2_bias: float32 [1024], P('narrow')
- grad_w_fc1: float32 [1024, 4096], P('wide', 'narrow')
- grad_fc1_bias: float32 [4096], P('narrow')
- grad_w_fc2: float32 [4096, 1024], P('narrow', 'wide')
- grad_fc2_bias: float32 [1024], P('narrow')
The draws below stay inside these ranges and needn't reach their ends.
Inputs may be any that keep to these rules, and one draw needn't show every extreme that they name: `counts`: each group's images fill its first slots; some group holds 2 images and some holds 1.
All inputs are finite; a program needn't handle non-finite values.
Results may differ from the reference program's by a relative error of at most 0.015.
The reference program's roundings to bfloat16 on the way count: a program that leaves them out, or rounds other values in their place, can miss the bound.
Values may be sent and summed in bfloat16 or wider, within the bound.
A program may use at most 192 MiB of HBM per device.

```python
import math
import jax
import jax.numpy as jnp
from jax import lax

D = 1024
H = 16
DH = 64
FF = 4096
SEQ = 577
IMG_SLOTS = 2
GROUPS = 16
ROWS = 1154
TOKENS = 18464


def draw_counts(key, part):
    drop = jax.random.randint(jax.random.fold_in(key, 1), (GROUPS,), 0, 2)
    counts_drawn = IMG_SLOTS - drop
    first = jax.random.randint(jax.random.fold_in(key, 2), (), 0, GROUPS)
    offset = jax.random.randint(jax.random.fold_in(key, 3), (), 1, GROUPS)
    second = (first + offset) % GROUPS
    counts_drawn = counts_drawn.at[first].set(IMG_SLOTS)
    counts_drawn = counts_drawn.at[second].set(IMG_SLOTS - 1)
    return counts_drawn.astype(jnp.int32)


def draw_w_qkv(key, part):
    base_draw = jax.random.normal(jax.random.fold_in(key, 11), (D, H, 3, DH), jnp.float32)
    base_draw = jnp.clip(base_draw, -6.0, 6.0) / math.sqrt(D)
    return base_draw.reshape(D, 3 * D).astype(jnp.bfloat16)


def block_scale(key, extent, pieces, least, high):
    loudness, own = 1.0, jax.random.fold_in(key, 6)
    for position, shards_of in pieces:
        draws = jnp.exp(jax.random.uniform(jax.random.fold_in(own, position), (shards_of,), jnp.float32, least / len(pieces), high / len(pieces)))
        loudness = loudness * jnp.repeat(draws, extent[position] // shards_of).reshape([-1 if axis == position else 1 for axis in range(len(extent))])
    return loudness


def centred(key, shape, scale, most, shards=(), dtype=jnp.bfloat16):
    drawn = scale * jax.random.normal(key, shape, jnp.float32)
    if shards:
        drawn = drawn * block_scale(key, shape, shards, -0.22, 0.18)
    return jnp.clip(drawn, -most, most).astype(dtype)


def setup_inputs(seed: int = 0) -> dict:
    seeds = jax.random.split(jax.random.key(seed), 16)
    return {
        "inputs": centred(seeds[0], (TOKENS, D), 1.0, 6.0, ((0, 16), (1, 2))),
        "counts": draw_counts(jax.random.fold_in(seeds[15], 71), 0),
        "ln1_gain": jnp.clip(1.0 + 0.1 * jax.random.normal(seeds[2], (D,), jnp.float32), 0.5, 1.5),
        "ln1_bias": centred(seeds[3], (D,), 0.5, 3.0, ((0, 2),), jnp.float32),
        "w_qkv": draw_w_qkv(jax.random.fold_in(seeds[15], 71), 0),
        "qv_bias": centred(seeds[5], (2 * D,), 0.5, 3.0, ((0, 2),), jnp.float32),
        "w_proj": centred(seeds[6], (D, D), (D // 64) ** -0.5, 1.5, ((0, 2), (1, 16))),
        "proj_bias": centred(seeds[7], (D,), 0.5, 3.0, ((0, 2),), jnp.float32),
        "ln2_gain": jnp.clip(1.0 + 0.1 * jax.random.normal(seeds[8], (D,), jnp.float32), 0.5, 1.5),
        "ln2_bias": centred(seeds[9], (D,), 0.5, 3.0, ((0, 2),), jnp.float32),
        "w_fc1": centred(seeds[10], (D, FF), D ** -0.5, 0.1875, ((0, 16), (1, 2))),
        "fc1_bias": centred(seeds[11], (FF,), 0.5, 3.0, ((0, 2),), jnp.float32),
        "w_fc2": centred(seeds[12], (FF, D), FF ** -0.5, 0.09375, ((0, 2), (1, 16))),
        "fc2_bias": centred(seeds[13], (D,), 0.5, 3.0, ((0, 2),), jnp.float32),
        "cotangent": centred(seeds[14], (TOKENS, D), 1.0, 6.0, ((0, 16), (1, 2))),
    }


norm_eps = 1e-06

def normal_cdf(values_in):
    return 0.5 * (1.0 + lax.erf(values_in * (1.0 / math.sqrt(2.0))))

def gelu_exact(values_in):
    return values_in * normal_cdf(values_in)

def gelu_slope(values_in):
    return normal_cdf(values_in) + values_in * jnp.exp(-0.5 * values_in * values_in) * (1.0 / math.sqrt(2.0 * math.pi))

def norm_forward(rows_in, gain_vec, shift_vec):
    center = lax.optimization_barrier(jnp.sum(rows_in, axis=1)) / D
    spread = lax.optimization_barrier(jnp.sum(rows_in * rows_in, axis=1)) / D - center * center
    inv_std = lax.rsqrt(spread + norm_eps)
    normalized = (rows_in - center[:, None]) * inv_std[:, None]
    return (normalized, inv_std, (normalized * gain_vec + shift_vec).astype(jnp.bfloat16))

def norm_backward(incoming, normalized, inv_std, gain_vec):
    scaled = incoming * gain_vec
    first_sum = lax.optimization_barrier(jnp.sum(scaled, axis=1))
    second_sum = lax.optimization_barrier(jnp.sum(scaled * normalized, axis=1))
    back = inv_std[:, None] * (scaled - first_sum[:, None] / D - normalized * (second_sum[:, None] / D))
    return (back, lax.optimization_barrier(jnp.sum(incoming * normalized, axis=0)), lax.optimization_barrier(jnp.sum(incoming, axis=0)))

def ein_float(form, left_mat, right_mat):
    return jnp.einsum(form, left_mat.astype(jnp.float32), right_mat.astype(jnp.float32))

def group_pass(params, group_rows, group_cot, count_live):
    ln1_gain, ln1_bias, w_qkv, qv_bias, w_proj, proj_bias, ln2_gain, ln2_bias, w_fc1, fc1_bias, w_fc2, fc2_bias = params
    slot_count = ROWS // SEQ
    score_scale = 1.0 / math.sqrt(DH)
    slot_of_row = lax.broadcasted_iota(jnp.int32, (ROWS, 1), 0) // SEQ
    live_rows = (slot_of_row < count_live).astype(jnp.float32)
    resid = group_rows.astype(jnp.float32)
    hat_one, inv_one, normed1 = norm_forward(resid, ln1_gain, ln1_bias)
    bias_qv = qv_bias.reshape(H, 2, DH)
    bias_full = jnp.stack([bias_qv[:, 0], jnp.zeros_like(bias_qv[:, 0]), bias_qv[:, 1]], axis=1)
    qkv_rows = jnp.dot(normed1, w_qkv, preferred_element_type=jnp.float32).reshape(ROWS, H, 3, DH) + bias_full
    qkv_rows = qkv_rows.astype(jnp.bfloat16).reshape(slot_count, SEQ, H, 3, DH)
    queries = qkv_rows[:, :, :, 0]
    key_rows = qkv_rows[:, :, :, 1]
    value_rows = qkv_rows[:, :, :, 2]
    scores = ein_float('sqhd,skhd->shqk', queries, key_rows) * score_scale
    row_max = lax.optimization_barrier(jnp.max(scores, axis=-1, keepdims=True))
    exp_scores = jnp.exp(scores - row_max)
    row_total = lax.optimization_barrier(jnp.sum(exp_scores, axis=-1, keepdims=True))
    probs_bf = (exp_scores / row_total).astype(jnp.bfloat16)
    logsum = (row_max + jnp.log(row_total))[..., 0]
    mixed_out = ein_float('shqk,skhd->sqhd', probs_bf, value_rows).astype(jnp.bfloat16)
    mixed_rows = mixed_out.reshape(ROWS, D)
    attn_out = jnp.dot(mixed_rows, w_proj, preferred_element_type=jnp.float32) + proj_bias
    resid_mid = resid + live_rows * attn_out
    hat_two, inv_two, normed2 = norm_forward(resid_mid, ln2_gain, ln2_bias)
    inner_pre = jnp.dot(normed2, w_fc1, preferred_element_type=jnp.float32) + fc1_bias
    activation = gelu_exact(inner_pre).astype(jnp.bfloat16)
    mlp_out = jnp.dot(activation, w_fc2, preferred_element_type=jnp.float32) + fc2_bias
    output = (resid_mid + live_rows * mlp_out).astype(jnp.bfloat16)
    grad_out = group_cot.astype(jnp.float32)
    masked2 = live_rows * grad_out
    sent2 = masked2.astype(jnp.bfloat16)
    grad_w_fc2 = jnp.dot(activation.T, sent2, preferred_element_type=jnp.float32)
    d_inner = jnp.dot(sent2, w_fc2.T, preferred_element_type=jnp.float32) * gelu_slope(inner_pre)
    d_inner_b = d_inner.astype(jnp.bfloat16)
    grad_w_fc1 = jnp.dot(normed2.T, d_inner_b, preferred_element_type=jnp.float32)
    d_norm2 = jnp.dot(d_inner_b, w_fc1.T, preferred_element_type=jnp.float32)
    back_two, grad_ln2_gain, grad_ln2_bias = norm_backward(d_norm2, hat_two, inv_two, ln2_gain)
    d_mid = grad_out + back_two
    masked1 = live_rows * d_mid
    sent1 = masked1.astype(jnp.bfloat16)
    grad_w_proj = jnp.dot(mixed_rows.T, sent1, preferred_element_type=jnp.float32)
    d_mixed = jnp.dot(sent1, w_proj.T, preferred_element_type=jnp.float32).astype(jnp.bfloat16)
    d_mixed = d_mixed.reshape(slot_count, SEQ, H, DH)
    scores_re = ein_float('sqhd,skhd->shqk', queries, key_rows) * score_scale
    probs_re = jnp.exp(scores_re - logsum[..., None])
    d_probs = ein_float('sqhd,skhd->shqk', d_mixed, value_rows)
    row_delta = lax.optimization_barrier(jnp.sum(d_mixed.astype(jnp.float32) * mixed_out.astype(jnp.float32), axis=-1))
    row_delta = jnp.transpose(row_delta, (0, 2, 1))
    d_scores = (probs_re * (d_probs - row_delta[..., None])).astype(jnp.bfloat16)
    d_query = ein_float('shqk,skhd->sqhd', d_scores, key_rows) * score_scale
    d_keys = ein_float('shqk,sqhd->skhd', d_scores, queries) * score_scale
    d_values = ein_float('shqk,sqhd->skhd', probs_re.astype(jnp.bfloat16), d_mixed)
    d_qkv = jnp.stack([d_query, d_keys, d_values], axis=3).reshape(ROWS, 3 * D)
    grad_qv_bias = jnp.stack([lax.optimization_barrier(jnp.sum(d_query, axis=(0, 1))), lax.optimization_barrier(jnp.sum(d_values, axis=(0, 1)))], axis=1).reshape(2 * D)
    d_qkv_b = d_qkv.astype(jnp.bfloat16)
    grad_w_qkv = jnp.dot(normed1.T, d_qkv_b, preferred_element_type=jnp.float32)
    d_norm1 = jnp.dot(d_qkv_b, w_qkv.T, preferred_element_type=jnp.float32)
    back_one, grad_ln1_gain, grad_ln1_bias = norm_backward(d_norm1, hat_one, inv_one, ln1_gain)
    grad_in = (d_mid + back_one).astype(jnp.bfloat16)
    grads = (grad_ln1_gain, grad_ln1_bias, grad_w_qkv, grad_qv_bias, grad_w_proj, lax.optimization_barrier(jnp.sum(masked1, axis=0)), grad_ln2_gain, grad_ln2_bias, grad_w_fc1, lax.optimization_barrier(jnp.sum(d_inner, axis=0)), grad_w_fc2, lax.optimization_barrier(jnp.sum(masked2, axis=0)))
    return ((output, grad_in), grads)

def reference(inputs, counts, ln1_gain, ln1_bias, w_qkv, qv_bias, w_proj, proj_bias, ln2_gain, ln2_bias, w_fc1, fc1_bias, w_fc2, fc2_bias, cotangent):
    params = (ln1_gain, ln1_bias, w_qkv, qv_bias, w_proj, proj_bias, ln2_gain, ln2_bias, w_fc1, fc1_bias, w_fc2, fc2_bias)
    input_groups = inputs.reshape(GROUPS, ROWS, D)
    cot_groups = cotangent.reshape(GROUPS, ROWS, D)

    def group_step(running, scan_item):
        group_rows, group_cot, count_live = scan_item
        outs_pair, grads = group_pass(params, group_rows, group_cot, count_live)
        return (jax.tree.map(lambda first, second: first + second, running, grads), outs_pair)
    zeros_init = tuple((jnp.zeros(param.shape, jnp.float32) for param in params))
    running, (outputs, grads_in) = lax.scan(group_step, zeros_init, (input_groups, cot_groups, counts))
    return (outputs.reshape(TOKENS, D), grads_in.reshape(TOKENS, D), running[0], running[1], running[2], running[3], running[4], running[5], running[6], running[7], running[8], running[9], running[10], running[11])
```

```python
import functools
import math

import jax
import jax.numpy as jnp
from jax import lax
from jax.experimental import pallas as pl
from jax.experimental.pallas import tpu as pltpu
from jax.sharding import PartitionSpec as P

DH = 64
SEQ = 577
ROW_TILE = 16


norm_eps = 1e-06
NT = (((1,), (1,)), ((), ()))
TN = (((0,), (0,)), ((), ()))
NN = (((1,), (0,)), ((), ()))


def dot_f32(left_mat, right_mat, dims=NN):
    return lax.dot_general(left_mat, right_mat, dims, preferred_element_type=jnp.float32)


def swap(piece):
    return lax.ppermute(piece, "narrow", ((0, 1), (1, 0)))


def widen(piece, me, size):
    if size != 2:
        return lax.all_gather(piece, "narrow", axis=1, tiled=True)
    other = swap(piece)
    return jnp.concatenate(
        [jnp.where(me == 0, piece, other), jnp.where(me == 0, other, piece)], axis=1
    )


def sum_whole(partial_rows, size):
    if size != 2:
        return lax.psum(partial_rows, "narrow")
    mine = partial_rows.astype(jnp.bfloat16)
    return mine.astype(jnp.float32) + swap(mine).astype(jnp.float32)


def sum_own(left_mat, right_rows, me, size, width):
    if size != 2:
        return lax.psum_scatter(
            dot_f32(left_mat, right_rows, NT), "narrow", scatter_dimension=1, tiled=True
        )
    theirs = lax.dynamic_slice_in_dim(right_rows, (1 - me) * width, width, 0)
    ours = lax.dynamic_slice_in_dim(right_rows, me * width, width, 0)
    moved = swap(dot_f32(left_mat, theirs, NT).astype(jnp.bfloat16))
    return dot_f32(left_mat, ours, NT) + moved.astype(jnp.float32)


def normal_cdf(values_in):
    return 0.5 * (1.0 + lax.erf(values_in * (1.0 / math.sqrt(2.0))))


def gelu_exact(values_in):
    return values_in * normal_cdf(values_in)


def gelu_slope(values_in):
    return normal_cdf(values_in) + values_in * jnp.exp(-0.5 * values_in * values_in) * (
        1.0 / math.sqrt(2.0 * math.pi)
    )


def norm_forward(rows_in, gain_vec, shift_vec):
    width = float(rows_in.shape[1])
    center = jnp.sum(rows_in, axis=1, keepdims=True) / width
    spread = jnp.sum(rows_in * rows_in, axis=1, keepdims=True) / width - center * center
    inv_std = lax.rsqrt(spread + norm_eps)
    normalized = (rows_in - center) * inv_std
    return (normalized, inv_std, (normalized * gain_vec + shift_vec).astype(jnp.bfloat16))


def scores_by_key(queries, key_rows, score_scale):
    scores = dot_f32(key_rows, queries, NT) * score_scale
    key_index = lax.broadcasted_iota(jnp.int32, scores.shape, 0)
    return jnp.where(key_index < SEQ, scores, -1e30)


def attend_kernel(qkv_ref, mixed_ref, logsum_ref, *, heads, score_scale):
    for head in range(heads):
        base = head * 3 * DH
        queries = qkv_ref[:, base : base + DH]
        key_rows = qkv_ref[:, base + DH : base + 2 * DH]
        value_rows = qkv_ref[:, base + 2 * DH : base + 3 * DH]
        scores = scores_by_key(queries, key_rows, score_scale)
        top = jnp.max(scores, axis=0, keepdims=True)
        exp_scores = jnp.exp(scores - top)
        total = jnp.sum(exp_scores, axis=0, keepdims=True)
        probs = (exp_scores * (1.0 / total)).astype(jnp.bfloat16)
        mixed_ref[:, head * DH : (head + 1) * DH] = dot_f32(probs, value_rows, TN).astype(
            jnp.bfloat16
        )
        logsum_ref[0, head : head + 1, :] = top + jnp.log(total)


def attend_back_kernel(
    qkv_ref, mixed_ref, d_mixed_ref, logsum_ref, d_qkv_ref, sums_ref, *, heads, score_scale
):
    for head in range(heads):
        base = head * 3 * DH
        queries = qkv_ref[:, base : base + DH]
        key_rows = qkv_ref[:, base + DH : base + 2 * DH]
        value_rows = qkv_ref[:, base + 2 * DH : base + 3 * DH]
        mixed = mixed_ref[:, head * DH : (head + 1) * DH]
        d_mixed = d_mixed_ref[:, head * DH : (head + 1) * DH]
        products = d_mixed.astype(jnp.float32) * mixed.astype(jnp.float32)
        delta = jnp.sum(jnp.transpose(products), axis=0, keepdims=True)
        scores = scores_by_key(queries, key_rows, score_scale)
        probs = jnp.exp(scores - logsum_ref[0, head : head + 1, :])
        d_probs = dot_f32(value_rows, d_mixed, NT)
        d_scores = (probs * (d_probs - delta)).astype(jnp.bfloat16)
        d_query = dot_f32(d_scores, key_rows, TN) * score_scale
        d_keys = dot_f32(d_scores, queries, NN) * score_scale
        d_values = dot_f32(probs.astype(jnp.bfloat16), d_mixed, NN)
        for part, grad in enumerate((d_query, d_keys, d_values)):
            columns = slice(base + part * DH, base + (part + 1) * DH)
            d_qkv_ref[:, columns] = grad.astype(jnp.bfloat16)
            sums_ref[0, :, columns] = jnp.broadcast_to(
                jnp.sum(grad, axis=0, keepdims=True), (8, DH)
            )


def head_pairs(width):
    heads = 2
    return heads, width // (3 * DH * heads)


def attend(qkv_rows, slot_rows, score_scale):
    row_count, width = qkv_rows.shape
    slots = row_count // slot_rows
    heads, pairs = head_pairs(width)
    return pl.pallas_call(
        functools.partial(attend_kernel, heads=heads, score_scale=score_scale),
        grid=(slots, pairs),
        in_specs=[pl.BlockSpec((slot_rows, heads * 3 * DH), lambda s, p: (s, p))],
        out_specs=[
            pl.BlockSpec((slot_rows, heads * DH), lambda s, p: (s, p)),
            pl.BlockSpec((1, 8, slot_rows), lambda s, p: (s * pairs + p, 0, 0)),
        ],
        out_shape=[
            jax.ShapeDtypeStruct((row_count, width // 3), jnp.bfloat16),
            jax.ShapeDtypeStruct((slots * pairs, 8, slot_rows), jnp.float32),
        ],
        cost_estimate=pl.CostEstimate(
            flops=4 * slots * pairs * heads * slot_rows * slot_rows * 256,
            bytes_accessed=row_count * width * 3,
            transcendentals=slots * pairs * heads * slot_rows * slot_rows,
        ),
        name="attend",
    )(qkv_rows)


def attend_backward(qkv_rows, mixed_rows, d_mixed, logsum, slot_rows, score_scale):
    row_count, width = qkv_rows.shape
    slots = row_count // slot_rows
    heads, pairs = head_pairs(width)
    narrow_block = pl.BlockSpec((slot_rows, heads * DH), lambda s, p: (s, p))
    wide_block = pl.BlockSpec((slot_rows, heads * 3 * DH), lambda s, p: (s, p))
    return pl.pallas_call(
        functools.partial(attend_back_kernel, heads=heads, score_scale=score_scale),
        grid=(slots, pairs),
        in_specs=[
            wide_block,
            narrow_block,
            narrow_block,
            pl.BlockSpec((1, 8, slot_rows), lambda s, p: (s * pairs + p, 0, 0)),
        ],
        out_specs=[
            wide_block,
            pl.BlockSpec((1, 8, heads * 3 * DH), lambda s, p: (s, 0, p)),
        ],
        out_shape=[
            jax.ShapeDtypeStruct((row_count, width), jnp.bfloat16),
            jax.ShapeDtypeStruct((slots, 8, width), jnp.float32),
        ],
        cost_estimate=pl.CostEstimate(
            flops=10 * slots * pairs * heads * slot_rows * slot_rows * 256,
            bytes_accessed=row_count * width * 6,
            transcendentals=slots * pairs * heads * slot_rows * slot_rows,
        ),
        name="attend_back",
    )(qkv_rows, mixed_rows, d_mixed, logsum)


def shards_any(
    inputs,
    counts,
    ln1_gain,
    ln1_bias,
    w_qkv,
    qv_bias,
    w_proj,
    proj_bias,
    ln2_gain,
    ln2_bias,
    w_fc1,
    fc1_bias,
    w_fc2,
    fc2_bias,
    cotangent,
):
    size = lax.axis_size("narrow")
    me = lax.axis_index("narrow")
    row_count, width = inputs.shape
    slot_count = row_count // SEQ
    slot_rows = -(-SEQ // ROW_TILE) * ROW_TILE
    padded = slot_count * slot_rows
    head_count = w_qkv.shape[1] // (3 * DH)
    score_scale = 1.0 / math.sqrt(DH)

    def pad_rows(rows):
        rows = rows.reshape(slot_count, SEQ, rows.shape[1])
        rows = jnp.pad(rows, ((0, 0), (0, slot_rows - SEQ), (0, 0)))
        return rows.reshape(padded, rows.shape[2])

    def trim_rows(rows):
        rows = rows.reshape(slot_count, slot_rows, rows.shape[1])[:, :SEQ]
        return rows.reshape(row_count, rows.shape[2])

    def own(rows):
        return lax.dynamic_slice_in_dim(rows, me * width, width, rows.ndim - 1)

    padded_index = lax.broadcasted_iota(jnp.int32, (padded, 1), 0)
    live_rows = (
        (padded_index // slot_rows < counts[0]) & (padded_index % slot_rows < SEQ)
    ).astype(jnp.float32)

    early = lax.all_gather(
        jnp.concatenate([w_qkv, w_proj.T], axis=1), "wide", axis=0, tiled=True
    )
    wqkv_full = early[:, : w_qkv.shape[1]]
    wproj_t = early[:, w_qkv.shape[1] :]
    late = lax.all_gather(
        jnp.concatenate([w_fc1, w_fc2.T], axis=1), "wide", axis=0, tiled=True
    )
    wfc1_full = late[:, : w_fc1.shape[1]]
    wfc2_t = late[:, w_fc1.shape[1] :]

    vectors = widen(
        jnp.stack([ln1_gain, ln1_bias, ln2_gain, ln2_bias, proj_bias]), me, size
    )
    gain_one, shift_one, gain_two, shift_two, proj_shift = (vectors[i : i + 1] for i in range(5))

    inputs_whole = widen(pad_rows(inputs), me, size)
    sent2 = widen((live_rows * pad_rows(cotangent).astype(jnp.float32)).astype(jnp.bfloat16), me, size)

    resid = inputs_whole.astype(jnp.float32)
    hat_one, inv_one, normed1 = norm_forward(resid, gain_one, shift_one)
    bias_qv = qv_bias.reshape(head_count, 2, DH)
    bias_full = jnp.stack(
        [bias_qv[:, 0], jnp.zeros_like(bias_qv[:, 0]), bias_qv[:, 1]], axis=1
    ).reshape(1, head_count * 3 * DH)
    qkv_rows = (dot_f32(normed1, wqkv_full) + bias_full).astype(jnp.bfloat16)
    qkv_rows, sent2 = lax.optimization_barrier((qkv_rows, sent2))
    mixed_rows, logsum = attend(qkv_rows, slot_rows, score_scale)
    attn_out = sum_whole(dot_f32(mixed_rows, wproj_t, NT), size) + proj_shift
    resid_mid = resid + live_rows * attn_out
    hat_two, inv_two, normed2 = norm_forward(resid_mid, gain_two, shift_two)
    inner_pre = dot_f32(normed2, wfc1_full) + fc1_bias
    activation = gelu_exact(inner_pre).astype(jnp.bfloat16)

    d_inner = dot_f32(sent2, wfc2_t) * gelu_slope(inner_pre)
    d_inner_b = d_inner.astype(jnp.bfloat16)
    d_norm2 = sum_whole(dot_f32(d_inner_b, wfc1_full, NT), size)
    grad_fc = jnp.concatenate(
        [
            dot_f32(normed2, d_inner_b, TN).astype(jnp.bfloat16),
            dot_f32(sent2, activation, TN).astype(jnp.bfloat16),
        ],
        axis=1,
    )
    d_norm2, _ = lax.optimization_barrier((d_norm2, grad_fc))
    grad_fc = lax.psum_scatter(grad_fc, "wide", scatter_dimension=0, tiled=True)

    mlp_out = sum_own(activation, wfc2_t, me, size, width) + fc2_bias

    full_width = float(width * size)
    scaled = d_norm2 * gain_two
    back_two = inv_two * (
        scaled
        - jnp.sum(scaled, axis=1, keepdims=True) / full_width
        - hat_two * (jnp.sum(scaled * hat_two, axis=1, keepdims=True) / full_width)
    )
    own_norm2 = own(d_norm2)
    grad_ln2_gain = jnp.sum(own_norm2 * own(hat_two), axis=0)
    grad_ln2_bias = jnp.sum(own_norm2, axis=0)
    own_cot = pad_rows(cotangent).astype(jnp.float32)
    masked1 = live_rows * (sent2.astype(jnp.float32) + back_two)
    own_mid = own_cot + own(back_two)
    sent1 = masked1.astype(jnp.bfloat16)
    d_mixed = dot_f32(sent1, wproj_t).astype(jnp.bfloat16)
    d_qkv_b, qkv_sums = attend_backward(
        qkv_rows, mixed_rows, d_mixed, logsum, slot_rows, score_scale
    )
    d_qkv_b, mlp_out = lax.optimization_barrier((d_qkv_b, mlp_out))
    output = trim_rows((own(resid_mid) + live_rows * mlp_out).astype(jnp.bfloat16))
    grad_attn = jnp.concatenate(
        [
            dot_f32(normed1, d_qkv_b, TN).astype(jnp.bfloat16),
            dot_f32(sent1, mixed_rows, TN).astype(jnp.bfloat16),
        ],
        axis=1,
    )
    grad_attn, grad_fc = lax.optimization_barrier((grad_attn, grad_fc))
    grad_attn = lax.psum_scatter(grad_attn, "wide", scatter_dimension=0, tiled=True)
    qkv_sums = jnp.sum(qkv_sums[:, 0], axis=0).reshape(head_count, 3, DH)
    grad_qv_bias = jnp.stack([qkv_sums[:, 0], qkv_sums[:, 2]], axis=1).reshape(-1)

    part1 = dot_f32(d_qkv_b, wqkv_full, NT)
    scaled_part = part1 * gain_one
    row_sums = jnp.stack([jnp.sum(scaled_part, axis=1), jnp.sum(scaled_part * hat_one, axis=1)])
    if size == 2:
        row_sums = row_sums + swap(row_sums)
        moved = swap(
            lax.dynamic_slice_in_dim(part1, (1 - me) * width, width, 1).astype(jnp.bfloat16)
        )
        d_norm1 = own(part1) + moved.astype(jnp.float32)
    else:
        row_sums = lax.psum(row_sums, "narrow")
        d_norm1 = lax.psum_scatter(part1, "narrow", scatter_dimension=1, tiled=True)
    own_hat = own(hat_one)
    back_one = inv_one * (
        d_norm1 * ln1_gain
        - row_sums[0][:, None] / full_width
        - own_hat * (row_sums[1][:, None] / full_width)
    )
    grad_in = trim_rows((own_mid + back_one).astype(jnp.bfloat16))

    vectors_out = [
        jnp.sum(d_norm1 * own_hat, axis=0),
        jnp.sum(d_norm1, axis=0),
        grad_qv_bias,
        jnp.sum(own(masked1), axis=0),
        grad_ln2_gain,
        grad_ln2_bias,
        jnp.sum(d_inner, axis=0),
        jnp.sum(live_rows * own_cot, axis=0),
    ]
    joined = jnp.concatenate(vectors_out)
    joined = lax.psum(joined.reshape(-1, 128), "wide").reshape(-1)
    summed, at = [], 0
    for vector in vectors_out:
        summed.append(joined[at : at + vector.shape[0]])
        at += vector.shape[0]
    qkv_columns, fc_columns = w_qkv.shape[1], w_fc1.shape[1]
    grad_w_qkv = grad_attn[:, :qkv_columns].astype(jnp.float32)
    grad_w_proj = grad_attn[:, qkv_columns:].T.astype(jnp.float32)
    grad_w_fc1 = grad_fc[:, :fc_columns].astype(jnp.float32)
    grad_w_fc2 = grad_fc[:, fc_columns:].T.astype(jnp.float32)
    return (
        output,
        grad_in,
        summed[0],
        summed[1],
        grad_w_qkv,
        summed[2],
        grad_w_proj,
        summed[3],
        summed[4],
        summed[5],
        grad_w_fc1,
        summed[6],
        grad_w_fc2,
        summed[7],
    )


def row_mask(info_ref, img, rows):
    index = lax.broadcasted_iota(jnp.int32, (rows, 1), 0)
    return ((index < SEQ) & (info_ref[1] > img)).astype(jnp.float32)


def halves(info_ref, own_ref, other_ref):
    first = info_ref[0] == 0
    own, other = own_ref[...].astype(jnp.float32), other_ref[...].astype(jnp.float32)
    return jnp.where(first, own, other), jnp.where(first, other, own)


def norm_halves(low, high):
    width = float(low.shape[1] * 2)
    center = (jnp.sum(low, axis=1, keepdims=True) + jnp.sum(high, axis=1, keepdims=True)) / width
    squares = jnp.sum(low * low, axis=1, keepdims=True) + jnp.sum(high * high, axis=1, keepdims=True)
    inv_std = lax.rsqrt(squares / width - center * center + norm_eps)
    return (low - center) * inv_std, (high - center) * inv_std, inv_std


def mask_keys(scores):
    edge = SEQ // 8 * 8
    tail = scores[edge:]
    index = lax.broadcasted_iota(jnp.int32, tail.shape, 0)
    return jnp.concatenate([scores[:edge], jnp.where(index < SEQ - edge, tail, -1e30)], axis=0)


def fwd_kernel(
    info, own, other, gain, shift, wqkv, bias, wproj, normed, qkv, mixed, logsum, part, held,
    *, heads, score_scale,
):
    step, steps = pl.program_id(0), held.shape[0]
    half = own.shape[1]

    @pl.when(step == 0)
    def _():
        low, high, _ = norm_halves(*halves(info, own, other))
        for at, hat in ((0, low), (half, high)):
            cols = slice(at, at + half)
            normed[:, cols] = (hat * gain[:, cols] + shift[:, cols]).astype(jnp.bfloat16)

    block = (dot_f32(normed[...], wqkv[...]) + bias[...]).astype(jnp.bfloat16)
    qkv[...] = block
    for head in range(heads):
        base = head * 3 * DH
        queries = block[:, base : base + DH]
        key_rows = block[:, base + DH : base + 2 * DH]
        value_rows = block[:, base + 2 * DH : base + 3 * DH]
        scores = mask_keys(dot_f32(key_rows, queries * score_scale, NT))
        top = jnp.max(scores, axis=0, keepdims=True)
        exp_scores = jnp.exp(scores - top)
        total = jnp.sum(exp_scores, axis=0, keepdims=True)
        probs = (exp_scores * (1.0 / total)).astype(jnp.bfloat16)
        made = dot_f32(probs, value_rows, TN).astype(jnp.bfloat16)
        mixed[:, head * DH : (head + 1) * DH] = made
        logsum[0, head : head + 1, :] = top + jnp.log(total)
    held[step] = mixed[...]

    @pl.when(step == steps - 1)
    def _():
        whole = jnp.concatenate([held[at] for at in range(steps)], axis=1)
        part[...] = dot_f32(whole, wproj[...], NT).astype(jnp.bfloat16)


def mlp_kernel(
    info, own, other, cot_own, cot_other, mine, theirs, proj_shift, gain, shift, out_shift,
    w1, b1, w2, normed, sent, act, d_inner, d_sum, hat, inv, d_part, out_base, out_sent,
    d_acc, m_acc, *, img,
):
    step, steps = pl.program_id(0), pl.num_programs(0)
    rows, half = own.shape
    first = info[0] == 0

    @pl.when(step == 0)
    def _():
        live = row_mask(info, img, rows)
        low, high = halves(info, own, other)
        attn = mine[...].astype(jnp.float32) + theirs[...].astype(jnp.float32) + proj_shift[...]
        low = low + live * attn[:, :half]
        high = high + live * attn[:, half:]
        out_base[...] = jnp.where(first, low, high)
        low, high, inv_std = norm_halves(low, high)
        inv[...] = inv_std
        cot = halves(info, cot_own, cot_other)
        for at, part, grad in ((0, low, cot[0]), (half, high, cot[1])):
            cols = slice(at, at + half)
            hat[:, cols] = part
            normed[:, cols] = (part * gain[:, cols] + shift[:, cols]).astype(jnp.bfloat16)
            sent[:, cols] = (live * grad).astype(jnp.bfloat16)
        d_acc[...] = jnp.zeros_like(d_acc)
        m_acc[...] = jnp.zeros_like(m_acc)

    inner = dot_f32(normed[...], w1[...]) + b1[...]
    cdf = normal_cdf(inner)
    made = (inner * cdf).astype(jnp.bfloat16)
    act[...] = made
    slope = cdf + inner * jnp.exp(-0.5 * inner * inner) * (1.0 / math.sqrt(2.0 * math.pi))
    grad = dot_f32(sent[...], w2[...]) * slope
    d_sum[...] = jnp.sum(grad, axis=0, keepdims=True)
    grad = grad.astype(jnp.bfloat16)
    d_inner[...] = grad
    d_acc[...] += dot_f32(grad, w1[...], NT)
    m_acc[...] += dot_f32(made, w2[...], NT)

    @pl.when(step == steps - 1)
    def _():
        d_part[...] = d_acc[...].astype(jnp.bfloat16)
        low, high = m_acc[:, :half], m_acc[:, half:]
        live = row_mask(info, img, rows)
        out_base[...] += live * (jnp.where(first, low, high) + out_shift[...])
        out_sent[...] = (live * jnp.where(first, high, low)).astype(jnp.bfloat16)


def bwd_kernel(
    info, own, other, cot_own, cot_other, mine, theirs, gain2, gain1, hat, inv, wproj, qkv, mixed,
    logsum, wqkv, sent, d_qkv, sums, mid, sum_gain, sum_bias, sum_proj, d_own, d_sent, hat_own,
    inv_one, row_sums, d_mixed, acc, *, img, heads, score_scale,
):
    step, steps = pl.program_id(0), pl.num_programs(0)
    rows, half = own.shape
    full_width = float(2 * half)
    first = info[0] == 0

    @pl.when(step == 0)
    def _():
        live = row_mask(info, img, rows)
        grad = mine[...].astype(jnp.float32) + theirs[...].astype(jnp.float32)
        scaled = grad * gain2[...]
        back = inv[...] * (
            scaled
            - jnp.sum(scaled, axis=1, keepdims=True) / full_width
            - hat[...] * (jnp.sum(scaled * hat[...], axis=1, keepdims=True) / full_width)
        )
        sum_gain[...] = jnp.sum(grad * hat[...], axis=0, keepdims=True)
        sum_bias[...] = jnp.sum(grad, axis=0, keepdims=True)
        low, high = halves(info, cot_own, cot_other)
        low, high = low + back[:, :half], high + back[:, half:]
        mid[...] = jnp.where(first, low, high)
        for at, part in ((0, low), (half, high)):
            cols = slice(at, at + half)
            masked = live * part
            sum_proj[:, cols] = jnp.sum(masked, axis=0, keepdims=True)
            sent[:, cols] = masked.astype(jnp.bfloat16)
        made = dot_f32(sent[...], wproj[...]).astype(jnp.bfloat16)
        for at in range(d_mixed.shape[0]):
            d_mixed[at] = made[:, at * heads * DH : (at + 1) * heads * DH]
        acc[...] = jnp.zeros_like(acc)

    for head in range(heads):
        base = head * 3 * DH
        queries = qkv[:, base : base + DH]
        key_rows = qkv[:, base + DH : base + 2 * DH]
        value_rows = qkv[:, base + 2 * DH : base + 3 * DH]
        out = mixed[:, head * DH : (head + 1) * DH]
        d_out = d_mixed[step, :, head * DH : (head + 1) * DH]
        products = d_out.astype(jnp.float32) * out.astype(jnp.float32)
        delta = jnp.sum(jnp.transpose(products), axis=0, keepdims=True)
        scores = mask_keys(dot_f32(key_rows, queries * score_scale, NT))
        probs = jnp.exp(scores - logsum[0, head : head + 1, :])
        d_probs = dot_f32(value_rows, d_out, NT)
        d_scores = (probs * (d_probs - delta)).astype(jnp.bfloat16)
        d_query = dot_f32(d_scores, key_rows, TN) * score_scale
        d_keys = dot_f32(d_scores, queries, NN) * score_scale
        d_values = dot_f32(probs.astype(jnp.bfloat16), d_out, NN)
        for at, grad in enumerate((d_query, d_keys, d_values)):
            cols = slice(base + at * DH, base + (at + 1) * DH)
            d_qkv[:, cols] = grad.astype(jnp.bfloat16)
            sums[:, cols] = jnp.sum(grad, axis=0, keepdims=True)
    acc[...] += dot_f32(d_qkv[...], wqkv[...], NT)

    @pl.when(step == steps - 1)
    def _():
        low, high, inv_std = norm_halves(*halves(info, own, other))
        inv_one[...] = inv_std
        hat_own[...] = jnp.where(first, low, high)
        left, right = acc[:, :half], acc[:, half:]
        d_own[...] = jnp.where(first, left, right)
        d_sent[...] = jnp.where(first, right, left).astype(jnp.bfloat16)
        left, right = left * gain1[:, :half], right * gain1[:, half:]
        plain = jnp.sum(left, axis=1, keepdims=True) + jnp.sum(right, axis=1, keepdims=True)
        hatted = jnp.sum(left * low, axis=1, keepdims=True) + jnp.sum(
            right * high, axis=1, keepdims=True
        )
        lane = lax.broadcasted_iota(jnp.int32, (rows, 128), 1)
        both = jnp.where(lane == 0, plain, jnp.where(lane == 1, hatted, 0.0))
        row_sums[...] = jnp.transpose(both)[:8]


def pair_grad_kernel(left0, left1, right0, right1, more0, more1, rest0, rest1, out, held, *, cut):
    step = pl.program_id(0)

    def load(one, two):
        held[...] = jnp.concatenate([one[...], two[...]], axis=0)

    def make(one, two):
        right = jnp.concatenate([one[...], two[...]], axis=0)
        out[...] = dot_f32(held[...], right, TN).astype(jnp.bfloat16)

    pl.when(step == 0)(lambda: load(left0, left1))
    pl.when(step == cut)(lambda: load(more0, more1))
    pl.when(step < cut)(lambda: make(right0, right1))
    pl.when(step >= cut)(lambda: make(rest0, rest1))


SCALARS = pl.BlockSpec(memory_space=pltpu.SMEM)
PARAMS = pltpu.CompilerParams(vmem_limit_bytes=56 * 1024 * 1024)


def whole(shape):
    return pl.BlockSpec(shape, lambda s: (0,) * len(shape))


def cols(rows, width, start=0):
    return pl.BlockSpec((rows, width), lambda s: (0, start + s))


def cost(flops, moved):
    return pl.CostEstimate(flops=flops, bytes_accessed=moved, transcendentals=0)


def shaped(*shapes):
    return [jax.ShapeDtypeStruct(shape, kind) for shape, kind in shapes]


F32, BF16 = jnp.float32, jnp.bfloat16


def forward(info, own, other, gain, shift, early, bias, score_scale):
    rows, half = own.shape
    wide, total = early.shape
    inner = total - bias.shape[1]
    heads = 2
    steps = inner // (heads * DH)
    span = heads * 3 * DH
    return pl.pallas_call(
        functools.partial(fwd_kernel, heads=heads, score_scale=score_scale),
        grid=(steps,),
        in_specs=[
            SCALARS, whole((rows, half)), whole((rows, half)), whole((1, wide)), whole((1, wide)),
            cols(wide, span), cols(1, span),
            pl.BlockSpec((wide, inner), lambda s: (0, bias.shape[1] // inner)),
        ],
        out_specs=[
            whole((rows, wide)), cols(rows, span), cols(rows, heads * DH),
            pl.BlockSpec((1, 8, rows), lambda s: (s, 0, 0)), whole((rows, wide)),
        ],
        out_shape=shaped(
            ((rows, wide), BF16), ((rows, steps * span), BF16), ((rows, inner), BF16),
            ((steps, 8, rows), F32), ((rows, wide), BF16),
        ),
        scratch_shapes=[pltpu.VMEM((steps, rows, heads * DH), BF16)],
        compiler_params=PARAMS,
        cost_estimate=cost(12_000_000_000, 12_000_000),
        name="attention_forward",
    )(info, own, other, gain, shift, early, bias, early)


def mlp_pass(info, img, own, other, cot_own, cot_other, mine, theirs, vectors, out_shift, late, b1):
    rows, half = own.shape
    wide = late.shape[0]
    hidden = b1.shape[1]
    tile = 512
    steps = hidden // tile
    proj_shift, gain, shift = vectors
    return pl.pallas_call(
        functools.partial(mlp_kernel, img=img),
        grid=(steps,),
        in_specs=[
            SCALARS, *[whole((rows, half))] * 4, *[whole((rows, wide))] * 2, *[whole((1, wide))] * 3,
            whole((1, half)), cols(wide, tile), cols(1, tile), cols(wide, tile, steps),
        ],
        out_specs=[
            whole((rows, wide)), whole((rows, wide)), cols(rows, tile), cols(rows, tile),
            cols(1, tile), whole((rows, wide)), whole((rows, 1)), whole((rows, wide)),
            whole((rows, half)), whole((rows, half)),
        ],
        out_shape=shaped(
            ((rows, wide), BF16), ((rows, wide), BF16), ((rows, hidden), BF16),
            ((rows, hidden), BF16), ((1, hidden), F32), ((rows, wide), F32), ((rows, 1), F32),
            ((rows, wide), BF16), ((rows, half), F32), ((rows, half), BF16),
        ),
        scratch_shapes=[pltpu.VMEM((rows, wide), F32), pltpu.VMEM((rows, wide), F32)],
        compiler_params=PARAMS,
        cost_estimate=cost(12_000_000_000, 30_000_000),
        name="feed_forward",
    )(info, own, other, cot_own, cot_other, mine, theirs, proj_shift, gain, shift, out_shift,
      late, b1, late)


def backward(
    info, img, own, other, cot_own, cot_other, mine, theirs, gain2, gain1, hat, inv, early, qkv,
    mixed, logsum, score_scale,
):
    rows, half = own.shape
    wide = early.shape[0]
    inner = mixed.shape[1]
    heads = 2
    steps = inner // (heads * DH)
    span = heads * 3 * DH
    return pl.pallas_call(
        functools.partial(bwd_kernel, img=img, heads=heads, score_scale=score_scale),
        grid=(steps,),
        in_specs=[
            SCALARS, *[whole((rows, half))] * 4, *[whole((rows, wide))] * 2, *[whole((1, wide))] * 2,
            whole((rows, wide)), whole((rows, 1)),
            pl.BlockSpec((wide, inner), lambda s: (0, qkv.shape[1] // inner)),
            cols(rows, span), cols(rows, heads * DH),
            pl.BlockSpec((1, 8, rows), lambda s: (s, 0, 0)), cols(wide, span),
        ],
        out_specs=[
            whole((rows, wide)), cols(rows, span), cols(1, span), whole((rows, half)),
            whole((1, wide)), whole((1, wide)), whole((1, wide)), whole((rows, half)),
            whole((rows, half)), whole((rows, half)), whole((rows, 1)), whole((8, rows)),
        ],
        out_shape=shaped(
            ((rows, wide), BF16), ((rows, 3 * inner), BF16), ((1, 3 * inner), F32),
            ((rows, half), F32), ((1, wide), F32), ((1, wide), F32), ((1, wide), F32),
            ((rows, half), F32), ((rows, half), BF16), ((rows, half), F32), ((rows, 1), F32),
            ((8, rows), F32),
        ),
        scratch_shapes=[
            pltpu.VMEM((steps, rows, heads * DH), BF16), pltpu.VMEM((rows, wide), F32)
        ],
        compiler_params=PARAMS,
        cost_estimate=cost(16_000_000_000, 30_000_000),
        name="attention_backward",
    )(info, own, other, cot_own, cot_other, mine, theirs, gain2, gain1, hat, inv, early, qkv, mixed,
      logsum, early)


def pair_grads(lefts, rights, mores, rests, tile=512):
    rows, wide = lefts[0].shape
    first, second = rights[0].shape[1] // tile, rests[0].shape[1] // tile
    left = whole((rows, wide))
    right = pl.BlockSpec((rows, tile), lambda s: (0, jnp.minimum(s, first - 1)))
    rest = pl.BlockSpec((rows, tile), lambda s: (0, jnp.maximum(s - first, 0)))
    return pl.pallas_call(
        functools.partial(pair_grad_kernel, cut=first),
        grid=(first + second,),
        in_specs=[left, left, right, right, left, left, rest, rest],
        out_specs=cols(wide, tile),
        out_shape=jax.ShapeDtypeStruct((wide, (first + second) * tile), BF16),
        scratch_shapes=[pltpu.VMEM((2 * rows, wide), BF16)],
        compiler_params=PARAMS,
        cost_estimate=cost(4 * rows * wide * (first + second) * tile, 20_000_000),
        name="weight_gradients",
    )(*lefts, *rights, *mores, *rests)


def sum_groups(vector, axis):
    count = lax.axis_size(axis)
    if count & (count - 1):
        return lax.psum(vector, axis)
    bit = 1
    while bit < count:
        vector = vector + lax.ppermute(vector, axis, [(at, at ^ bit) for at in range(count)])
        bit *= 2
    return vector


def shards_pair(
    inputs, counts, ln1_gain, ln1_bias, w_qkv, qv_bias, w_proj, proj_bias, ln2_gain, ln2_bias,
    w_fc1, fc1_bias, w_fc2, fc2_bias, cotangent,
):
    me = lax.axis_index("narrow")
    row_count, half = inputs.shape
    images = row_count // SEQ
    rows = -(-SEQ // ROW_TILE) * ROW_TILE
    head_count = w_qkv.shape[1] // (3 * DH)
    score_scale = 1.0 / math.sqrt(DH)
    span = range(images)
    info = jnp.stack([me.astype(jnp.int32), counts[0]])

    def slot(array, img):
        return jnp.pad(array[img * SEQ : (img + 1) * SEQ], ((0, rows - SEQ), (0, 0)))

    def own(vector):
        return lax.dynamic_slice_in_dim(vector, me * half, half, vector.ndim - 1)

    early = lax.all_gather(
        jnp.concatenate([w_qkv, w_proj.T], axis=1), "wide", axis=0, tiled=True
    )
    late = lax.all_gather(jnp.concatenate([w_fc1, w_fc2.T], axis=1), "wide", axis=0, tiled=True)

    vectors = widen(jnp.stack([ln1_gain, ln1_bias, ln2_gain, ln2_bias, proj_bias]), me, 2)
    gain_one, shift_one, gain_two, shift_two, proj_shift = (vectors[i : i + 1] for i in range(5))
    mine = [slot(inputs, i) for i in span]
    theirs = [swap(x) for x in mine]
    cot = [slot(cotangent, i) for i in span]
    cot_theirs = [swap(x) for x in cot]

    bias_qv = qv_bias.reshape(head_count, 2, DH)
    bias_full = jnp.stack(
        [bias_qv[:, 0], jnp.zeros_like(bias_qv[:, 0]), bias_qv[:, 1]], axis=1
    ).reshape(1, head_count * 3 * DH)

    early, cot_theirs, theirs = lax.optimization_barrier((early, cot_theirs, theirs))
    front = [
        forward(info, mine[i], theirs[i], gain_one, shift_one, early, bias_full, score_scale)
        for i in span
    ]
    normed1, qkv, mixed, logsum, part = zip(*front)
    part_theirs = [swap(x) for x in part]
    middle = [
        mlp_pass(
            info, i, mine[i], theirs[i], cot[i], cot_theirs[i], part[i], part_theirs[i],
            (proj_shift, gain_two, shift_two), fc2_bias.reshape(1, -1), late,
            fc1_bias.reshape(1, -1),
        )
        for i in span
    ]
    normed2, sent2, act, d_inner, d_sum, hat2, inv2, d_part, out_base, out_sent = zip(*middle)
    d_theirs = [swap(x) for x in d_part]
    out_theirs = [swap(x) for x in out_sent]
    grad_fc = pair_grads(normed2, d_inner, sent2, act)
    d_theirs, grad_fc = lax.optimization_barrier((d_theirs, grad_fc))
    grad_fc = lax.psum_scatter(grad_fc, "wide", scatter_dimension=0, tiled=True)
    ends = [
        backward(
            info, i, mine[i], theirs[i], cot[i], cot_theirs[i], d_part[i], d_theirs[i], gain_two,
            gain_one, hat2[i], inv2[i], early, qkv[i], mixed[i], logsum[i], score_scale,
        )
        for i in span
    ]
    (sent1, d_qkv, qkv_sums, mid, sum_gain, sum_bias, sum_proj, d_own, d_sent, hat_own, inv_one,
     row_sums) = zip(*ends)
    d_moved = [swap(x) for x in d_sent]
    row_sums = [x + swap(x) for x in row_sums]
    grad_attn = pair_grads(normed1, d_qkv, sent1, mixed)
    grad_attn, grad_fc = lax.optimization_barrier((grad_attn, grad_fc))
    grad_attn = lax.psum_scatter(grad_attn, "wide", scatter_dimension=0, tiled=True)

    output = jnp.concatenate(
        [(out_base[i] + out_theirs[i].astype(F32)).astype(BF16)[:SEQ] for i in span], axis=0
    )
    full_width = float(2 * half)
    grads_in, gain_sums, bias_sums = [], [], []
    for i in span:
        d_norm1 = d_own[i] + d_moved[i].astype(F32)
        gain_sums.append(jnp.sum(d_norm1 * hat_own[i], axis=0))
        bias_sums.append(jnp.sum(d_norm1, axis=0))
        back = inv_one[i] * (
            d_norm1 * ln1_gain
            - row_sums[i][0][:, None] / full_width
            - hat_own[i] * (row_sums[i][1][:, None] / full_width)
        )
        grads_in.append((mid[i] + back).astype(BF16)[:SEQ])
    grad_in = jnp.concatenate(grads_in, axis=0)

    qkv_sums = sum(qkv_sums).reshape(head_count, 3, DH)
    grad_qv = jnp.stack([qkv_sums[:, 0], qkv_sums[:, 2]], axis=1).reshape(-1)
    own_cot = sum(
        jnp.sum(jnp.where(counts[0] > i, cot[i].astype(F32), 0.0), axis=0) for i in span
    )
    soon = jnp.concatenate(
        [
            grad_qv, own(sum(sum_proj))[0], own(sum(sum_gain))[0], own(sum(sum_bias))[0],
            sum(d_sum)[0], own_cot,
        ]
    )
    last = jnp.concatenate([sum(gain_sums), sum(bias_sums)])
    soon = sum_groups(soon.reshape(-1, 128), "wide").reshape(-1)
    last = sum_groups(last.reshape(-1, 128), "wide").reshape(-1)
    qv, ff = grad_qv.shape[0], fc1_bias.shape[0]
    edges = [0]
    for extent in (qv, half, half, half, ff, half):
        edges.append(edges[-1] + extent)
    pieces = [soon[a:b] for a, b in zip(edges[:-1], edges[1:])]
    split_attn, split_fc = w_qkv.shape[1], w_fc1.shape[1]
    return (
        output,
        grad_in,
        last[:half],
        last[half:],
        grad_attn[:, :split_attn].astype(F32),
        pieces[0],
        grad_attn[:, split_attn:].T.astype(F32),
        pieces[1],
        pieces[2],
        pieces[3],
        grad_fc[:, :split_fc].astype(F32),
        pieces[4],
        grad_fc[:, split_fc:].T.astype(F32),
        pieces[5],
    )


def shards(*arrays):
    if lax.axis_size("narrow") == 2:
        return shards_pair(*arrays)
    return shards_any(*arrays)


def solution(mesh):
    return jax.shard_map(
        shards,
        mesh=mesh,
        in_specs=(
            P("wide", "narrow"),
            P("wide"),
            P("narrow"),
            P("narrow"),
            P("wide", "narrow"),
            P("narrow"),
            P("narrow", "wide"),
            P("narrow"),
            P("narrow"),
            P("narrow"),
            P("wide", "narrow"),
            P("narrow"),
            P("narrow", "wide"),
            P("narrow"),
            P("wide", "narrow"),
        ),
        out_specs=(
            P("wide", "narrow"),
            P("wide", "narrow"),
            P("narrow"),
            P("narrow"),
            P("wide", "narrow"),
            P("narrow"),
            P("narrow", "wide"),
            P("narrow"),
            P("narrow"),
            P("narrow"),
            P("wide", "narrow"),
            P("narrow"),
            P("narrow", "wide"),
            P("narrow"),
        ),
        check_vma=False,
    )
```

```python
import functools
import math

import jax
import jax.numpy as jnp
from jax import lax
from jax.experimental import pallas as pl
from jax.experimental.pallas import tpu as pltpu
from jax.sharding import PartitionSpec as P

DH = 64
SEQ = 577
ROW_TILE = 16


norm_eps = 1e-06
NT = (((1,), (1,)), ((), ()))
TN = (((0,), (0,)), ((), ()))
NN = (((1,), (0,)), ((), ()))


def dot_f32(left_mat, right_mat, dims=NN):
    return lax.dot_general(left_mat, right_mat, dims, preferred_element_type=jnp.float32)


def swap(piece):
    return lax.ppermute(piece, "narrow", ((0, 1), (1, 0)))


def widen(piece, me, size):
    if size != 2:
        return lax.all_gather(piece, "narrow", axis=1, tiled=True)
    other = swap(piece)
    return jnp.concatenate(
        [jnp.where(me == 0, piece, other), jnp.where(me == 0, other, piece)], axis=1
    )


def sum_whole(partial_rows, size):
    if size != 2:
        return lax.psum(partial_rows, "narrow")
    mine = partial_rows.astype(jnp.bfloat16)
    return mine.astype(jnp.float32) + swap(mine).astype(jnp.float32)


def sum_own(left_mat, right_rows, me, size, width):
    if size != 2:
        return lax.psum_scatter(
            dot_f32(left_mat, right_rows, NT), "narrow", scatter_dimension=1, tiled=True
        )
    theirs = lax.dynamic_slice_in_dim(right_rows, (1 - me) * width, width, 0)
    ours = lax.dynamic_slice_in_dim(right_rows, me * width, width, 0)
    moved = swap(dot_f32(left_mat, theirs, NT).astype(jnp.bfloat16))
    return dot_f32(left_mat, ours, NT) + moved.astype(jnp.float32)


def normal_cdf(values_in):
    return 0.5 * (1.0 + lax.erf(values_in * (1.0 / math.sqrt(2.0))))


def gelu_exact(values_in):
    return values_in * normal_cdf(values_in)


def gelu_slope(values_in):
    return normal_cdf(values_in) + values_in * jnp.exp(-0.5 * values_in * values_in) * (
        1.0 / math.sqrt(2.0 * math.pi)
    )


def norm_forward(rows_in, gain_vec, shift_vec):
    width = float(rows_in.shape[1])
    center = jnp.sum(rows_in, axis=1, keepdims=True) / width
    spread = jnp.sum(rows_in * rows_in, axis=1, keepdims=True) / width - center * center
    inv_std = lax.rsqrt(spread + norm_eps)
    normalized = (rows_in - center) * inv_std
    return (normalized, inv_std, (normalized * gain_vec + shift_vec).astype(jnp.bfloat16))


def scores_by_key(queries, key_rows, score_scale):
    scores = dot_f32(key_rows, queries, NT) * score_scale
    key_index = lax.broadcasted_iota(jnp.int32, scores.shape, 0)
    return jnp.where(key_index < SEQ, scores, -1e30)


def attend_kernel(qkv_ref, mixed_ref, logsum_ref, *, heads, score_scale):
    for head in range(heads):
        base = head * 3 * DH
        queries = qkv_ref[:, base : base + DH]
        key_rows = qkv_ref[:, base + DH : base + 2 * DH]
        value_rows = qkv_ref[:, base + 2 * DH : base + 3 * DH]
        scores = scores_by_key(queries, key_rows, score_scale)
        top = jnp.max(scores, axis=0, keepdims=True)
        exp_scores = jnp.exp(scores - top)
        total = jnp.sum(exp_scores, axis=0, keepdims=True)
        probs = (exp_scores * (1.0 / total)).astype(jnp.bfloat16)
        mixed_ref[:, head * DH : (head + 1) * DH] = dot_f32(probs, value_rows, TN).astype(
            jnp.bfloat16
        )
        logsum_ref[0, head : head + 1, :] = top + jnp.log(total)


def attend_back_kernel(
    qkv_ref, mixed_ref, d_mixed_ref, logsum_ref, d_qkv_ref, sums_ref, *, heads, score_scale
):
    for head in range(heads):
        base = head * 3 * DH
        queries = qkv_ref[:, base : base + DH]
        key_rows = qkv_ref[:, base + DH : base + 2 * DH]
        value_rows = qkv_ref[:, base + 2 * DH : base + 3 * DH]
        mixed = mixed_ref[:, head * DH : (head + 1) * DH]
        d_mixed = d_mixed_ref[:, head * DH : (head + 1) * DH]
        products = d_mixed.astype(jnp.float32) * mixed.astype(jnp.float32)
        delta = jnp.sum(jnp.transpose(products), axis=0, keepdims=True)
        scores = scores_by_key(queries, key_rows, score_scale)
        probs = jnp.exp(scores - logsum_ref[0, head : head + 1, :])
        d_probs = dot_f32(value_rows, d_mixed, NT)
        d_scores = (probs * (d_probs - delta)).astype(jnp.bfloat16)
        d_query = dot_f32(d_scores, key_rows, TN) * score_scale
        d_keys = dot_f32(d_scores, queries, NN) * score_scale
        d_values = dot_f32(probs.astype(jnp.bfloat16), d_mixed, NN)
        for part, grad in enumerate((d_query, d_keys, d_values)):
            columns = slice(base + part * DH, base + (part + 1) * DH)
            d_qkv_ref[:, columns] = grad.astype(jnp.bfloat16)
            sums_ref[0, :, columns] = jnp.broadcast_to(
                jnp.sum(grad, axis=0, keepdims=True), (8, DH)
            )


def head_pairs(width):
    heads = 2
    return heads, width // (3 * DH * heads)


def attend(qkv_rows, slot_rows, score_scale):
    row_count, width = qkv_rows.shape
    slots = row_count // slot_rows
    heads, pairs = head_pairs(width)
    return pl.pallas_call(
        functools.partial(attend_kernel, heads=heads, score_scale=score_scale),
        grid=(slots, pairs),
        in_specs=[pl.BlockSpec((slot_rows, heads * 3 * DH), lambda s, p: (s, p))],
        out_specs=[
            pl.BlockSpec((slot_rows, heads * DH), lambda s, p: (s, p)),
            pl.BlockSpec((1, 8, slot_rows), lambda s, p: (s * pairs + p, 0, 0)),
        ],
        out_shape=[
            jax.ShapeDtypeStruct((row_count, width // 3), jnp.bfloat16),
            jax.ShapeDtypeStruct((slots * pairs, 8, slot_rows), jnp.float32),
        ],
        cost_estimate=pl.CostEstimate(
            flops=4 * slots * pairs * heads * slot_rows * slot_rows * 256,
            bytes_accessed=row_count * width * 3,
            transcendentals=slots * pairs * heads * slot_rows * slot_rows,
        ),
        name="attend",
    )(qkv_rows)


def attend_backward(qkv_rows, mixed_rows, d_mixed, logsum, slot_rows, score_scale):
    row_count, width = qkv_rows.shape
    slots = row_count // slot_rows
    heads, pairs = head_pairs(width)
    narrow_block = pl.BlockSpec((slot_rows, heads * DH), lambda s, p: (s, p))
    wide_block = pl.BlockSpec((slot_rows, heads * 3 * DH), lambda s, p: (s, p))
    return pl.pallas_call(
        functools.partial(attend_back_kernel, heads=heads, score_scale=score_scale),
        grid=(slots, pairs),
        in_specs=[
            wide_block,
            narrow_block,
            narrow_block,
            pl.BlockSpec((1, 8, slot_rows), lambda s, p: (s * pairs + p, 0, 0)),
        ],
        out_specs=[
            wide_block,
            pl.BlockSpec((1, 8, heads * 3 * DH), lambda s, p: (s, 0, p)),
        ],
        out_shape=[
            jax.ShapeDtypeStruct((row_count, width), jnp.bfloat16),
            jax.ShapeDtypeStruct((slots, 8, width), jnp.float32),
        ],
        cost_estimate=pl.CostEstimate(
            flops=10 * slots * pairs * heads * slot_rows * slot_rows * 256,
            bytes_accessed=row_count * width * 6,
            transcendentals=slots * pairs * heads * slot_rows * slot_rows,
        ),
        name="attend_back",
    )(qkv_rows, mixed_rows, d_mixed, logsum)


def shards_any(
    inputs,
    counts,
    ln1_gain,
    ln1_bias,
    w_qkv,
    qv_bias,
    w_proj,
    proj_bias,
    ln2_gain,
    ln2_bias,
    w_fc1,
    fc1_bias,
    w_fc2,
    fc2_bias,
    cotangent,
):
    size = lax.axis_size("narrow")
    me = lax.axis_index("narrow")
    row_count, width = inputs.shape
    slot_count = row_count // SEQ
    slot_rows = -(-SEQ // ROW_TILE) * ROW_TILE
    padded = slot_count * slot_rows
    head_count = w_qkv.shape[1] // (3 * DH)
    score_scale = 1.0 / math.sqrt(DH)

    def pad_rows(rows):
        rows = rows.reshape(slot_count, SEQ, rows.shape[1])
        rows = jnp.pad(rows, ((0, 0), (0, slot_rows - SEQ), (0, 0)))
        return rows.reshape(padded, rows.shape[2])

    def trim_rows(rows):
        rows = rows.reshape(slot_count, slot_rows, rows.shape[1])[:, :SEQ]
        return rows.reshape(row_count, rows.shape[2])

    def own(rows):
        return lax.dynamic_slice_in_dim(rows, me * width, width, rows.ndim - 1)

    padded_index = lax.broadcasted_iota(jnp.int32, (padded, 1), 0)
    live_rows = (
        (padded_index // slot_rows < counts[0]) & (padded_index % slot_rows < SEQ)
    ).astype(jnp.float32)

    early = lax.all_gather(
        jnp.concatenate([w_qkv, w_proj.T], axis=1), "wide", axis=0, tiled=True
    )
    wqkv_full = early[:, : w_qkv.shape[1]]
    wproj_t = early[:, w_qkv.shape[1] :]
    late = lax.all_gather(
        jnp.concatenate([w_fc1, w_fc2.T], axis=1), "wide", axis=0, tiled=True
    )
    wfc1_full = late[:, : w_fc1.shape[1]]
    wfc2_t = late[:, w_fc1.shape[1] :]

    vectors = widen(
        jnp.stack([ln1_gain, ln1_bias, ln2_gain, ln2_bias, proj_bias]), me, size
    )
    gain_one, shift_one, gain_two, shift_two, proj_shift = (vectors[i : i + 1] for i in range(5))

    inputs_whole = widen(pad_rows(inputs), me, size)
    sent2 = widen((live_rows * pad_rows(cotangent).astype(jnp.float32)).astype(jnp.bfloat16), me, size)

    resid = inputs_whole.astype(jnp.float32)
    hat_one, inv_one, normed1 = norm_forward(resid, gain_one, shift_one)
    bias_qv = qv_bias.reshape(head_count, 2, DH)
    bias_full = jnp.stack(
        [bias_qv[:, 0], jnp.zeros_like(bias_qv[:, 0]), bias_qv[:, 1]], axis=1
    ).reshape(1, head_count * 3 * DH)
    qkv_rows = (dot_f32(normed1, wqkv_full) + bias_full).astype(jnp.bfloat16)
    qkv_rows, sent2 = lax.optimization_barrier((qkv_rows, sent2))
    mixed_rows, logsum = attend(qkv_rows, slot_rows, score_scale)
    attn_out = sum_whole(dot_f32(mixed_rows, wproj_t, NT), size) + proj_shift
    resid_mid = resid + live_rows * attn_out
    hat_two, inv_two, normed2 = norm_forward(resid_mid, gain_two, shift_two)
    inner_pre = dot_f32(normed2, wfc1_full) + fc1_bias
    activation = gelu_exact(inner_pre).astype(jnp.bfloat16)

    d_inner = dot_f32(sent2, wfc2_t) * gelu_slope(inner_pre)
    d_inner_b = d_inner.astype(jnp.bfloat16)
    d_norm2 = sum_whole(dot_f32(d_inner_b, wfc1_full, NT), size)
    grad_fc = jnp.concatenate(
        [
            dot_f32(normed2, d_inner_b, TN).astype(jnp.bfloat16),
            dot_f32(sent2, activation, TN).astype(jnp.bfloat16),
        ],
        axis=1,
    )
    d_norm2, _ = lax.optimization_barrier((d_norm2, grad_fc))
    grad_fc = lax.psum_scatter(grad_fc, "wide", scatter_dimension=0, tiled=True)

    mlp_out = sum_own(activation, wfc2_t, me, size, width) + fc2_bias

    full_width = float(width * size)
    scaled = d_norm2 * gain_two
    back_two = inv_two * (
        scaled
        - jnp.sum(scaled, axis=1, keepdims=True) / full_width
        - hat_two * (jnp.sum(scaled * hat_two, axis=1, keepdims=True) / full_width)
    )
    own_norm2 = own(d_norm2)
    grad_ln2_gain = jnp.sum(own_norm2 * own(hat_two), axis=0)
    grad_ln2_bias = jnp.sum(own_norm2, axis=0)
    own_cot = pad_rows(cotangent).astype(jnp.float32)
    masked1 = live_rows * (sent2.astype(jnp.float32) + back_two)
    own_mid = own_cot + own(back_two)
    sent1 = masked1.astype(jnp.bfloat16)
    d_mixed = dot_f32(sent1, wproj_t).astype(jnp.bfloat16)
    d_qkv_b, qkv_sums = attend_backward(
        qkv_rows, mixed_rows, d_mixed, logsum, slot_rows, score_scale
    )
    d_qkv_b, mlp_out = lax.optimization_barrier((d_qkv_b, mlp_out))
    output = trim_rows((own(resid_mid) + live_rows * mlp_out).astype(jnp.bfloat16))
    grad_attn = jnp.concatenate(
        [
            dot_f32(normed1, d_qkv_b, TN).astype(jnp.bfloat16),
            dot_f32(sent1, mixed_rows, TN).astype(jnp.bfloat16),
        ],
        axis=1,
    )
    grad_attn, grad_fc = lax.optimization_barrier((grad_attn, grad_fc))
    grad_attn = lax.psum_scatter(grad_attn, "wide", scatter_dimension=0, tiled=True)
    qkv_sums = jnp.sum(qkv_sums[:, 0], axis=0).reshape(head_count, 3, DH)
    grad_qv_bias = jnp.stack([qkv_sums[:, 0], qkv_sums[:, 2]], axis=1).reshape(-1)

    part1 = dot_f32(d_qkv_b, wqkv_full, NT)
    scaled_part = part1 * gain_one
    row_sums = jnp.stack([jnp.sum(scaled_part, axis=1), jnp.sum(scaled_part * hat_one, axis=1)])
    if size == 2:
        row_sums = row_sums + swap(row_sums)
        moved = swap(
            lax.dynamic_slice_in_dim(part1, (1 - me) * width, width, 1).astype(jnp.bfloat16)
        )
        d_norm1 = own(part1) + moved.astype(jnp.float32)
    else:
        row_sums = lax.psum(row_sums, "narrow")
        d_norm1 = lax.psum_scatter(part1, "narrow", scatter_dimension=1, tiled=True)
    own_hat = own(hat_one)
    back_one = inv_one * (
        d_norm1 * ln1_gain
        - row_sums[0][:, None] / full_width
        - own_hat * (row_sums[1][:, None] / full_width)
    )
    grad_in = trim_rows((own_mid + back_one).astype(jnp.bfloat16))

    vectors_out = [
        jnp.sum(d_norm1 * own_hat, axis=0),
        jnp.sum(d_norm1, axis=0),
        grad_qv_bias,
        jnp.sum(own(masked1), axis=0),
        grad_ln2_gain,
        grad_ln2_bias,
        jnp.sum(d_inner, axis=0),
        jnp.sum(live_rows * own_cot, axis=0),
    ]
    joined = jnp.concatenate(vectors_out)
    joined = lax.psum(joined.reshape(-1, 128), "wide").reshape(-1)
    summed, at = [], 0
    for vector in vectors_out:
        summed.append(joined[at : at + vector.shape[0]])
        at += vector.shape[0]
    qkv_columns, fc_columns = w_qkv.shape[1], w_fc1.shape[1]
    grad_w_qkv = grad_attn[:, :qkv_columns].astype(jnp.float32)
    grad_w_proj = grad_attn[:, qkv_columns:].T.astype(jnp.float32)
    grad_w_fc1 = grad_fc[:, :fc_columns].astype(jnp.float32)
    grad_w_fc2 = grad_fc[:, fc_columns:].T.astype(jnp.float32)
    return (
        output,
        grad_in,
        summed[0],
        summed[1],
        grad_w_qkv,
        summed[2],
        grad_w_proj,
        summed[3],
        summed[4],
        summed[5],
        grad_w_fc1,
        summed[6],
        grad_w_fc2,
        summed[7],
    )


def row_mask(info_ref, img, rows):
    index = lax.broadcasted_iota(jnp.int32, (rows, 1), 0)
    return ((index < SEQ) & (info_ref[1] > img)).astype(jnp.float32)


def halves(info_ref, own_ref, other_ref):
    first = info_ref[0] == 0
    own, other = own_ref[...].astype(jnp.float32), other_ref[...].astype(jnp.float32)
    return jnp.where(first, own, other), jnp.where(first, other, own)


def norm_halves(low, high):
    width = float(low.shape[1] * 2)
    center = (jnp.sum(low, axis=1, keepdims=True) + jnp.sum(high, axis=1, keepdims=True)) / width
    squares = jnp.sum(low * low, axis=1, keepdims=True) + jnp.sum(high * high, axis=1, keepdims=True)
    inv_std = lax.rsqrt(squares / width - center * center + norm_eps)
    return (low - center) * inv_std, (high - center) * inv_std, inv_std


def mask_keys(scores):
    edge = SEQ // 8 * 8
    tail = scores[edge:]
    index = lax.broadcasted_iota(jnp.int32, tail.shape, 0)
    return jnp.concatenate([scores[:edge], jnp.where(index < SEQ - edge, tail, -1e30)], axis=0)


def fwd_kernel(
    info, own, other, gain, shift, wqkv, bias, wproj, normed, qkv, mixed, logsum, part, held,
    *, heads, score_scale,
):
    step, steps = pl.program_id(0), held.shape[0]
    half = own.shape[1]

    @pl.when(step == 0)
    def _():
        low, high, _ = norm_halves(*halves(info, own, other))
        for at, hat in ((0, low), (half, high)):
            cols = slice(at, at + half)
            normed[:, cols] = (hat * gain[:, cols] + shift[:, cols]).astype(jnp.bfloat16)

    block = (dot_f32(normed[...], wqkv[...]) + bias[...]).astype(jnp.bfloat16)
    qkv[...] = block
    for head in range(heads):
        base = head * 3 * DH
        queries = block[:, base : base + DH]
        key_rows = block[:, base + DH : base + 2 * DH]
        value_rows = block[:, base + 2 * DH : base + 3 * DH]
        scores = mask_keys(dot_f32(key_rows, queries * score_scale, NT))
        top = jnp.max(scores, axis=0, keepdims=True)
        exp_scores = jnp.exp(scores - top)
        total = jnp.sum(exp_scores, axis=0, keepdims=True)
        probs = (exp_scores * (1.0 / total)).astype(jnp.bfloat16)
        made = dot_f32(probs, value_rows, TN).astype(jnp.bfloat16)
        mixed[:, head * DH : (head + 1) * DH] = made
        logsum[0, head : head + 1, :] = top + jnp.log(total)
    held[step] = mixed[...]

    @pl.when(step == steps - 1)
    def _():
        whole = jnp.concatenate([held[at] for at in range(steps)], axis=1)
        part[...] = dot_f32(whole, wproj[...], NT).astype(jnp.bfloat16)


def mlp_kernel(
    info, own, other, cot_own, cot_other, mine, theirs, proj_shift, gain, shift, out_shift,
    w1, b1, w2, normed, sent, act, d_inner, d_sum, hat, inv, d_part, out_base, out_sent,
    d_acc, m_acc, *, img,
):
    step, steps = pl.program_id(0), pl.num_programs(0)
    rows, half = own.shape
    first = info[0] == 0

    @pl.when(step == 0)
    def _():
        live = row_mask(info, img, rows)
        low, high = halves(info, own, other)
        attn = mine[...].astype(jnp.float32) + theirs[...].astype(jnp.float32) + proj_shift[...]
        low = low + live * attn[:, :half]
        high = high + live * attn[:, half:]
        out_base[...] = jnp.where(first, low, high)
        low, high, inv_std = norm_halves(low, high)
        inv[...] = inv_std
        cot = halves(info, cot_own, cot_other)
        for at, part, grad in ((0, low, cot[0]), (half, high, cot[1])):
            cols = slice(at, at + half)
            hat[:, cols] = part
            normed[:, cols] = (part * gain[:, cols] + shift[:, cols]).astype(jnp.bfloat16)
            sent[:, cols] = (live * grad).astype(jnp.bfloat16)
        d_acc[...] = jnp.zeros_like(d_acc)
        m_acc[...] = jnp.zeros_like(m_acc)

    inner = dot_f32(normed[...], w1[...]) + b1[...]
    cdf = normal_cdf(inner)
    made = (inner * cdf).astype(jnp.bfloat16)
    act[...] = made
    slope = cdf + inner * jnp.exp(-0.5 * inner * inner) * (1.0 / math.sqrt(2.0 * math.pi))
    grad = dot_f32(sent[...], w2[...]) * slope
    d_sum[...] = jnp.sum(grad, axis=0, keepdims=True)
    grad = grad.astype(jnp.bfloat16)
    d_inner[...] = grad
    d_acc[...] += dot_f32(grad, w1[...], NT)
    m_acc[...] += dot_f32(made, w2[...], NT)

    @pl.when(step == steps - 1)
    def _():
        d_part[...] = d_acc[...].astype(jnp.bfloat16)
        low, high = m_acc[:, :half], m_acc[:, half:]
        live = row_mask(info, img, rows)
        out_base[...] += live * (jnp.where(first, low, high) + out_shift[...])
        out_sent[...] = (live * jnp.where(first, high, low)).astype(jnp.bfloat16)


def bwd_kernel(
    info, own, other, cot_own, cot_other, mine, theirs, gain2, gain1, hat, inv, wproj, qkv, mixed,
    logsum, wqkv, sent, d_qkv, sums, mid, sum_gain, sum_bias, sum_proj, d_own, d_sent, hat_own,
    inv_one, row_sums, sum_hat, sum_plain, d_mixed, acc, *, img, heads, score_scale,
):
    step, steps = pl.program_id(0), pl.num_programs(0)
    rows, half = own.shape
    full_width = float(2 * half)
    first = info[0] == 0

    @pl.when(step == 0)
    def _():
        live = row_mask(info, img, rows)
        grad = mine[...].astype(jnp.float32) + theirs[...].astype(jnp.float32)
        scaled = grad * gain2[...]
        back = inv[...] * (
            scaled
            - jnp.sum(scaled, axis=1, keepdims=True) / full_width
            - hat[...] * (jnp.sum(scaled * hat[...], axis=1, keepdims=True) / full_width)
        )
        sum_gain[...] = jnp.sum(grad * hat[...], axis=0, keepdims=True)
        sum_bias[...] = jnp.sum(grad, axis=0, keepdims=True)
        low, high = halves(info, cot_own, cot_other)
        low, high = low + back[:, :half], high + back[:, half:]
        mid[...] = jnp.where(first, low, high)
        for at, part in ((0, low), (half, high)):
            cols = slice(at, at + half)
            masked = live * part
            sum_proj[:, cols] = jnp.sum(masked, axis=0, keepdims=True)
            sent[:, cols] = masked.astype(jnp.bfloat16)
        made = dot_f32(sent[...], wproj[...]).astype(jnp.bfloat16)
        for at in range(d_mixed.shape[0]):
            d_mixed[at] = made[:, at * heads * DH : (at + 1) * heads * DH]
        acc[...] = jnp.zeros_like(acc)

    for head in range(heads):
        base = head * 3 * DH
        queries = qkv[:, base : base + DH]
        key_rows = qkv[:, base + DH : base + 2 * DH]
        value_rows = qkv[:, base + 2 * DH : base + 3 * DH]
        out = mixed[:, head * DH : (head + 1) * DH]
        d_out = d_mixed[step, :, head * DH : (head + 1) * DH]
        products = d_out.astype(jnp.float32) * out.astype(jnp.float32)
        delta = jnp.sum(jnp.transpose(products), axis=0, keepdims=True)
        scores = mask_keys(dot_f32(key_rows, queries * score_scale, NT))
        probs = jnp.exp(scores - logsum[0, head : head + 1, :])
        d_probs = dot_f32(value_rows, d_out, NT)
        d_scores = (probs * (d_probs - delta)).astype(jnp.bfloat16)
        d_query = dot_f32(d_scores, key_rows, TN) * score_scale
        d_keys = dot_f32(d_scores, queries, NN) * score_scale
        d_values = dot_f32(probs.astype(jnp.bfloat16), d_out, NN)
        for at, grad in enumerate((d_query, d_keys, d_values)):
            cols = slice(base + at * DH, base + (at + 1) * DH)
            d_qkv[:, cols] = grad.astype(jnp.bfloat16)
            sums[:, cols] = jnp.sum(grad, axis=0, keepdims=True)
    acc[...] += dot_f32(d_qkv[...], wqkv[...], NT)

    @pl.when(step == steps - 1)
    def _():
        low, high, inv_std = norm_halves(*halves(info, own, other))
        inv_one[...] = inv_std
        hat_own[...] = jnp.where(first, low, high)
        left, right = acc[:, :half], acc[:, half:]
        d_own[...] = jnp.where(first, left, right)
        d_sent[...] = jnp.where(first, right, left).astype(jnp.bfloat16)
        for at, grad, part in ((0, left, low), (half, right, high)):
            columns = slice(at, at + half)
            sum_hat[:, columns] = jnp.sum(grad * part, axis=0, keepdims=True)
            sum_plain[:, columns] = jnp.sum(grad, axis=0, keepdims=True)
        left, right = left * gain1[:, :half], right * gain1[:, half:]
        plain = jnp.sum(left, axis=1, keepdims=True) + jnp.sum(right, axis=1, keepdims=True)
        hatted = jnp.sum(left * low, axis=1, keepdims=True) + jnp.sum(
            right * high, axis=1, keepdims=True
        )
        lane = lax.broadcasted_iota(jnp.int32, (rows, 128), 1)
        both = jnp.where(lane == 0, plain, jnp.where(lane == 1, hatted, 0.0))
        row_sums[...] = jnp.transpose(both)[:8]


def pair_grad_kernel(left0, left1, right0, right1, more0, more1, rest0, rest1, out, held, *, cut):
    step = pl.program_id(0)

    def load(one, two):
        held[...] = jnp.concatenate([one[...], two[...]], axis=0)

    def make(one, two):
        right = jnp.concatenate([one[...], two[...]], axis=0)
        out[...] = dot_f32(held[...], right, TN).astype(jnp.bfloat16)

    pl.when(step == 0)(lambda: load(left0, left1))
    pl.when(step == cut)(lambda: load(more0, more1))
    pl.when(step < cut)(lambda: make(right0, right1))
    pl.when(step >= cut)(lambda: make(rest0, rest1))


SCALARS = pl.BlockSpec(memory_space=pltpu.SMEM)
PARAMS = pltpu.CompilerParams(vmem_limit_bytes=56 * 1024 * 1024)


def whole(shape):
    return pl.BlockSpec(shape, lambda s: (0,) * len(shape))


def cols(rows, width, start=0):
    return pl.BlockSpec((rows, width), lambda s: (0, start + s))


def cost(flops, moved):
    return pl.CostEstimate(flops=flops, bytes_accessed=moved, transcendentals=0)


def shaped(*shapes):
    return [jax.ShapeDtypeStruct(shape, kind) for shape, kind in shapes]


F32, BF16 = jnp.float32, jnp.bfloat16


def forward(info, own, other, gain, shift, early, bias, score_scale):
    rows, half = own.shape
    wide, total = early.shape
    inner = total - bias.shape[1]
    heads = 2
    steps = inner // (heads * DH)
    span = heads * 3 * DH
    return pl.pallas_call(
        functools.partial(fwd_kernel, heads=heads, score_scale=score_scale),
        grid=(steps,),
        in_specs=[
            SCALARS, whole((rows, half)), whole((rows, half)), whole((1, wide)), whole((1, wide)),
            cols(wide, span), cols(1, span),
            pl.BlockSpec((wide, inner), lambda s: (0, bias.shape[1] // inner)),
        ],
        out_specs=[
            whole((rows, wide)), cols(rows, span), cols(rows, heads * DH),
            pl.BlockSpec((1, 8, rows), lambda s: (s, 0, 0)), whole((rows, wide)),
        ],
        out_shape=shaped(
            ((rows, wide), BF16), ((rows, steps * span), BF16), ((rows, inner), BF16),
            ((steps, 8, rows), F32), ((rows, wide), BF16),
        ),
        scratch_shapes=[pltpu.VMEM((steps, rows, heads * DH), BF16)],
        compiler_params=PARAMS,
        cost_estimate=cost(3_000_000_000, 3_000_000),
        name="attention_forward",
    )(info, own, other, gain, shift, early, bias, early)


def mlp_pass(info, img, own, other, cot_own, cot_other, mine, theirs, vectors, out_shift, late, b1):
    rows, half = own.shape
    wide = late.shape[0]
    hidden = b1.shape[1]
    tile = 512
    steps = hidden // tile
    proj_shift, gain, shift = vectors
    return pl.pallas_call(
        functools.partial(mlp_kernel, img=img),
        grid=(steps,),
        in_specs=[
            SCALARS, *[whole((rows, half))] * 4, *[whole((rows, wide))] * 2, *[whole((1, wide))] * 3,
            whole((1, half)), cols(wide, tile), cols(1, tile), cols(wide, tile, steps),
        ],
        out_specs=[
            whole((rows, wide)), whole((rows, wide)), cols(rows, tile), cols(rows, tile),
            cols(1, tile), whole((rows, wide)), whole((rows, 1)), whole((rows, wide)),
            whole((rows, half)), whole((rows, half)),
        ],
        out_shape=shaped(
            ((rows, wide), BF16), ((rows, wide), BF16), ((rows, hidden), BF16),
            ((rows, hidden), BF16), ((1, hidden), F32), ((rows, wide), F32), ((rows, 1), F32),
            ((rows, wide), BF16), ((rows, half), F32), ((rows, half), BF16),
        ),
        scratch_shapes=[pltpu.VMEM((rows, wide), F32), pltpu.VMEM((rows, wide), F32)],
        compiler_params=PARAMS,
        cost_estimate=cost(4_000_000_000, 8_000_000),
        name="feed_forward",
    )(info, own, other, cot_own, cot_other, mine, theirs, proj_shift, gain, shift, out_shift,
      late, b1, late)


def backward(
    info, img, own, other, cot_own, cot_other, mine, theirs, gain2, gain1, hat, inv, early, qkv,
    mixed, logsum, score_scale,
):
    rows, half = own.shape
    wide = early.shape[0]
    inner = mixed.shape[1]
    heads = 2
    steps = inner // (heads * DH)
    span = heads * 3 * DH
    return pl.pallas_call(
        functools.partial(bwd_kernel, img=img, heads=heads, score_scale=score_scale),
        grid=(steps,),
        in_specs=[
            SCALARS, *[whole((rows, half))] * 4, *[whole((rows, wide))] * 2, *[whole((1, wide))] * 2,
            whole((rows, wide)), whole((rows, 1)),
            pl.BlockSpec((wide, inner), lambda s: (0, qkv.shape[1] // inner)),
            cols(rows, span), cols(rows, heads * DH),
            pl.BlockSpec((1, 8, rows), lambda s: (s, 0, 0)), cols(wide, span),
        ],
        out_specs=[
            whole((rows, wide)), cols(rows, span), cols(1, span), whole((rows, half)),
            whole((1, wide)), whole((1, wide)), whole((1, wide)), whole((rows, half)),
            whole((rows, half)), whole((rows, half)), whole((rows, 1)), whole((8, rows)),
            whole((1, wide)), whole((1, wide)),
        ],
        out_shape=shaped(
            ((rows, wide), BF16), ((rows, 3 * inner), BF16), ((1, 3 * inner), F32),
            ((rows, half), F32), ((1, wide), F32), ((1, wide), F32), ((1, wide), F32),
            ((rows, half), F32), ((rows, half), BF16), ((rows, half), F32), ((rows, 1), F32),
            ((8, rows), F32), ((1, wide), F32), ((1, wide), F32),
        ),
        scratch_shapes=[
            pltpu.VMEM((steps, rows, heads * DH), BF16), pltpu.VMEM((rows, wide), F32)
        ],
        compiler_params=PARAMS,
        cost_estimate=cost(5_000_000_000, 8_000_000),
        name="attention_backward",
    )(info, own, other, cot_own, cot_other, mine, theirs, gain2, gain1, hat, inv, early, qkv, mixed,
      logsum, early)


def pair_grads(lefts, rights, mores, rests, tile=512):
    rows, wide = lefts[0].shape
    first, second = rights[0].shape[1] // tile, rests[0].shape[1] // tile
    left = whole((rows, wide))
    right = pl.BlockSpec((rows, tile), lambda s: (0, jnp.minimum(s, first - 1)))
    rest = pl.BlockSpec((rows, tile), lambda s: (0, jnp.maximum(s - first, 0)))
    return pl.pallas_call(
        functools.partial(pair_grad_kernel, cut=first),
        grid=(first + second,),
        in_specs=[left, left, right, right, left, left, rest, rest],
        out_specs=cols(wide, tile),
        out_shape=jax.ShapeDtypeStruct((wide, (first + second) * tile), BF16),
        scratch_shapes=[pltpu.VMEM((2 * rows, wide), BF16)],
        compiler_params=PARAMS,
        cost_estimate=cost(rows * wide * (first + second) * tile, 5_000_000),
        name="weight_gradients",
    )(*lefts, *rights, *mores, *rests)


MESH = pl.DeviceIdType.MESH


def place():
    index = lax.axis_index("wide")
    return index, lax.div(index, 4), lax.rem(lax.div(index, 2), 2), lax.rem(index, 2)


def greet(partners):
    barrier = pltpu.get_barrier_semaphore()
    count = 0
    for when, device in partners:
        def signal(device=device):
            pl.semaphore_signal(barrier, inc=1, device_id=device, device_id_type=MESH)

        if when is None:
            signal()
            count = count + 1
        else:
            pl.when(when)(signal)
            count = count + when.astype(jnp.int32)
    pl.semaphore_wait(barrier, count)


def gather_kernel(shard, *refs, deep, extra):
    rows, out, moved = refs[:extra], refs[extra], refs[extra + 1 : 2 * extra + 1]
    here_sem, send_sem, recv_sem, x_send, x_recv = refs[2 * extra + 1 :]
    index, z, y, core = place()
    across = {"narrow": 1 - lax.axis_index("narrow")}
    beside, near = index + 2 - 4 * y, index + 1 - 2 * core
    more, less = z + 1 < deep, z > 0
    greet([
        (None, across), (None, {"wide": beside}), (None, {"wide": near}),
        (more, {"wide": index + 4}), (less, {"wide": index - 4}),
    ])
    sent = []

    def build(owner, way, target, source):
        return pltpu.make_async_remote_copy(
            src_ref=source, dst_ref=out.at[owner], send_sem=send_sem.at[owner, way],
            recv_sem=recv_sem.at[owner], device_id={"wide": target}, device_id_type=MESH,
        )

    def guarded(when, step):
        if when is None:
            step()
        else:
            pl.when(when)(step)

    def send(when, owner, way, target, source=None):
        source = out.at[owner] if source is None else source
        guarded(when, lambda: build(owner, way, target, source).start())
        sent.append((when, owner, way, target, source))

    def arrive(when, owner):
        guarded(when, lambda: build(owner, 0, near, out.at[owner]).wait_recv())

    swaps = [
        pltpu.make_async_remote_copy(
            src_ref=source, dst_ref=target, send_sem=x_send.at[at], recv_sem=x_recv.at[at],
            device_id=across, device_id_type=MESH,
        )
        for at, (source, target) in enumerate(zip(rows, moved))
    ]
    send(more, index, 0, index + 4, shard)
    send(less, index, 1, index - 4, shard)
    send(None, index, 2, beside, shard)
    send(None, index, 3, near, shard)
    for copy in swaps:
        copy.start()
    here = pltpu.make_async_copy(shard, out.at[index], here_sem)
    here.start()
    for step in range(1, deep):
        for sign, way, onward in ((-1, 0, more), (1, 1, less)):
            owner = index + 4 * sign * step
            holds = z >= step if sign < 0 else z + step < deep
            arrive(holds, owner)
            send(holds & onward, owner, way, index - 4 * sign)
            send(holds, owner, 2, beside)
            send(holds, owner, 3, near)
        owner = beside
        for owner, holds in (
            [(beside, None)] if step == 1 else []
        ) + [(beside - 4 * step, z >= step), (beside + 4 * step, z + step < deep)]:
            arrive(holds, owner)
            send(holds, owner, 3, near)
    base = 1 - core
    for other in range(2 * deep):
        arrive(None, 2 * other + base)
    for copy in swaps:
        copy.wait()
    here.wait()
    for when, owner, way, target, source in sent:
        guarded(when, lambda: build(owner, way, target, source).wait_send())


def gather_early(shard, rows):
    count, extra = lax.axis_size("wide"), len(rows)
    anywhere = pl.BlockSpec(memory_space=pl.ANY)
    dma = pltpu.SemaphoreType.DMA
    out, *moved = pl.pallas_call(
        functools.partial(gather_kernel, deep=count // 4, extra=extra),
        in_specs=[anywhere] * (1 + extra),
        out_specs=[anywhere] * (1 + extra),
        out_shape=[jax.ShapeDtypeStruct((count, *shard.shape), shard.dtype)]
        + [jax.ShapeDtypeStruct(part.shape, part.dtype) for part in rows],
        scratch_shapes=[dma, dma((count, 4)), dma((count,)), dma((extra,)), dma((extra,))],
        compiler_params=pltpu.CompilerParams(collective_id=0, has_side_effects=True),
        cost_estimate=cost(15_000_000_000, 8_000_000),
        name="gather_early",
    )(shard, *rows)
    return out.reshape(count * shard.shape[0], shard.shape[1]), moved


def scatter_kernel(
    grads, vector, out, vector_out, near_in, side_out, side_in, line_out, line_in, sums,
    v_near, v_side, v_line, near_send, near_recv, side_send, side_recv, line_send, line_recv,
    v_send, v_recv, *, deep,
):
    index, z, y, core = place()
    beside, near = {"wide": index + 2 - 4 * y}, {"wide": index + 1 - 2 * core}
    more, less = z + 1 < deep, z > 0
    column = lax.rem(index, 4)
    greet([(None, beside), (None, near)] + [
        (z != at, {"wide": 4 * at + column}) for at in range(deep)
    ])

    def remote(source, target, send, recv, device):
        return pltpu.make_async_remote_copy(
            src_ref=source, dst_ref=target, send_sem=send, recv_sem=recv, device_id=device,
            device_id_type=MESH,
        )

    def add(*parts):
        return functools.reduce(lambda a, b: a + b, [part.astype(jnp.float32) for part in parts])

    order = [at for pair in zip(range(deep - 1, -1, -1), range(deep)) for at in pair][:deep]
    waits = []

    def to_near(at, side):
        slot = 2 * at + side
        copy = remote(
            grads.at[2 * slot + 1 - core], near_in.at[slot], near_send.at[slot],
            near_recv.at[slot], near,
        )
        return copy

    near_copies = {}
    v_copy = remote(vector, v_near, v_send.at[0], v_recv.at[0], near)
    v_copy.start()
    for part in (0, 1):
        side = 1 - y if part == 0 else y
        for at in order:
            near_copies[part, at] = to_near(at, side)
            near_copies[part, at].start()
    v_copy.wait()
    v_near[...] += vector[...]
    v_copy = remote(v_near, v_side, v_send.at[1], v_recv.at[1], beside)
    v_copy.start()

    side_copies = {}
    for at in order:
        slot = 2 * at + 1 - y
        near_copies[0, at].wait_recv()
        side_out[at] = add(grads[2 * slot + core], near_in[slot]).astype(jnp.bfloat16)
        side_copies[at] = remote(
            side_out.at[at], side_in.at[at], side_send.at[at], side_recv.at[at], beside
        )
        side_copies[at].start()
    v_copy.wait()
    v_line[z] = v_near[...] + v_side[...]
    v_pushes = [
        (z != at, remote(v_line.at[z], v_line.at[z], v_send.at[2 + at], v_recv.at[2 + z],
                         {"wide": 4 * at + column}))
        for at in range(deep)
    ]
    for when, copy in v_pushes:
        pl.when(when)(copy.start)

    def hop(at, way):
        slot = at * 2 + way
        return remote(
            line_out.at[at], line_in.at[slot], line_send.at[at], line_recv.at[slot],
            {"wide": index + (4 if way == 0 else -4)},
        )

    for at in order:
        slot = 2 * at + y
        near_copies[1, at].wait_recv()
        side_copies[at].wait_recv()
        sums[at] = add(grads[2 * slot + core], near_in[slot], side_in[at])
        for way, goes, joins in ((0, z < at, z > 0), (1, z > at, z < deep - 1)):
            @pl.when(goes & joins)
            def _(way=way):
                hop(at, way).wait_recv()
                line_out[at] = (sums[at] + line_in[2 * at + way].astype(jnp.float32)).astype(
                    jnp.bfloat16
                )
                hop(at, way).start()

            @pl.when(goes & ~joins)
            def _(way=way):
                line_out[at] = sums[at].astype(jnp.bfloat16)
                hop(at, way).start()

    for at in range(deep):
        @pl.when(z == at)
        def _():
            out[...] = sums[at]
            if at > 0:
                hop(at, 0).wait_recv()
                out[...] += line_in[2 * at].astype(jnp.float32)
            if at < deep - 1:
                hop(at, 1).wait_recv()
                out[...] += line_in[2 * at + 1].astype(jnp.float32)

        @pl.when(z != at)
        def _():
            hop(at, 0).wait_send()
            remote(v_line.at[at], v_line.at[at], v_send.at[2 + at], v_recv.at[2 + at],
                   near).wait_recv()
            remote(v_line.at[z], v_line.at[z], v_send.at[2 + at], v_recv.at[2 + z],
                   near).wait_send()
    total = v_line[0]
    for at in range(1, deep):
        total = total + v_line[at]
    vector_out[...] = total
    for copy in near_copies.values():
        copy.wait_send()
    for copy in side_copies.values():
        copy.wait_send()


def scatter_late(grads, vector):
    count = lax.axis_size("wide")
    deep = count // 4
    rows, width = grads.shape[0] // count, grads.shape[1]
    block = (rows, width)
    inside = pl.BlockSpec(memory_space=pltpu.VMEM)
    dma = pltpu.SemaphoreType.DMA
    return pl.pallas_call(
        functools.partial(scatter_kernel, deep=deep),
        in_specs=[inside] * 2,
        out_specs=[inside] * 2,
        out_shape=shaped((block, F32), (vector.shape, F32)),
        scratch_shapes=[
            pltpu.VMEM((2 * deep, *block), BF16), pltpu.VMEM((deep, *block), BF16),
            pltpu.VMEM((deep, *block), BF16), pltpu.VMEM((deep, *block), BF16),
            pltpu.VMEM((2 * deep, *block), BF16), pltpu.VMEM((deep, *block), F32),
            pltpu.VMEM(vector.shape, F32), pltpu.VMEM(vector.shape, F32),
            pltpu.VMEM((deep, *vector.shape), F32),
            dma((2 * deep,)), dma((2 * deep,)), dma((deep,)), dma((deep,)), dma((deep,)),
            dma((2 * deep,)), dma((2 + deep,)), dma((2 + deep,)),
        ],
        compiler_params=pltpu.CompilerParams(
            collective_id=1, has_side_effects=True, vmem_limit_bytes=56 * 1024 * 1024
        ),
        cost_estimate=cost(15_000_000_000, 8_000_000),
        name="scatter_late",
    )(grads.reshape(count, rows, width), vector)


def shards_pair(
    inputs, counts, ln1_gain, ln1_bias, w_qkv, qv_bias, w_proj, proj_bias, ln2_gain, ln2_bias,
    w_fc1, fc1_bias, w_fc2, fc2_bias, cotangent,
):
    me = lax.axis_index("narrow")
    row_count, half = inputs.shape
    images = row_count // SEQ
    rows = -(-SEQ // ROW_TILE) * ROW_TILE
    head_count = w_qkv.shape[1] // (3 * DH)
    score_scale = 1.0 / math.sqrt(DH)
    span = range(images)
    info = jnp.stack([me.astype(jnp.int32), counts[0]])

    def slot(array, img):
        return jnp.pad(array[img * SEQ : (img + 1) * SEQ], ((0, rows - SEQ), (0, 0)))

    def own(vector):
        return lax.dynamic_slice_in_dim(vector, me * half, half, vector.ndim - 1)

    mine = [slot(inputs, i) for i in span]
    vectors = widen(jnp.stack([ln1_gain, ln1_bias, ln2_gain, ln2_bias, proj_bias]), me, 2)
    gain_one, shift_one, gain_two, shift_two, proj_shift = (vectors[i : i + 1] for i in range(5))
    late = lax.all_gather(jnp.concatenate([w_fc1, w_fc2.T], axis=1), "wide", axis=0, tiled=True)
    cot = [slot(cotangent, i) for i in span]
    early, moved = gather_early(jnp.concatenate([w_qkv, w_proj.T], axis=1), mine + cot)
    theirs, cot_theirs = moved[:images], moved[images:]

    bias_qv = qv_bias.reshape(head_count, 2, DH)
    bias_full = jnp.stack(
        [bias_qv[:, 0], jnp.zeros_like(bias_qv[:, 0]), bias_qv[:, 1]], axis=1
    ).reshape(1, head_count * 3 * DH)

    front = [
        forward(info, mine[i], theirs[i], gain_one, shift_one, early, bias_full, score_scale)
        for i in span
    ]
    normed1, qkv, mixed, logsum, part = zip(*front)
    part_theirs = [swap(x) for x in part]
    middle = [
        mlp_pass(
            info, i, mine[i], theirs[i], cot[i], cot_theirs[i], part[i], part_theirs[i],
            (proj_shift, gain_two, shift_two), fc2_bias.reshape(1, -1), late,
            fc1_bias.reshape(1, -1),
        )
        for i in span
    ]
    normed2, sent2, act, d_inner, d_sum, hat2, inv2, d_part, out_base, out_sent = zip(*middle)
    d_theirs = [swap(x) for x in d_part]
    out_theirs = [swap(x) for x in out_sent]
    grad_fc = pair_grads(normed2, d_inner, sent2, act)
    d_theirs, grad_fc = lax.optimization_barrier((d_theirs, grad_fc))
    grad_fc = lax.psum_scatter(grad_fc, "wide", scatter_dimension=0, tiled=True)
    ends = [
        backward(
            info, i, mine[i], theirs[i], cot[i], cot_theirs[i], d_part[i], d_theirs[i], gain_two,
            gain_one, hat2[i], inv2[i], early, qkv[i], mixed[i], logsum[i], score_scale,
        )
        for i in span
    ]
    (sent1, d_qkv, qkv_sums, mid, sum_gain, sum_bias, sum_proj, d_own, d_sent, hat_own, inv_one,
     row_sums, sum_hat, sum_plain) = zip(*ends)
    d_moved = [swap(x) for x in d_sent]
    row_sums = [x + swap(x) for x in row_sums]
    d_qkv, out_theirs = lax.optimization_barrier((d_qkv, out_theirs))
    grad_attn = pair_grads(normed1, d_qkv, sent1, mixed)

    qkv_sums = sum(qkv_sums).reshape(head_count, 3, DH)
    grad_qv = jnp.stack([qkv_sums[:, 0], qkv_sums[:, 2]], axis=1).reshape(-1)
    own_cot = sum(
        jnp.sum(jnp.where(counts[0] > i, cot[i].astype(F32), 0.0), axis=0) for i in span
    )
    first_sums = jnp.concatenate([sum(sum_hat), sum(sum_plain)], axis=0)
    first_sums = first_sums + swap(first_sums)
    joined = jnp.concatenate(
        [
            grad_qv, own(sum(sum_proj))[0], own(sum(sum_gain))[0], own(sum(sum_bias))[0],
            sum(d_sum)[0], own_cot, own(first_sums).reshape(-1),
        ]
    )
    grad_attn, joined = scatter_late(grad_attn, joined.reshape(-1, 128))
    joined = joined.reshape(-1)

    output = jnp.concatenate(
        [(out_base[i] + out_theirs[i].astype(F32)).astype(BF16)[:SEQ] for i in span], axis=0
    )
    full_width = float(2 * half)
    grads_in = []
    for i in span:
        d_norm1 = d_own[i] + d_moved[i].astype(F32)
        back = inv_one[i] * (
            d_norm1 * ln1_gain
            - row_sums[i][0][:, None] / full_width
            - hat_own[i] * (row_sums[i][1][:, None] / full_width)
        )
        grads_in.append((mid[i] + back).astype(BF16)[:SEQ])
    grad_in = jnp.concatenate(grads_in, axis=0)
    qv, ff = grad_qv.shape[0], fc1_bias.shape[0]
    edges = [0]
    for extent in (qv, half, half, half, ff, half, half, half):
        edges.append(edges[-1] + extent)
    pieces = [joined[a:b] for a, b in zip(edges[:-1], edges[1:])]
    split_attn, split_fc = w_qkv.shape[1], w_fc1.shape[1]
    return (
        output,
        grad_in,
        pieces[6],
        pieces[7],
        grad_attn[:, :split_attn],
        pieces[0],
        grad_attn[:, split_attn:].T,
        pieces[1],
        pieces[2],
        pieces[3],
        grad_fc[:, :split_fc].astype(F32),
        pieces[4],
        grad_fc[:, split_fc:].T.astype(F32),
        pieces[5],
    )


def shards(*arrays):
    if lax.axis_size("narrow") == 2:
        return shards_pair(*arrays)
    return shards_any(*arrays)


def solution(mesh):
    return jax.shard_map(
        shards,
        mesh=mesh,
        in_specs=(
            P("wide", "narrow"),
            P("wide"),
            P("narrow"),
            P("narrow"),
            P("wide", "narrow"),
            P("narrow"),
            P("narrow", "wide"),
            P("narrow"),
            P("narrow"),
            P("narrow"),
            P("wide", "narrow"),
            P("narrow"),
            P("narrow", "wide"),
            P("narrow"),
            P("wide", "narrow"),
        ),
        out_specs=(
            P("wide", "narrow"),
            P("wide", "narrow"),
            P("narrow"),
            P("narrow"),
            P("wide", "narrow"),
            P("narrow"),
            P("narrow", "wide"),
            P("narrow"),
            P("narrow"),
            P("narrow"),
            P("wide", "narrow"),
            P("narrow"),
            P("narrow", "wide"),
            P("narrow"),
        ),
        check_vma=False,
    )
```

```python
import functools
import math

import jax
import jax.numpy as jnp
from jax import lax
from jax.experimental import pallas as pl
from jax.experimental.pallas import tpu as pltpu
from jax.sharding import PartitionSpec as P

DH = 64
SEQ = 577
ROW_TILE = 16


norm_eps = 1e-06
NT = (((1,), (1,)), ((), ()))
TN = (((0,), (0,)), ((), ()))
NN = (((1,), (0,)), ((), ()))


def dot_f32(left_mat, right_mat, dims=NN):
    return lax.dot_general(left_mat, right_mat, dims, preferred_element_type=jnp.float32)


def swap(piece):
    return lax.ppermute(piece, "narrow", ((0, 1), (1, 0)))


def widen(piece, me, size):
    if size != 2:
        return lax.all_gather(piece, "narrow", axis=1, tiled=True)
    other = swap(piece)
    return jnp.concatenate(
        [jnp.where(me == 0, piece, other), jnp.where(me == 0, other, piece)], axis=1
    )


def sum_whole(partial_rows, size):
    if size != 2:
        return lax.psum(partial_rows, "narrow")
    mine = partial_rows.astype(jnp.bfloat16)
    return mine.astype(jnp.float32) + swap(mine).astype(jnp.float32)


def sum_own(left_mat, right_rows, me, size, width):
    if size != 2:
        return lax.psum_scatter(
            dot_f32(left_mat, right_rows, NT), "narrow", scatter_dimension=1, tiled=True
        )
    theirs = lax.dynamic_slice_in_dim(right_rows, (1 - me) * width, width, 0)
    ours = lax.dynamic_slice_in_dim(right_rows, me * width, width, 0)
    moved = swap(dot_f32(left_mat, theirs, NT).astype(jnp.bfloat16))
    return dot_f32(left_mat, ours, NT) + moved.astype(jnp.float32)


def normal_cdf(values_in):
    return 0.5 * (1.0 + lax.erf(values_in * (1.0 / math.sqrt(2.0))))


def gelu_exact(values_in):
    return values_in * normal_cdf(values_in)


def gelu_slope(values_in):
    return normal_cdf(values_in) + values_in * jnp.exp(-0.5 * values_in * values_in) * (
        1.0 / math.sqrt(2.0 * math.pi)
    )


def norm_forward(rows_in, gain_vec, shift_vec):
    width = float(rows_in.shape[1])
    center = jnp.sum(rows_in, axis=1, keepdims=True) / width
    spread = jnp.sum(rows_in * rows_in, axis=1, keepdims=True) / width - center * center
    inv_std = lax.rsqrt(spread + norm_eps)
    normalized = (rows_in - center) * inv_std
    return (normalized, inv_std, (normalized * gain_vec + shift_vec).astype(jnp.bfloat16))


def scores_by_key(queries, key_rows, score_scale):
    scores = dot_f32(key_rows, queries, NT) * score_scale
    key_index = lax.broadcasted_iota(jnp.int32, scores.shape, 0)
    return jnp.where(key_index < SEQ, scores, -1e30)


def attend_kernel(qkv_ref, mixed_ref, logsum_ref, *, heads, score_scale):
    for head in range(heads):
        base = head * 3 * DH
        queries = qkv_ref[:, base : base + DH]
        key_rows = qkv_ref[:, base + DH : base + 2 * DH]
        value_rows = qkv_ref[:, base + 2 * DH : base + 3 * DH]
        scores = scores_by_key(queries, key_rows, score_scale)
        top = jnp.max(scores, axis=0, keepdims=True)
        exp_scores = jnp.exp(scores - top)
        total = jnp.sum(exp_scores, axis=0, keepdims=True)
        probs = (exp_scores * (1.0 / total)).astype(jnp.bfloat16)
        mixed_ref[:, head * DH : (head + 1) * DH] = dot_f32(probs, value_rows, TN).astype(
            jnp.bfloat16
        )
        logsum_ref[0, head : head + 1, :] = top + jnp.log(total)


def attend_back_kernel(
    qkv_ref, mixed_ref, d_mixed_ref, logsum_ref, d_qkv_ref, sums_ref, *, heads, score_scale
):
    for head in range(heads):
        base = head * 3 * DH
        queries = qkv_ref[:, base : base + DH]
        key_rows = qkv_ref[:, base + DH : base + 2 * DH]
        value_rows = qkv_ref[:, base + 2 * DH : base + 3 * DH]
        mixed = mixed_ref[:, head * DH : (head + 1) * DH]
        d_mixed = d_mixed_ref[:, head * DH : (head + 1) * DH]
        products = d_mixed.astype(jnp.float32) * mixed.astype(jnp.float32)
        delta = jnp.sum(jnp.transpose(products), axis=0, keepdims=True)
        scores = scores_by_key(queries, key_rows, score_scale)
        probs = jnp.exp(scores - logsum_ref[0, head : head + 1, :])
        d_probs = dot_f32(value_rows, d_mixed, NT)
        d_scores = (probs * (d_probs - delta)).astype(jnp.bfloat16)
        d_query = dot_f32(d_scores, key_rows, TN) * score_scale
        d_keys = dot_f32(d_scores, queries, NN) * score_scale
        d_values = dot_f32(probs.astype(jnp.bfloat16), d_mixed, NN)
        for part, grad in enumerate((d_query, d_keys, d_values)):
            columns = slice(base + part * DH, base + (part + 1) * DH)
            d_qkv_ref[:, columns] = grad.astype(jnp.bfloat16)
            sums_ref[0, :, columns] = jnp.broadcast_to(
                jnp.sum(grad, axis=0, keepdims=True), (8, DH)
            )


def head_pairs(width):
    heads = 2
    return heads, width // (3 * DH * heads)


def attend(qkv_rows, slot_rows, score_scale):
    row_count, width = qkv_rows.shape
    slots = row_count // slot_rows
    heads, pairs = head_pairs(width)
    return pl.pallas_call(
        functools.partial(attend_kernel, heads=heads, score_scale=score_scale),
        grid=(slots, pairs),
        in_specs=[pl.BlockSpec((slot_rows, heads * 3 * DH), lambda s, p: (s, p))],
        out_specs=[
            pl.BlockSpec((slot_rows, heads * DH), lambda s, p: (s, p)),
            pl.BlockSpec((1, 8, slot_rows), lambda s, p: (s * pairs + p, 0, 0)),
        ],
        out_shape=[
            jax.ShapeDtypeStruct((row_count, width // 3), jnp.bfloat16),
            jax.ShapeDtypeStruct((slots * pairs, 8, slot_rows), jnp.float32),
        ],
        cost_estimate=pl.CostEstimate(
            flops=4 * slots * pairs * heads * slot_rows * slot_rows * 256,
            bytes_accessed=row_count * width * 3,
            transcendentals=slots * pairs * heads * slot_rows * slot_rows,
        ),
        name="attend",
    )(qkv_rows)


def attend_backward(qkv_rows, mixed_rows, d_mixed, logsum, slot_rows, score_scale):
    row_count, width = qkv_rows.shape
    slots = row_count // slot_rows
    heads, pairs = head_pairs(width)
    narrow_block = pl.BlockSpec((slot_rows, heads * DH), lambda s, p: (s, p))
    wide_block = pl.BlockSpec((slot_rows, heads * 3 * DH), lambda s, p: (s, p))
    return pl.pallas_call(
        functools.partial(attend_back_kernel, heads=heads, score_scale=score_scale),
        grid=(slots, pairs),
        in_specs=[
            wide_block,
            narrow_block,
            narrow_block,
            pl.BlockSpec((1, 8, slot_rows), lambda s, p: (s * pairs + p, 0, 0)),
        ],
        out_specs=[
            wide_block,
            pl.BlockSpec((1, 8, heads * 3 * DH), lambda s, p: (s, 0, p)),
        ],
        out_shape=[
            jax.ShapeDtypeStruct((row_count, width), jnp.bfloat16),
            jax.ShapeDtypeStruct((slots, 8, width), jnp.float32),
        ],
        cost_estimate=pl.CostEstimate(
            flops=10 * slots * pairs * heads * slot_rows * slot_rows * 256,
            bytes_accessed=row_count * width * 6,
            transcendentals=slots * pairs * heads * slot_rows * slot_rows,
        ),
        name="attend_back",
    )(qkv_rows, mixed_rows, d_mixed, logsum)


def shards_any(
    inputs,
    counts,
    ln1_gain,
    ln1_bias,
    w_qkv,
    qv_bias,
    w_proj,
    proj_bias,
    ln2_gain,
    ln2_bias,
    w_fc1,
    fc1_bias,
    w_fc2,
    fc2_bias,
    cotangent,
):
    size = lax.axis_size("narrow")
    me = lax.axis_index("narrow")
    row_count, width = inputs.shape
    slot_count = row_count // SEQ
    slot_rows = -(-SEQ // ROW_TILE) * ROW_TILE
    padded = slot_count * slot_rows
    head_count = w_qkv.shape[1] // (3 * DH)
    score_scale = 1.0 / math.sqrt(DH)

    def pad_rows(rows):
        rows = rows.reshape(slot_count, SEQ, rows.shape[1])
        rows = jnp.pad(rows, ((0, 0), (0, slot_rows - SEQ), (0, 0)))
        return rows.reshape(padded, rows.shape[2])

    def trim_rows(rows):
        rows = rows.reshape(slot_count, slot_rows, rows.shape[1])[:, :SEQ]
        return rows.reshape(row_count, rows.shape[2])

    def own(rows):
        return lax.dynamic_slice_in_dim(rows, me * width, width, rows.ndim - 1)

    padded_index = lax.broadcasted_iota(jnp.int32, (padded, 1), 0)
    live_rows = (
        (padded_index // slot_rows < counts[0]) & (padded_index % slot_rows < SEQ)
    ).astype(jnp.float32)

    early = lax.all_gather(
        jnp.concatenate([w_qkv, w_proj.T], axis=1), "wide", axis=0, tiled=True
    )
    wqkv_full = early[:, : w_qkv.shape[1]]
    wproj_t = early[:, w_qkv.shape[1] :]
    late = lax.all_gather(
        jnp.concatenate([w_fc1, w_fc2.T], axis=1), "wide", axis=0, tiled=True
    )
    wfc1_full = late[:, : w_fc1.shape[1]]
    wfc2_t = late[:, w_fc1.shape[1] :]

    vectors = widen(
        jnp.stack([ln1_gain, ln1_bias, ln2_gain, ln2_bias, proj_bias]), me, size
    )
    gain_one, shift_one, gain_two, shift_two, proj_shift = (vectors[i : i + 1] for i in range(5))

    inputs_whole = widen(pad_rows(inputs), me, size)
    sent2 = widen((live_rows * pad_rows(cotangent).astype(jnp.float32)).astype(jnp.bfloat16), me, size)

    resid = inputs_whole.astype(jnp.float32)
    hat_one, inv_one, normed1 = norm_forward(resid, gain_one, shift_one)
    bias_qv = qv_bias.reshape(head_count, 2, DH)
    bias_full = jnp.stack(
        [bias_qv[:, 0], jnp.zeros_like(bias_qv[:, 0]), bias_qv[:, 1]], axis=1
    ).reshape(1, head_count * 3 * DH)
    qkv_rows = (dot_f32(normed1, wqkv_full) + bias_full).astype(jnp.bfloat16)
    qkv_rows, sent2 = lax.optimization_barrier((qkv_rows, sent2))
    mixed_rows, logsum = attend(qkv_rows, slot_rows, score_scale)
    attn_out = sum_whole(dot_f32(mixed_rows, wproj_t, NT), size) + proj_shift
    resid_mid = resid + live_rows * attn_out
    hat_two, inv_two, normed2 = norm_forward(resid_mid, gain_two, shift_two)
    inner_pre = dot_f32(normed2, wfc1_full) + fc1_bias
    activation = gelu_exact(inner_pre).astype(jnp.bfloat16)

    d_inner = dot_f32(sent2, wfc2_t) * gelu_slope(inner_pre)
    d_inner_b = d_inner.astype(jnp.bfloat16)
    d_norm2 = sum_whole(dot_f32(d_inner_b, wfc1_full, NT), size)
    grad_fc = jnp.concatenate(
        [
            dot_f32(normed2, d_inner_b, TN).astype(jnp.bfloat16),
            dot_f32(sent2, activation, TN).astype(jnp.bfloat16),
        ],
        axis=1,
    )
    d_norm2, _ = lax.optimization_barrier((d_norm2, grad_fc))
    grad_fc = lax.psum_scatter(grad_fc, "wide", scatter_dimension=0, tiled=True)

    mlp_out = sum_own(activation, wfc2_t, me, size, width) + fc2_bias

    full_width = float(width * size)
    scaled = d_norm2 * gain_two
    back_two = inv_two * (
        scaled
        - jnp.sum(scaled, axis=1, keepdims=True) / full_width
        - hat_two * (jnp.sum(scaled * hat_two, axis=1, keepdims=True) / full_width)
    )
    own_norm2 = own(d_norm2)
    grad_ln2_gain = jnp.sum(own_norm2 * own(hat_two), axis=0)
    grad_ln2_bias = jnp.sum(own_norm2, axis=0)
    own_cot = pad_rows(cotangent).astype(jnp.float32)
    masked1 = live_rows * (sent2.astype(jnp.float32) + back_two)
    own_mid = own_cot + own(back_two)
    sent1 = masked1.astype(jnp.bfloat16)
    d_mixed = dot_f32(sent1, wproj_t).astype(jnp.bfloat16)
    d_qkv_b, qkv_sums = attend_backward(
        qkv_rows, mixed_rows, d_mixed, logsum, slot_rows, score_scale
    )
    d_qkv_b, mlp_out = lax.optimization_barrier((d_qkv_b, mlp_out))
    output = trim_rows((own(resid_mid) + live_rows * mlp_out).astype(jnp.bfloat16))
    grad_attn = jnp.concatenate(
        [
            dot_f32(normed1, d_qkv_b, TN).astype(jnp.bfloat16),
            dot_f32(sent1, mixed_rows, TN).astype(jnp.bfloat16),
        ],
        axis=1,
    )
    grad_attn, grad_fc = lax.optimization_barrier((grad_attn, grad_fc))
    grad_attn = lax.psum_scatter(grad_attn, "wide", scatter_dimension=0, tiled=True)
    qkv_sums = jnp.sum(qkv_sums[:, 0], axis=0).reshape(head_count, 3, DH)
    grad_qv_bias = jnp.stack([qkv_sums[:, 0], qkv_sums[:, 2]], axis=1).reshape(-1)

    part1 = dot_f32(d_qkv_b, wqkv_full, NT)
    scaled_part = part1 * gain_one
    row_sums = jnp.stack([jnp.sum(scaled_part, axis=1), jnp.sum(scaled_part * hat_one, axis=1)])
    if size == 2:
        row_sums = row_sums + swap(row_sums)
        moved = swap(
            lax.dynamic_slice_in_dim(part1, (1 - me) * width, width, 1).astype(jnp.bfloat16)
        )
        d_norm1 = own(part1) + moved.astype(jnp.float32)
    else:
        row_sums = lax.psum(row_sums, "narrow")
        d_norm1 = lax.psum_scatter(part1, "narrow", scatter_dimension=1, tiled=True)
    own_hat = own(hat_one)
    back_one = inv_one * (
        d_norm1 * ln1_gain
        - row_sums[0][:, None] / full_width
        - own_hat * (row_sums[1][:, None] / full_width)
    )
    grad_in = trim_rows((own_mid + back_one).astype(jnp.bfloat16))

    vectors_out = [
        jnp.sum(d_norm1 * own_hat, axis=0),
        jnp.sum(d_norm1, axis=0),
        grad_qv_bias,
        jnp.sum(own(masked1), axis=0),
        grad_ln2_gain,
        grad_ln2_bias,
        jnp.sum(d_inner, axis=0),
        jnp.sum(live_rows * own_cot, axis=0),
    ]
    joined = jnp.concatenate(vectors_out)
    joined = lax.psum(joined.reshape(-1, 128), "wide").reshape(-1)
    summed, at = [], 0
    for vector in vectors_out:
        summed.append(joined[at : at + vector.shape[0]])
        at += vector.shape[0]
    qkv_columns, fc_columns = w_qkv.shape[1], w_fc1.shape[1]
    grad_w_qkv = grad_attn[:, :qkv_columns].astype(jnp.float32)
    grad_w_proj = grad_attn[:, qkv_columns:].T.astype(jnp.float32)
    grad_w_fc1 = grad_fc[:, :fc_columns].astype(jnp.float32)
    grad_w_fc2 = grad_fc[:, fc_columns:].T.astype(jnp.float32)
    return (
        output,
        grad_in,
        summed[0],
        summed[1],
        grad_w_qkv,
        summed[2],
        grad_w_proj,
        summed[3],
        summed[4],
        summed[5],
        grad_w_fc1,
        summed[6],
        grad_w_fc2,
        summed[7],
    )


def row_mask(info_ref, img, rows):
    index = lax.broadcasted_iota(jnp.int32, (rows, 1), 0)
    return ((index < SEQ) & (info_ref[1] > img)).astype(jnp.float32)


def halves(info_ref, own_ref, other_ref):
    first = info_ref[0] == 0
    own, other = own_ref[...].astype(jnp.float32), other_ref[...].astype(jnp.float32)
    return jnp.where(first, own, other), jnp.where(first, other, own)


def norm_halves(low, high):
    width = float(low.shape[1] * 2)
    center = (jnp.sum(low, axis=1, keepdims=True) + jnp.sum(high, axis=1, keepdims=True)) / width
    squares = jnp.sum(low * low, axis=1, keepdims=True) + jnp.sum(high * high, axis=1, keepdims=True)
    inv_std = lax.rsqrt(squares / width - center * center + norm_eps)
    return (low - center) * inv_std, (high - center) * inv_std, inv_std


def mask_keys(scores):
    edge = SEQ // 8 * 8
    tail = scores[edge:]
    index = lax.broadcasted_iota(jnp.int32, tail.shape, 0)
    return jnp.concatenate([scores[:edge], jnp.where(index < SEQ - edge, tail, -1e30)], axis=0)


def fwd_kernel(
    info, own, other, gain, shift, wqkv, bias, wproj, normed, qkv, mixed, logsum, part, held,
    *, heads, score_scale,
):
    step, steps = pl.program_id(0), held.shape[0]
    half = own.shape[1]

    @pl.when(step == 0)
    def _():
        low, high, _ = norm_halves(*halves(info, own, other))
        for at, hat in ((0, low), (half, high)):
            cols = slice(at, at + half)
            normed[:, cols] = (hat * gain[:, cols] + shift[:, cols]).astype(jnp.bfloat16)

    block = (dot_f32(normed[...], wqkv[...]) + bias[...]).astype(jnp.bfloat16)
    qkv[...] = block
    for head in range(heads):
        base = head * 3 * DH
        queries = block[:, base : base + DH]
        key_rows = block[:, base + DH : base + 2 * DH]
        value_rows = block[:, base + 2 * DH : base + 3 * DH]
        scores = mask_keys(dot_f32(key_rows, queries * score_scale, NT))
        top = jnp.max(scores, axis=0, keepdims=True)
        exp_scores = jnp.exp(scores - top)
        total = jnp.sum(exp_scores, axis=0, keepdims=True)
        probs = (exp_scores * (1.0 / total)).astype(jnp.bfloat16)
        made = jnp.transpose(dot_f32(value_rows, probs, TN)).astype(jnp.bfloat16)
        mixed[:, head * DH : (head + 1) * DH] = made
        logsum[0, head : head + 1, :] = top + jnp.log(total)
    held[step] = mixed[...]

    @pl.when(step == steps - 1)
    def _():
        whole = jnp.concatenate([held[at] for at in range(steps)], axis=1)
        part[...] = dot_f32(whole, wproj[...], NT).astype(jnp.bfloat16)


def mlp_kernel(
    info, own, other, cot_own, cot_other, mine, theirs, proj_shift, gain, shift, out_shift,
    w1, b1, w2, normed, sent, act, d_inner, d_sum, hat, inv, d_part, out_base, out_sent,
    d_acc, m_acc, *, img,
):
    step, steps = pl.program_id(0), pl.num_programs(0)
    rows, half = own.shape
    first = info[0] == 0

    @pl.when(step == 0)
    def _():
        live = row_mask(info, img, rows)
        low, high = halves(info, own, other)
        attn = mine[...].astype(jnp.float32) + theirs[...].astype(jnp.float32) + proj_shift[...]
        low = low + live * attn[:, :half]
        high = high + live * attn[:, half:]
        out_base[...] = jnp.where(first, low, high)
        low, high, inv_std = norm_halves(low, high)
        inv[...] = inv_std
        cot = halves(info, cot_own, cot_other)
        for at, part, grad in ((0, low, cot[0]), (half, high, cot[1])):
            cols = slice(at, at + half)
            hat[:, cols] = part
            normed[:, cols] = (part * gain[:, cols] + shift[:, cols]).astype(jnp.bfloat16)
            sent[:, cols] = (live * grad).astype(jnp.bfloat16)
        d_acc[...] = jnp.zeros_like(d_acc)
        m_acc[...] = jnp.zeros_like(m_acc)

    inner = dot_f32(normed[...], w1[...]) + b1[...]
    cdf = normal_cdf(inner)
    made = (inner * cdf).astype(jnp.bfloat16)
    act[...] = made
    slope = cdf + inner * jnp.exp(-0.5 * inner * inner) * (1.0 / math.sqrt(2.0 * math.pi))
    grad = dot_f32(sent[...], w2[...]) * slope
    d_sum[...] = jnp.sum(grad, axis=0, keepdims=True)
    grad = grad.astype(jnp.bfloat16)
    d_inner[...] = grad
    d_acc[...] += dot_f32(grad, w1[...], NT)
    m_acc[...] += dot_f32(made, w2[...], NT)

    @pl.when(step == steps - 1)
    def _():
        d_part[...] = d_acc[...].astype(jnp.bfloat16)
        low, high = m_acc[:, :half], m_acc[:, half:]
        live = row_mask(info, img, rows)
        out_base[...] += live * (jnp.where(first, low, high) + out_shift[...])
        out_sent[...] = (live * jnp.where(first, high, low)).astype(jnp.bfloat16)


def bwd_kernel(
    info, own, other, cot_own, cot_other, mine, theirs, gain2, gain1, hat, inv, wproj, qkv, mixed,
    logsum, wqkv, sent, d_qkv, sums, mid, sum_gain, sum_bias, sum_proj, d_own, d_sent, hat_own,
    inv_one, row_sums, sum_hat, sum_plain, d_mixed, acc, *, img, heads, score_scale,
):
    step, steps = pl.program_id(0), pl.num_programs(0)
    rows, half = own.shape
    full_width = float(2 * half)
    first = info[0] == 0

    @pl.when(step == 0)
    def _():
        live = row_mask(info, img, rows)
        grad = mine[...].astype(jnp.float32) + theirs[...].astype(jnp.float32)
        scaled = grad * gain2[...]
        back = inv[...] * (
            scaled
            - jnp.sum(scaled, axis=1, keepdims=True) / full_width
            - hat[...] * (jnp.sum(scaled * hat[...], axis=1, keepdims=True) / full_width)
        )
        sum_gain[...] = jnp.sum(grad * hat[...], axis=0, keepdims=True)
        sum_bias[...] = jnp.sum(grad, axis=0, keepdims=True)
        low, high = halves(info, cot_own, cot_other)
        low, high = low + back[:, :half], high + back[:, half:]
        mid[...] = jnp.where(first, low, high)
        for at, part in ((0, low), (half, high)):
            cols = slice(at, at + half)
            masked = live * part
            sum_proj[:, cols] = jnp.sum(masked, axis=0, keepdims=True)
            sent[:, cols] = masked.astype(jnp.bfloat16)
        made = dot_f32(sent[...], wproj[...]).astype(jnp.bfloat16)
        for at in range(d_mixed.shape[0]):
            d_mixed[at] = made[:, at * heads * DH : (at + 1) * heads * DH]
        acc[...] = jnp.zeros_like(acc)

    for head in range(heads):
        base = head * 3 * DH
        queries = qkv[:, base : base + DH]
        key_rows = qkv[:, base + DH : base + 2 * DH]
        value_rows = qkv[:, base + 2 * DH : base + 3 * DH]
        out = mixed[:, head * DH : (head + 1) * DH]
        d_out = d_mixed[step, :, head * DH : (head + 1) * DH]
        products = d_out.astype(jnp.float32) * out.astype(jnp.float32)
        delta = jnp.sum(jnp.transpose(products), axis=0, keepdims=True)
        scores = mask_keys(dot_f32(key_rows, queries * score_scale, NT))
        probs = jnp.exp(scores - logsum[0, head : head + 1, :])
        d_probs = dot_f32(value_rows, d_out, NT)
        d_scores = (probs * (d_probs - delta)).astype(jnp.bfloat16)
        d_query = jnp.transpose(dot_f32(key_rows, d_scores, TN)) * score_scale
        d_keys = dot_f32(d_scores, queries, NN) * score_scale
        d_values = dot_f32(probs.astype(jnp.bfloat16), d_out, NN)
        for at, grad in enumerate((d_query, d_keys, d_values)):
            cols = slice(base + at * DH, base + (at + 1) * DH)
            d_qkv[:, cols] = grad.astype(jnp.bfloat16)
            sums[:, cols] = jnp.sum(grad, axis=0, keepdims=True)
    acc[...] += dot_f32(d_qkv[...], wqkv[...], NT)

    @pl.when(step == steps - 1)
    def _():
        low, high, inv_std = norm_halves(*halves(info, own, other))
        inv_one[...] = inv_std
        hat_own[...] = jnp.where(first, low, high)
        left, right = acc[:, :half], acc[:, half:]
        d_own[...] = jnp.where(first, left, right)
        d_sent[...] = jnp.where(first, right, left).astype(jnp.bfloat16)
        for at, grad, part in ((0, left, low), (half, right, high)):
            columns = slice(at, at + half)
            sum_hat[:, columns] = jnp.sum(grad * part, axis=0, keepdims=True)
            sum_plain[:, columns] = jnp.sum(grad, axis=0, keepdims=True)
        left, right = left * gain1[:, :half], right * gain1[:, half:]
        plain = jnp.sum(left, axis=1, keepdims=True) + jnp.sum(right, axis=1, keepdims=True)
        hatted = jnp.sum(left * low, axis=1, keepdims=True) + jnp.sum(
            right * high, axis=1, keepdims=True
        )
        lane = lax.broadcasted_iota(jnp.int32, (rows, 128), 1)
        both = jnp.where(lane == 0, plain, jnp.where(lane == 1, hatted, 0.0))
        row_sums[...] = jnp.transpose(both)[:8]


def pair_grad_kernel(left0, left1, right0, right1, more0, more1, rest0, rest1, out, held, *, cut):
    step = pl.program_id(0)

    def load(one, two):
        held[...] = jnp.concatenate([one[...], two[...]], axis=0)

    def make(one, two):
        right = jnp.concatenate([one[...], two[...]], axis=0)
        out[...] = dot_f32(held[...], right, TN).astype(jnp.bfloat16)

    pl.when(step == 0)(lambda: load(left0, left1))
    pl.when(step == cut)(lambda: load(more0, more1))
    pl.when(step < cut)(lambda: make(right0, right1))
    pl.when(step >= cut)(lambda: make(rest0, rest1))


SCALARS = pl.BlockSpec(memory_space=pltpu.SMEM)
PARAMS = pltpu.CompilerParams(vmem_limit_bytes=48 * 1024 * 1024)


def whole(shape):
    return pl.BlockSpec(shape, lambda s: (0,) * len(shape), pipeline_mode=pl.Buffered(1))


def cols(rows, width, start=0):
    return pl.BlockSpec((rows, width), lambda s: (0, start + s))


def cost(flops, moved):
    return pl.CostEstimate(flops=flops, bytes_accessed=moved, transcendentals=0)


def shaped(*shapes):
    return [jax.ShapeDtypeStruct(shape, kind) for shape, kind in shapes]


F32, BF16 = jnp.float32, jnp.bfloat16


def forward(info, own, other, gain, shift, early, bias, score_scale):
    rows, half = own.shape
    wide, total = early.shape
    inner = total - bias.shape[1]
    heads = 2
    steps = inner // (heads * DH)
    span = heads * 3 * DH
    return pl.pallas_call(
        functools.partial(fwd_kernel, heads=heads, score_scale=score_scale),
        grid=(steps,),
        in_specs=[
            SCALARS, whole((rows, half)), whole((rows, half)), whole((1, wide)), whole((1, wide)),
            cols(wide, span), cols(1, span),
            pl.BlockSpec((wide, inner), lambda s: (0, bias.shape[1] // inner)),
        ],
        out_specs=[
            whole((rows, wide)), cols(rows, span), cols(rows, heads * DH),
            pl.BlockSpec((1, 8, rows), lambda s: (s, 0, 0)), whole((rows, wide)),
        ],
        out_shape=shaped(
            ((rows, wide), BF16), ((rows, steps * span), BF16), ((rows, inner), BF16),
            ((steps, 8, rows), F32), ((rows, wide), BF16),
        ),
        scratch_shapes=[pltpu.VMEM((steps, rows, heads * DH), BF16)],
        compiler_params=PARAMS,
        cost_estimate=cost(3_000_000_000, 3_000_000),
        name="attention_forward",
    )(info, own, other, gain, shift, early, bias, early)


def mlp_pass(info, img, own, other, cot_own, cot_other, mine, theirs, vectors, out_shift, late, b1):
    rows, half = own.shape
    wide = late.shape[0]
    hidden = b1.shape[1]
    tile = 512
    steps = hidden // tile
    proj_shift, gain, shift = vectors
    return pl.pallas_call(
        functools.partial(mlp_kernel, img=img),
        grid=(steps,),
        in_specs=[
            SCALARS, *[whole((rows, half))] * 4, *[whole((rows, wide))] * 2, *[whole((1, wide))] * 3,
            whole((1, half)), cols(wide, tile), cols(1, tile), cols(wide, tile, steps),
        ],
        out_specs=[
            whole((rows, wide)), whole((rows, wide)), cols(rows, tile), cols(rows, tile),
            cols(1, tile), whole((rows, wide)), whole((rows, 1)), whole((rows, wide)),
            whole((rows, half)), whole((rows, half)),
        ],
        out_shape=shaped(
            ((rows, wide), BF16), ((rows, wide), BF16), ((rows, hidden), BF16),
            ((rows, hidden), BF16), ((1, hidden), F32), ((rows, wide), F32), ((rows, 1), F32),
            ((rows, wide), BF16), ((rows, half), F32), ((rows, half), BF16),
        ),
        scratch_shapes=[pltpu.VMEM((rows, wide), F32), pltpu.VMEM((rows, wide), F32)],
        compiler_params=PARAMS,
        cost_estimate=cost(4_000_000_000, 8_000_000),
        name="feed_forward",
    )(info, own, other, cot_own, cot_other, mine, theirs, proj_shift, gain, shift, out_shift,
      late, b1, late)


def backward(
    info, img, own, other, cot_own, cot_other, mine, theirs, gain2, gain1, hat, inv, early, qkv,
    mixed, logsum, score_scale,
):
    rows, half = own.shape
    wide = early.shape[0]
    inner = mixed.shape[1]
    heads = 2
    steps = inner // (heads * DH)
    span = heads * 3 * DH
    return pl.pallas_call(
        functools.partial(bwd_kernel, img=img, heads=heads, score_scale=score_scale),
        grid=(steps,),
        in_specs=[
            SCALARS, *[whole((rows, half))] * 4, *[whole((rows, wide))] * 2, *[whole((1, wide))] * 2,
            whole((rows, wide)), whole((rows, 1)),
            pl.BlockSpec((wide, inner), lambda s: (0, qkv.shape[1] // inner)),
            cols(rows, span), cols(rows, heads * DH),
            pl.BlockSpec((1, 8, rows), lambda s: (s, 0, 0)), cols(wide, span),
        ],
        out_specs=[
            whole((rows, wide)), cols(rows, span), cols(1, span), whole((rows, half)),
            whole((1, wide)), whole((1, wide)), whole((1, wide)), whole((rows, half)),
            whole((rows, half)), whole((rows, half)), whole((rows, 1)), whole((8, rows)),
            whole((1, wide)), whole((1, wide)),
        ],
        out_shape=shaped(
            ((rows, wide), BF16), ((rows, 3 * inner), BF16), ((1, 3 * inner), F32),
            ((rows, half), F32), ((1, wide), F32), ((1, wide), F32), ((1, wide), F32),
            ((rows, half), F32), ((rows, half), BF16), ((rows, half), F32), ((rows, 1), F32),
            ((8, rows), F32), ((1, wide), F32), ((1, wide), F32),
        ),
        scratch_shapes=[
            pltpu.VMEM((steps, rows, heads * DH), BF16), pltpu.VMEM((rows, wide), F32)
        ],
        compiler_params=PARAMS,
        cost_estimate=cost(5_000_000_000, 8_000_000),
        name="attention_backward",
    )(info, own, other, cot_own, cot_other, mine, theirs, gain2, gain1, hat, inv, early, qkv, mixed,
      logsum, early)


def pair_grads(lefts, rights, mores, rests, tile=512):
    rows, wide = lefts[0].shape
    first, second = rights[0].shape[1] // tile, rests[0].shape[1] // tile
    left = whole((rows, wide))
    right = pl.BlockSpec((rows, tile), lambda s: (0, jnp.minimum(s, first - 1)))
    rest = pl.BlockSpec((rows, tile), lambda s: (0, jnp.maximum(s - first, 0)))
    return pl.pallas_call(
        functools.partial(pair_grad_kernel, cut=first),
        grid=(first + second,),
        in_specs=[left, left, right, right, left, left, rest, rest],
        out_specs=cols(wide, tile),
        out_shape=jax.ShapeDtypeStruct((wide, (first + second) * tile), BF16),
        scratch_shapes=[pltpu.VMEM((2 * rows, wide), BF16)],
        compiler_params=PARAMS,
        cost_estimate=cost(rows * wide * (first + second) * tile, 5_000_000),
        name="weight_gradients",
    )(*lefts, *rights, *mores, *rests)


MESH = pl.DeviceIdType.MESH


def place():
    index = lax.axis_index("wide")
    return index, lax.div(index, 4), lax.rem(lax.div(index, 2), 2), lax.rem(index, 2)


def greet(partners):
    barrier = pltpu.get_barrier_semaphore()
    count = 0
    for when, device in partners:
        def signal(device=device):
            pl.semaphore_signal(barrier, inc=1, device_id=device, device_id_type=MESH)

        if when is None:
            signal()
            count = count + 1
        else:
            pl.when(when)(signal)
            count = count + when.astype(jnp.int32)
    pl.semaphore_wait(barrier, count)


def gather_kernel(shard, *refs, deep, extra):
    rows, out, moved = refs[:extra], refs[extra], refs[extra + 1 : 2 * extra + 1]
    here_sem, send_sem, recv_sem, x_send, x_recv = refs[2 * extra + 1 :]
    index, z, y, core = place()
    across = {"narrow": 1 - lax.axis_index("narrow")}
    beside, near = index + 2 - 4 * y, index + 1 - 2 * core
    more, less = z + 1 < deep, z > 0
    greet([
        (None, across), (None, {"wide": beside}), (None, {"wide": near}),
        (more, {"wide": index + 4}), (less, {"wide": index - 4}),
    ])
    sent = []

    def build(owner, way, target, source):
        return pltpu.make_async_remote_copy(
            src_ref=source, dst_ref=out.at[owner], send_sem=send_sem.at[owner, way],
            recv_sem=recv_sem.at[owner], device_id={"wide": target}, device_id_type=MESH,
        )

    def guarded(when, step):
        if when is None:
            step()
        else:
            pl.when(when)(step)

    def send(when, owner, way, target, source=None):
        source = out.at[owner] if source is None else source
        guarded(when, lambda: build(owner, way, target, source).start())
        sent.append((when, owner, way, target, source))

    def arrive(when, owner):
        guarded(when, lambda: build(owner, 0, near, out.at[owner]).wait_recv())

    swaps = [
        pltpu.make_async_remote_copy(
            src_ref=source, dst_ref=target, send_sem=x_send.at[at], recv_sem=x_recv.at[at],
            device_id=across, device_id_type=MESH,
        )
        for at, (source, target) in enumerate(zip(rows, moved))
    ]
    send(more, index, 0, index + 4, shard)
    send(less, index, 1, index - 4, shard)
    send(None, index, 2, beside, shard)
    send(None, index, 3, near, shard)
    for copy in swaps:
        copy.start()
    here = pltpu.make_async_copy(shard, out.at[index], here_sem)
    here.start()
    for step in range(1, deep):
        for sign, way, onward in ((-1, 0, more), (1, 1, less)):
            owner = index + 4 * sign * step
            holds = z >= step if sign < 0 else z + step < deep
            arrive(holds, owner)
            send(holds & onward, owner, way, index - 4 * sign)
            send(holds, owner, 2, beside)
            send(holds, owner, 3, near)
        owner = beside
        for owner, holds in (
            [(beside, None)] if step == 1 else []
        ) + [(beside - 4 * step, z >= step), (beside + 4 * step, z + step < deep)]:
            arrive(holds, owner)
            send(holds, owner, 3, near)
    base = 1 - core
    for other in range(2 * deep):
        arrive(None, 2 * other + base)
    for copy in swaps:
        copy.wait()
    here.wait()
    for when, owner, way, target, source in sent:
        guarded(when, lambda: build(owner, way, target, source).wait_send())


def gather_early(shard, rows):
    count, extra = lax.axis_size("wide"), len(rows)
    anywhere = pl.BlockSpec(memory_space=pl.ANY)
    dma = pltpu.SemaphoreType.DMA
    out, *moved = pl.pallas_call(
        functools.partial(gather_kernel, deep=count // 4, extra=extra),
        in_specs=[anywhere] * (1 + extra),
        out_specs=[anywhere] * (1 + extra),
        out_shape=[jax.ShapeDtypeStruct((count, *shard.shape), shard.dtype)]
        + [jax.ShapeDtypeStruct(part.shape, part.dtype) for part in rows],
        scratch_shapes=[dma, dma((count, 4)), dma((count,)), dma((extra,)), dma((extra,))],
        compiler_params=pltpu.CompilerParams(collective_id=0, has_side_effects=True),
        cost_estimate=cost(15_000_000_000, 8_000_000),
        name="gather_early",
    )(shard, *rows)
    return out.reshape(count * shard.shape[0], shard.shape[1]), moved


def scatter_kernel(
    grads, vector, out, vector_out, near_in, side_out, side_in, line_out, line_in, sums,
    v_near, v_side, v_line, near_send, near_recv, side_send, side_recv, line_send, line_recv,
    v_send, v_recv, *, deep,
):
    index, z, y, core = place()
    beside, near = {"wide": index + 2 - 4 * y}, {"wide": index + 1 - 2 * core}
    more, less = z + 1 < deep, z > 0
    column = lax.rem(index, 4)
    greet([(None, beside), (None, near)] + [
        (z != at, {"wide": 4 * at + column}) for at in range(deep)
    ])

    def remote(source, target, send, recv, device):
        return pltpu.make_async_remote_copy(
            src_ref=source, dst_ref=target, send_sem=send, recv_sem=recv, device_id=device,
            device_id_type=MESH,
        )

    def add(*parts):
        return functools.reduce(lambda a, b: a + b, [part.astype(jnp.float32) for part in parts])

    order = [at for pair in zip(range(deep - 1, -1, -1), range(deep)) for at in pair][:deep]
    waits = []

    def to_near(at, side):
        slot = 2 * at + side
        copy = remote(
            grads.at[2 * slot + 1 - core], near_in.at[slot], near_send.at[slot],
            near_recv.at[slot], near,
        )
        return copy

    near_copies = {}
    v_copy = remote(vector, v_near, v_send.at[0], v_recv.at[0], near)
    v_copy.start()
    for part in (0, 1):
        side = 1 - y if part == 0 else y
        for at in order:
            near_copies[part, at] = to_near(at, side)
            near_copies[part, at].start()
    v_copy.wait()
    v_near[...] += vector[...]
    v_copy = remote(v_near, v_side, v_send.at[1], v_recv.at[1], beside)
    v_copy.start()

    side_copies = {}
    for at in order:
        slot = 2 * at + 1 - y
        near_copies[0, at].wait_recv()
        side_out[at] = add(grads[2 * slot + core], near_in[slot]).astype(jnp.bfloat16)
        side_copies[at] = remote(
            side_out.at[at], side_in.at[at], side_send.at[at], side_recv.at[at], beside
        )
        side_copies[at].start()
    v_copy.wait()
    v_line[z] = v_near[...] + v_side[...]
    v_pushes = [
        (z != at, remote(v_line.at[z], v_line.at[z], v_send.at[2 + at], v_recv.at[2 + z],
                         {"wide": 4 * at + column}))
        for at in range(deep)
    ]
    for when, copy in v_pushes:
        pl.when(when)(copy.start)

    def hop(at, way):
        slot = at * 2 + way
        return remote(
            line_out.at[at], line_in.at[slot], line_send.at[at], line_recv.at[slot],
            {"wide": index + (4 if way == 0 else -4)},
        )

    for at in order:
        slot = 2 * at + y
        near_copies[1, at].wait_recv()
        side_copies[at].wait_recv()
        sums[at] = add(grads[2 * slot + core], near_in[slot], side_in[at])
        for way, goes, joins in ((0, z < at, z > 0), (1, z > at, z < deep - 1)):
            @pl.when(goes & joins)
            def _(way=way):
                hop(at, way).wait_recv()
                line_out[at] = (sums[at] + line_in[2 * at + way].astype(jnp.float32)).astype(
                    jnp.bfloat16
                )
                hop(at, way).start()

            @pl.when(goes & ~joins)
            def _(way=way):
                line_out[at] = sums[at].astype(jnp.bfloat16)
                hop(at, way).start()

    for at in range(deep):
        @pl.when(z == at)
        def _():
            out[...] = sums[at]
            if at > 0:
                hop(at, 0).wait_recv()
                out[...] += line_in[2 * at].astype(jnp.float32)
            if at < deep - 1:
                hop(at, 1).wait_recv()
                out[...] += line_in[2 * at + 1].astype(jnp.float32)

        @pl.when(z != at)
        def _():
            hop(at, 0).wait_send()
            remote(v_line.at[at], v_line.at[at], v_send.at[2 + at], v_recv.at[2 + at],
                   near).wait_recv()
            remote(v_line.at[z], v_line.at[z], v_send.at[2 + at], v_recv.at[2 + z],
                   near).wait_send()
    total = v_line[0]
    for at in range(1, deep):
        total = total + v_line[at]
    vector_out[...] = total
    for copy in near_copies.values():
        copy.wait_send()
    for copy in side_copies.values():
        copy.wait_send()


def scatter_late(grads, vector):
    count = lax.axis_size("wide")
    deep = count // 4
    rows, width = grads.shape[0] // count, grads.shape[1]
    block = (rows, width)
    inside = pl.BlockSpec(memory_space=pltpu.VMEM)
    dma = pltpu.SemaphoreType.DMA
    return pl.pallas_call(
        functools.partial(scatter_kernel, deep=deep),
        in_specs=[inside] * 2,
        out_specs=[inside] * 2,
        out_shape=shaped((block, F32), (vector.shape, F32)),
        scratch_shapes=[
            pltpu.VMEM((2 * deep, *block), BF16), pltpu.VMEM((deep, *block), BF16),
            pltpu.VMEM((deep, *block), BF16), pltpu.VMEM((deep, *block), BF16),
            pltpu.VMEM((2 * deep, *block), BF16), pltpu.VMEM((deep, *block), F32),
            pltpu.VMEM(vector.shape, F32), pltpu.VMEM(vector.shape, F32),
            pltpu.VMEM((deep, *vector.shape), F32),
            dma((2 * deep,)), dma((2 * deep,)), dma((deep,)), dma((deep,)), dma((deep,)),
            dma((2 * deep,)), dma((2 + deep,)), dma((2 + deep,)),
        ],
        compiler_params=pltpu.CompilerParams(
            collective_id=1, has_side_effects=True, vmem_limit_bytes=56 * 1024 * 1024
        ),
        cost_estimate=cost(15_000_000_000, 8_000_000),
        name="scatter_late",
    )(grads.reshape(count, rows, width), vector)


def shards_pair(
    inputs, counts, ln1_gain, ln1_bias, w_qkv, qv_bias, w_proj, proj_bias, ln2_gain, ln2_bias,
    w_fc1, fc1_bias, w_fc2, fc2_bias, cotangent,
):
    me = lax.axis_index("narrow")
    row_count, half = inputs.shape
    images = row_count // SEQ
    rows = -(-SEQ // ROW_TILE) * ROW_TILE
    head_count = w_qkv.shape[1] // (3 * DH)
    score_scale = 1.0 / math.sqrt(DH)
    span = range(images)
    info = jnp.stack([me.astype(jnp.int32), counts[0]])

    def slot(array, img):
        return jnp.pad(array[img * SEQ : (img + 1) * SEQ], ((0, rows - SEQ), (0, 0)))

    def own(vector):
        return lax.dynamic_slice_in_dim(vector, me * half, half, vector.ndim - 1)

    mine = [slot(inputs, i) for i in span]
    vectors = jnp.stack([ln1_gain, ln1_bias, ln2_gain, ln2_bias, proj_bias] + [proj_bias] * 3)
    late = lax.all_gather(jnp.concatenate([w_fc1, w_fc2.T], axis=1), "wide", axis=0, tiled=True)
    cot = [slot(cotangent, i) for i in span]
    early, moved = gather_early(jnp.concatenate([w_qkv, w_proj.T], axis=1), mine + cot + [vectors])
    theirs, cot_theirs = moved[:images], moved[images : 2 * images]
    vectors = jnp.concatenate(
        [jnp.where(me == 0, vectors, moved[-1]), jnp.where(me == 0, moved[-1], vectors)], axis=1
    )
    gain_one, shift_one, gain_two, shift_two, proj_shift = (vectors[i : i + 1] for i in range(5))

    bias_qv = qv_bias.reshape(head_count, 2, DH)
    bias_full = jnp.stack(
        [bias_qv[:, 0], jnp.zeros_like(bias_qv[:, 0]), bias_qv[:, 1]], axis=1
    ).reshape(1, head_count * 3 * DH)

    front = [
        forward(info, mine[i], theirs[i], gain_one, shift_one, early, bias_full, score_scale)
        for i in span
    ]
    normed1, qkv, mixed, logsum, part = zip(*front)
    part_theirs = [swap(x) for x in part]
    middle = [
        mlp_pass(
            info, i, mine[i], theirs[i], cot[i], cot_theirs[i], part[i], part_theirs[i],
            (proj_shift, gain_two, shift_two), fc2_bias.reshape(1, -1), late,
            fc1_bias.reshape(1, -1),
        )
        for i in span
    ]
    normed2, sent2, act, d_inner, d_sum, hat2, inv2, d_part, out_base, out_sent = zip(*middle)
    d_theirs = [swap(x) for x in d_part]
    out_theirs = [swap(x) for x in out_sent]
    grad_fc = pair_grads(normed2, d_inner, sent2, act)
    d_theirs[0], grad_fc = lax.optimization_barrier((d_theirs[0], grad_fc))
    grad_fc = lax.psum_scatter(grad_fc, "wide", scatter_dimension=0, tiled=True)
    ends = [
        backward(
            info, i, mine[i], theirs[i], cot[i], cot_theirs[i], d_part[i], d_theirs[i], gain_two,
            gain_one, hat2[i], inv2[i], early, qkv[i], mixed[i], logsum[i], score_scale,
        )
        for i in span
    ]
    (sent1, d_qkv, qkv_sums, mid, sum_gain, sum_bias, sum_proj, d_own, d_sent, hat_own, inv_one,
     row_sums, sum_hat, sum_plain) = zip(*ends)
    d_moved = [swap(x) for x in d_sent]
    row_sums = [x + swap(x) for x in row_sums]
    d_qkv, out_theirs = lax.optimization_barrier((d_qkv, out_theirs))
    grad_attn = pair_grads(normed1, d_qkv, sent1, mixed)

    qkv_sums = sum(qkv_sums).reshape(head_count, 3, DH)
    grad_qv = jnp.stack([qkv_sums[:, 0], qkv_sums[:, 2]], axis=1).reshape(-1)
    own_cot = sum(
        jnp.sum(jnp.where(counts[0] > i, cot[i].astype(F32), 0.0), axis=0) for i in span
    )
    first_sums = jnp.concatenate([sum(sum_hat), sum(sum_plain)], axis=0)
    first_sums = first_sums + swap(first_sums)
    joined = jnp.concatenate(
        [
            grad_qv, own(sum(sum_proj))[0], own(sum(sum_gain))[0], own(sum(sum_bias))[0],
            sum(d_sum)[0], own_cot, own(first_sums).reshape(-1),
        ]
    )
    grad_attn, joined = scatter_late(grad_attn, joined.reshape(-1, 128))
    joined = joined.reshape(-1)

    output = jnp.concatenate(
        [(out_base[i] + out_theirs[i].astype(F32)).astype(BF16)[:SEQ] for i in span], axis=0
    )
    full_width = float(2 * half)
    grads_in = []
    for i in span:
        d_norm1 = d_own[i] + d_moved[i].astype(F32)
        back = inv_one[i] * (
            d_norm1 * ln1_gain
            - row_sums[i][0][:, None] / full_width
            - hat_own[i] * (row_sums[i][1][:, None] / full_width)
        )
        grads_in.append((mid[i] + back).astype(BF16)[:SEQ])
    grad_in = jnp.concatenate(grads_in, axis=0)
    qv, ff = grad_qv.shape[0], fc1_bias.shape[0]
    edges = [0]
    for extent in (qv, half, half, half, ff, half, half, half):
        edges.append(edges[-1] + extent)
    pieces = [joined[a:b] for a, b in zip(edges[:-1], edges[1:])]
    split_attn, split_fc = w_qkv.shape[1], w_fc1.shape[1]
    return (
        output,
        grad_in,
        pieces[6],
        pieces[7],
        grad_attn[:, :split_attn],
        pieces[0],
        grad_attn[:, split_attn:].T,
        pieces[1],
        pieces[2],
        pieces[3],
        grad_fc[:, :split_fc].astype(F32),
        pieces[4],
        grad_fc[:, split_fc:].T.astype(F32),
        pieces[5],
    )


def shards(*arrays):
    if lax.axis_size("narrow") == 2:
        return shards_pair(*arrays)
    return shards_any(*arrays)


def solution(mesh):
    return jax.shard_map(
        shards,
        mesh=mesh,
        in_specs=(
            P("wide", "narrow"),
            P("wide"),
            P("narrow"),
            P("narrow"),
            P("wide", "narrow"),
            P("narrow"),
            P("narrow", "wide"),
            P("narrow"),
            P("narrow"),
            P("narrow"),
            P("wide", "narrow"),
            P("narrow"),
            P("narrow", "wide"),
            P("narrow"),
            P("wide", "narrow"),
        ),
        out_specs=(
            P("wide", "narrow"),
            P("wide", "narrow"),
            P("narrow"),
            P("narrow"),
            P("wide", "narrow"),
            P("narrow"),
            P("narrow", "wide"),
            P("narrow"),
            P("narrow"),
            P("narrow"),
            P("wide", "narrow"),
            P("narrow"),
            P("narrow", "wide"),
            P("narrow"),
        ),
        check_vma=False,
    )
```

```python
import functools
import math

import jax
import jax.numpy as jnp
from jax import lax
from jax.experimental import pallas as pl
from jax.experimental.pallas import tpu as pltpu
from jax.sharding import PartitionSpec as P

DH = 64
SEQ = 577
ROW_TILE = 16


norm_eps = 1e-06
NT = (((1,), (1,)), ((), ()))
TN = (((0,), (0,)), ((), ()))
NN = (((1,), (0,)), ((), ()))


def dot_f32(left_mat, right_mat, dims=NN):
    return lax.dot_general(left_mat, right_mat, dims, preferred_element_type=jnp.float32)


def swap(piece):
    return lax.ppermute(piece, "narrow", ((0, 1), (1, 0)))


def widen(piece, me, size):
    if size != 2:
        return lax.all_gather(piece, "narrow", axis=1, tiled=True)
    other = swap(piece)
    return jnp.concatenate(
        [jnp.where(me == 0, piece, other), jnp.where(me == 0, other, piece)], axis=1
    )


def sum_whole(partial_rows, size):
    if size != 2:
        return lax.psum(partial_rows, "narrow")
    mine = partial_rows.astype(jnp.bfloat16)
    return mine.astype(jnp.float32) + swap(mine).astype(jnp.float32)


def sum_own(left_mat, right_rows, me, size, width):
    if size != 2:
        return lax.psum_scatter(
            dot_f32(left_mat, right_rows, NT), "narrow", scatter_dimension=1, tiled=True
        )
    theirs = lax.dynamic_slice_in_dim(right_rows, (1 - me) * width, width, 0)
    ours = lax.dynamic_slice_in_dim(right_rows, me * width, width, 0)
    moved = swap(dot_f32(left_mat, theirs, NT).astype(jnp.bfloat16))
    return dot_f32(left_mat, ours, NT) + moved.astype(jnp.float32)


def normal_cdf(values_in):
    return 0.5 * (1.0 + lax.erf(values_in * (1.0 / math.sqrt(2.0))))


def gelu_exact(values_in):
    return values_in * normal_cdf(values_in)


def gelu_slope(values_in):
    return normal_cdf(values_in) + values_in * jnp.exp(-0.5 * values_in * values_in) * (
        1.0 / math.sqrt(2.0 * math.pi)
    )


def norm_forward(rows_in, gain_vec, shift_vec):
    width = float(rows_in.shape[1])
    center = jnp.sum(rows_in, axis=1, keepdims=True) / width
    spread = jnp.sum(rows_in * rows_in, axis=1, keepdims=True) / width - center * center
    inv_std = lax.rsqrt(spread + norm_eps)
    normalized = (rows_in - center) * inv_std
    return (normalized, inv_std, (normalized * gain_vec + shift_vec).astype(jnp.bfloat16))


def scores_by_key(queries, key_rows, score_scale):
    scores = dot_f32(key_rows, queries, NT) * score_scale
    key_index = lax.broadcasted_iota(jnp.int32, scores.shape, 0)
    return jnp.where(key_index < SEQ, scores, -1e30)


def attend_kernel(qkv_ref, mixed_ref, logsum_ref, *, heads, score_scale):
    for head in range(heads):
        base = head * 3 * DH
        queries = qkv_ref[:, base : base + DH]
        key_rows = qkv_ref[:, base + DH : base + 2 * DH]
        value_rows = qkv_ref[:, base + 2 * DH : base + 3 * DH]
        scores = scores_by_key(queries, key_rows, score_scale)
        top = jnp.max(scores, axis=0, keepdims=True)
        exp_scores = jnp.exp(scores - top)
        total = jnp.sum(exp_scores, axis=0, keepdims=True)
        probs = (exp_scores * (1.0 / total)).astype(jnp.bfloat16)
        mixed_ref[:, head * DH : (head + 1) * DH] = dot_f32(probs, value_rows, TN).astype(
            jnp.bfloat16
        )
        logsum_ref[0, head : head + 1, :] = top + jnp.log(total)


def attend_back_kernel(
    qkv_ref, mixed_ref, d_mixed_ref, logsum_ref, d_qkv_ref, sums_ref, *, heads, score_scale
):
    for head in range(heads):
        base = head * 3 * DH
        queries = qkv_ref[:, base : base + DH]
        key_rows = qkv_ref[:, base + DH : base + 2 * DH]
        value_rows = qkv_ref[:, base + 2 * DH : base + 3 * DH]
        mixed = mixed_ref[:, head * DH : (head + 1) * DH]
        d_mixed = d_mixed_ref[:, head * DH : (head + 1) * DH]
        products = d_mixed.astype(jnp.float32) * mixed.astype(jnp.float32)
        delta = jnp.sum(jnp.transpose(products), axis=0, keepdims=True)
        scores = scores_by_key(queries, key_rows, score_scale)
        probs = jnp.exp(scores - logsum_ref[0, head : head + 1, :])
        d_probs = dot_f32(value_rows, d_mixed, NT)
        d_scores = (probs * (d_probs - delta)).astype(jnp.bfloat16)
        d_query = dot_f32(d_scores, key_rows, TN) * score_scale
        d_keys = dot_f32(d_scores, queries, NN) * score_scale
        d_values = dot_f32(probs.astype(jnp.bfloat16), d_mixed, NN)
        for part, grad in enumerate((d_query, d_keys, d_values)):
            columns = slice(base + part * DH, base + (part + 1) * DH)
            d_qkv_ref[:, columns] = grad.astype(jnp.bfloat16)
            sums_ref[0, :, columns] = jnp.broadcast_to(
                jnp.sum(grad, axis=0, keepdims=True), (8, DH)
            )


def head_pairs(width):
    heads = 2
    return heads, width // (3 * DH * heads)


def attend(qkv_rows, slot_rows, score_scale):
    row_count, width = qkv_rows.shape
    slots = row_count // slot_rows
    heads, pairs = head_pairs(width)
    return pl.pallas_call(
        functools.partial(attend_kernel, heads=heads, score_scale=score_scale),
        grid=(slots, pairs),
        in_specs=[pl.BlockSpec((slot_rows, heads * 3 * DH), lambda s, p: (s, p))],
        out_specs=[
            pl.BlockSpec((slot_rows, heads * DH), lambda s, p: (s, p)),
            pl.BlockSpec((1, 8, slot_rows), lambda s, p: (s * pairs + p, 0, 0)),
        ],
        out_shape=[
            jax.ShapeDtypeStruct((row_count, width // 3), jnp.bfloat16),
            jax.ShapeDtypeStruct((slots * pairs, 8, slot_rows), jnp.float32),
        ],
        cost_estimate=pl.CostEstimate(
            flops=4 * slots * pairs * heads * slot_rows * slot_rows * 256,
            bytes_accessed=row_count * width * 3,
            transcendentals=slots * pairs * heads * slot_rows * slot_rows,
        ),
        name="attend",
    )(qkv_rows)


def attend_backward(qkv_rows, mixed_rows, d_mixed, logsum, slot_rows, score_scale):
    row_count, width = qkv_rows.shape
    slots = row_count // slot_rows
    heads, pairs = head_pairs(width)
    narrow_block = pl.BlockSpec((slot_rows, heads * DH), lambda s, p: (s, p))
    wide_block = pl.BlockSpec((slot_rows, heads * 3 * DH), lambda s, p: (s, p))
    return pl.pallas_call(
        functools.partial(attend_back_kernel, heads=heads, score_scale=score_scale),
        grid=(slots, pairs),
        in_specs=[
            wide_block,
            narrow_block,
            narrow_block,
            pl.BlockSpec((1, 8, slot_rows), lambda s, p: (s * pairs + p, 0, 0)),
        ],
        out_specs=[
            wide_block,
            pl.BlockSpec((1, 8, heads * 3 * DH), lambda s, p: (s, 0, p)),
        ],
        out_shape=[
            jax.ShapeDtypeStruct((row_count, width), jnp.bfloat16),
            jax.ShapeDtypeStruct((slots, 8, width), jnp.float32),
        ],
        cost_estimate=pl.CostEstimate(
            flops=10 * slots * pairs * heads * slot_rows * slot_rows * 256,
            bytes_accessed=row_count * width * 6,
            transcendentals=slots * pairs * heads * slot_rows * slot_rows,
        ),
        name="attend_back",
    )(qkv_rows, mixed_rows, d_mixed, logsum)


def shards_any(
    inputs,
    counts,
    ln1_gain,
    ln1_bias,
    w_qkv,
    qv_bias,
    w_proj,
    proj_bias,
    ln2_gain,
    ln2_bias,
    w_fc1,
    fc1_bias,
    w_fc2,
    fc2_bias,
    cotangent,
):
    size = lax.axis_size("narrow")
    me = lax.axis_index("narrow")
    row_count, width = inputs.shape
    slot_count = row_count // SEQ
    slot_rows = -(-SEQ // ROW_TILE) * ROW_TILE
    padded = slot_count * slot_rows
    head_count = w_qkv.shape[1] // (3 * DH)
    score_scale = 1.0 / math.sqrt(DH)

    def pad_rows(rows):
        rows = rows.reshape(slot_count, SEQ, rows.shape[1])
        rows = jnp.pad(rows, ((0, 0), (0, slot_rows - SEQ), (0, 0)))
        return rows.reshape(padded, rows.shape[2])

    def trim_rows(rows):
        rows = rows.reshape(slot_count, slot_rows, rows.shape[1])[:, :SEQ]
        return rows.reshape(row_count, rows.shape[2])

    def own(rows):
        return lax.dynamic_slice_in_dim(rows, me * width, width, rows.ndim - 1)

    padded_index = lax.broadcasted_iota(jnp.int32, (padded, 1), 0)
    live_rows = (
        (padded_index // slot_rows < counts[0]) & (padded_index % slot_rows < SEQ)
    ).astype(jnp.float32)

    early = lax.all_gather(
        jnp.concatenate([w_qkv, w_proj.T], axis=1), "wide", axis=0, tiled=True
    )
    wqkv_full = early[:, : w_qkv.shape[1]]
    wproj_t = early[:, w_qkv.shape[1] :]
    late = lax.all_gather(
        jnp.concatenate([w_fc1, w_fc2.T], axis=1), "wide", axis=0, tiled=True
    )
    wfc1_full = late[:, : w_fc1.shape[1]]
    wfc2_t = late[:, w_fc1.shape[1] :]

    vectors = widen(
        jnp.stack([ln1_gain, ln1_bias, ln2_gain, ln2_bias, proj_bias]), me, size
    )
    gain_one, shift_one, gain_two, shift_two, proj_shift = (vectors[i : i + 1] for i in range(5))

    inputs_whole = widen(pad_rows(inputs), me, size)
    sent2 = widen((live_rows * pad_rows(cotangent).astype(jnp.float32)).astype(jnp.bfloat16), me, size)

    resid = inputs_whole.astype(jnp.float32)
    hat_one, inv_one, normed1 = norm_forward(resid, gain_one, shift_one)
    bias_qv = qv_bias.reshape(head_count, 2, DH)
    bias_full = jnp.stack(
        [bias_qv[:, 0], jnp.zeros_like(bias_qv[:, 0]), bias_qv[:, 1]], axis=1
    ).reshape(1, head_count * 3 * DH)
    qkv_rows = (dot_f32(normed1, wqkv_full) + bias_full).astype(jnp.bfloat16)
    qkv_rows, sent2 = lax.optimization_barrier((qkv_rows, sent2))
    mixed_rows, logsum = attend(qkv_rows, slot_rows, score_scale)
    attn_out = sum_whole(dot_f32(mixed_rows, wproj_t, NT), size) + proj_shift
    resid_mid = resid + live_rows * attn_out
    hat_two, inv_two, normed2 = norm_forward(resid_mid, gain_two, shift_two)
    inner_pre = dot_f32(normed2, wfc1_full) + fc1_bias
    activation = gelu_exact(inner_pre).astype(jnp.bfloat16)

    d_inner = dot_f32(sent2, wfc2_t) * gelu_slope(inner_pre)
    d_inner_b = d_inner.astype(jnp.bfloat16)
    d_norm2 = sum_whole(dot_f32(d_inner_b, wfc1_full, NT), size)
    grad_fc = jnp.concatenate(
        [
            dot_f32(normed2, d_inner_b, TN).astype(jnp.bfloat16),
            dot_f32(sent2, activation, TN).astype(jnp.bfloat16),
        ],
        axis=1,
    )
    d_norm2, _ = lax.optimization_barrier((d_norm2, grad_fc))
    grad_fc = lax.psum_scatter(grad_fc, "wide", scatter_dimension=0, tiled=True)

    mlp_out = sum_own(activation, wfc2_t, me, size, width) + fc2_bias

    full_width = float(width * size)
    scaled = d_norm2 * gain_two
    back_two = inv_two * (
        scaled
        - jnp.sum(scaled, axis=1, keepdims=True) / full_width
        - hat_two * (jnp.sum(scaled * hat_two, axis=1, keepdims=True) / full_width)
    )
    own_norm2 = own(d_norm2)
    grad_ln2_gain = jnp.sum(own_norm2 * own(hat_two), axis=0)
    grad_ln2_bias = jnp.sum(own_norm2, axis=0)
    own_cot = pad_rows(cotangent).astype(jnp.float32)
    masked1 = live_rows * (sent2.astype(jnp.float32) + back_two)
    own_mid = own_cot + own(back_two)
    sent1 = masked1.astype(jnp.bfloat16)
    d_mixed = dot_f32(sent1, wproj_t).astype(jnp.bfloat16)
    d_qkv_b, qkv_sums = attend_backward(
        qkv_rows, mixed_rows, d_mixed, logsum, slot_rows, score_scale
    )
    d_qkv_b, mlp_out = lax.optimization_barrier((d_qkv_b, mlp_out))
    output = trim_rows((own(resid_mid) + live_rows * mlp_out).astype(jnp.bfloat16))
    grad_attn = jnp.concatenate(
        [
            dot_f32(normed1, d_qkv_b, TN).astype(jnp.bfloat16),
            dot_f32(sent1, mixed_rows, TN).astype(jnp.bfloat16),
        ],
        axis=1,
    )
    grad_attn, grad_fc = lax.optimization_barrier((grad_attn, grad_fc))
    grad_attn = lax.psum_scatter(grad_attn, "wide", scatter_dimension=0, tiled=True)
    qkv_sums = jnp.sum(qkv_sums[:, 0], axis=0).reshape(head_count, 3, DH)
    grad_qv_bias = jnp.stack([qkv_sums[:, 0], qkv_sums[:, 2]], axis=1).reshape(-1)

    part1 = dot_f32(d_qkv_b, wqkv_full, NT)
    scaled_part = part1 * gain_one
    row_sums = jnp.stack([jnp.sum(scaled_part, axis=1), jnp.sum(scaled_part * hat_one, axis=1)])
    if size == 2:
        row_sums = row_sums + swap(row_sums)
        moved = swap(
            lax.dynamic_slice_in_dim(part1, (1 - me) * width, width, 1).astype(jnp.bfloat16)
        )
        d_norm1 = own(part1) + moved.astype(jnp.float32)
    else:
        row_sums = lax.psum(row_sums, "narrow")
        d_norm1 = lax.psum_scatter(part1, "narrow", scatter_dimension=1, tiled=True)
    own_hat = own(hat_one)
    back_one = inv_one * (
        d_norm1 * ln1_gain
        - row_sums[0][:, None] / full_width
        - own_hat * (row_sums[1][:, None] / full_width)
    )
    grad_in = trim_rows((own_mid + back_one).astype(jnp.bfloat16))

    vectors_out = [
        jnp.sum(d_norm1 * own_hat, axis=0),
        jnp.sum(d_norm1, axis=0),
        grad_qv_bias,
        jnp.sum(own(masked1), axis=0),
        grad_ln2_gain,
        grad_ln2_bias,
        jnp.sum(d_inner, axis=0),
        jnp.sum(live_rows * own_cot, axis=0),
    ]
    joined = jnp.concatenate(vectors_out)
    joined = lax.psum(joined.reshape(-1, 128), "wide").reshape(-1)
    summed, at = [], 0
    for vector in vectors_out:
        summed.append(joined[at : at + vector.shape[0]])
        at += vector.shape[0]
    qkv_columns, fc_columns = w_qkv.shape[1], w_fc1.shape[1]
    grad_w_qkv = grad_attn[:, :qkv_columns].astype(jnp.float32)
    grad_w_proj = grad_attn[:, qkv_columns:].T.astype(jnp.float32)
    grad_w_fc1 = grad_fc[:, :fc_columns].astype(jnp.float32)
    grad_w_fc2 = grad_fc[:, fc_columns:].T.astype(jnp.float32)
    return (
        output,
        grad_in,
        summed[0],
        summed[1],
        grad_w_qkv,
        summed[2],
        grad_w_proj,
        summed[3],
        summed[4],
        summed[5],
        grad_w_fc1,
        summed[6],
        grad_w_fc2,
        summed[7],
    )


def row_mask(info_ref, img, rows):
    index = lax.broadcasted_iota(jnp.int32, (rows, 1), 0)
    return ((index < SEQ) & (info_ref[1] > img)).astype(jnp.float32)


def halves(info_ref, own_ref, other_ref):
    first = info_ref[0] == 0
    own, other = own_ref[...].astype(jnp.float32), other_ref[...].astype(jnp.float32)
    return jnp.where(first, own, other), jnp.where(first, other, own)


def norm_halves(low, high):
    width = float(low.shape[1] * 2)
    center = (jnp.sum(low, axis=1, keepdims=True) + jnp.sum(high, axis=1, keepdims=True)) / width
    squares = jnp.sum(low * low, axis=1, keepdims=True) + jnp.sum(high * high, axis=1, keepdims=True)
    inv_std = lax.rsqrt(squares / width - center * center + norm_eps)
    return (low - center) * inv_std, (high - center) * inv_std, inv_std


def mask_keys(scores):
    edge = SEQ // 8 * 8
    tail = scores[edge:]
    index = lax.broadcasted_iota(jnp.int32, tail.shape, 0)
    return jnp.concatenate([scores[:edge], jnp.where(index < SEQ - edge, tail, -1e30)], axis=0)


def fwd_kernel(
    info, own, other, gain, shift, wqkv, bias, wproj, normed, qkv, mixed, logsum, part, held,
    *, heads, score_scale,
):
    step, steps = pl.program_id(0), held.shape[0]
    half = own.shape[1]

    @pl.when(step == 0)
    def _():
        low, high, _ = norm_halves(*halves(info, own, other))
        for at, hat in ((0, low), (half, high)):
            cols = slice(at, at + half)
            normed[:, cols] = (hat * gain[:, cols] + shift[:, cols]).astype(jnp.bfloat16)

    block = (dot_f32(normed[...], wqkv[...]) + bias[...]).astype(jnp.bfloat16)
    qkv[...] = block
    for head in range(heads):
        base = head * 3 * DH
        queries = block[:, base : base + DH]
        key_rows = block[:, base + DH : base + 2 * DH]
        value_rows = block[:, base + 2 * DH : base + 3 * DH]
        scores = mask_keys(dot_f32(key_rows, queries * score_scale, NT))
        top = jnp.max(scores, axis=0, keepdims=True)
        exp_scores = jnp.exp(scores - top)
        total = jnp.sum(exp_scores, axis=0, keepdims=True)
        probs = (exp_scores * (1.0 / total)).astype(jnp.bfloat16)
        made = jnp.transpose(dot_f32(value_rows, probs, TN)).astype(jnp.bfloat16)
        mixed[:, head * DH : (head + 1) * DH] = made
        logsum[0, head : head + 1, :] = top + jnp.log(total)
    held[step] = mixed[...]

    @pl.when(step == steps - 1)
    def _():
        whole = jnp.concatenate([held[at] for at in range(steps)], axis=1)
        part[...] = dot_f32(whole, wproj[...], NT).astype(jnp.bfloat16)


def mlp_kernel(
    info, own, other, cot_own, cot_other, mine, theirs, proj_shift, gain, shift, out_shift,
    w1, b1, w2, normed, sent, act, d_inner, d_sum, hat, inv, d_part, out_base, out_sent,
    d_acc, m_acc, *, img,
):
    step, steps = pl.program_id(0), pl.num_programs(0)
    rows, half = own.shape
    first = info[0] == 0

    @pl.when(step == 0)
    def _():
        live = row_mask(info, img, rows)
        low, high = halves(info, own, other)
        attn = mine[...].astype(jnp.float32) + theirs[...].astype(jnp.float32) + proj_shift[...]
        low = low + live * attn[:, :half]
        high = high + live * attn[:, half:]
        out_base[...] = jnp.where(first, low, high)
        low, high, inv_std = norm_halves(low, high)
        inv[...] = inv_std
        cot = halves(info, cot_own, cot_other)
        for at, part, grad in ((0, low, cot[0]), (half, high, cot[1])):
            cols = slice(at, at + half)
            hat[:, cols] = part
            normed[:, cols] = (part * gain[:, cols] + shift[:, cols]).astype(jnp.bfloat16)
            sent[:, cols] = (live * grad).astype(jnp.bfloat16)
        d_acc[...] = jnp.zeros_like(d_acc)
        m_acc[...] = jnp.zeros_like(m_acc)

    inner = dot_f32(normed[...], w1[...]) + b1[...]
    cdf = normal_cdf(inner)
    made = (inner * cdf).astype(jnp.bfloat16)
    act[...] = made
    slope = cdf + inner * jnp.exp(-0.5 * inner * inner) * (1.0 / math.sqrt(2.0 * math.pi))
    grad = dot_f32(sent[...], w2[...]) * slope
    d_sum[...] = jnp.sum(grad, axis=0, keepdims=True)
    grad = grad.astype(jnp.bfloat16)
    d_inner[...] = grad
    d_acc[...] += dot_f32(grad, w1[...], NT)
    m_acc[...] += dot_f32(made, w2[...], NT)

    @pl.when(step == steps - 1)
    def _():
        d_part[...] = d_acc[...].astype(jnp.bfloat16)
        low, high = m_acc[:, :half], m_acc[:, half:]
        live = row_mask(info, img, rows)
        out_base[...] += live * (jnp.where(first, low, high) + out_shift[...])
        out_sent[...] = (live * jnp.where(first, high, low)).astype(jnp.bfloat16)


def bwd_kernel(
    info, own, other, cot_own, cot_other, mine, theirs, gain2, gain1, hat, inv, wproj, qkv, mixed,
    logsum, wqkv, sent, d_qkv, sums, mid, sum_gain, sum_bias, sum_proj, d_own, d_sent, hat_own,
    inv_one, row_sums, sum_hat, sum_plain, d_mixed, acc, *, img, heads, score_scale,
):
    step, steps = pl.program_id(0), pl.num_programs(0)
    rows, half = own.shape
    full_width = float(2 * half)
    first = info[0] == 0

    @pl.when(step == 0)
    def _():
        live = row_mask(info, img, rows)
        grad = mine[...].astype(jnp.float32) + theirs[...].astype(jnp.float32)
        scaled = grad * gain2[...]
        back = inv[...] * (
            scaled
            - jnp.sum(scaled, axis=1, keepdims=True) / full_width
            - hat[...] * (jnp.sum(scaled * hat[...], axis=1, keepdims=True) / full_width)
        )
        sum_gain[...] = jnp.sum(grad * hat[...], axis=0, keepdims=True)
        sum_bias[...] = jnp.sum(grad, axis=0, keepdims=True)
        low, high = halves(info, cot_own, cot_other)
        low, high = low + back[:, :half], high + back[:, half:]
        mid[...] = jnp.where(first, low, high)
        for at, part in ((0, low), (half, high)):
            cols = slice(at, at + half)
            masked = live * part
            sum_proj[:, cols] = jnp.sum(masked, axis=0, keepdims=True)
            sent[:, cols] = masked.astype(jnp.bfloat16)
        made = dot_f32(sent[...], wproj[...]).astype(jnp.bfloat16)
        for at in range(d_mixed.shape[0]):
            d_mixed[at] = made[:, at * heads * DH : (at + 1) * heads * DH]
        acc[...] = jnp.zeros_like(acc)

    for head in range(heads):
        base = head * 3 * DH
        queries = qkv[:, base : base + DH]
        key_rows = qkv[:, base + DH : base + 2 * DH]
        value_rows = qkv[:, base + 2 * DH : base + 3 * DH]
        out = mixed[:, head * DH : (head + 1) * DH]
        d_out = d_mixed[step, :, head * DH : (head + 1) * DH]
        products = d_out.astype(jnp.float32) * out.astype(jnp.float32)
        delta = jnp.sum(jnp.transpose(products), axis=0, keepdims=True)
        scores = mask_keys(dot_f32(key_rows, queries * score_scale, NT))
        probs = jnp.exp(scores - logsum[0, head : head + 1, :])
        d_probs = dot_f32(value_rows, d_out, NT)
        d_scores = (probs * (d_probs - delta)).astype(jnp.bfloat16)
        d_query = jnp.transpose(dot_f32(key_rows, d_scores, TN)) * score_scale
        d_keys = dot_f32(d_scores, queries, NN) * score_scale
        d_values = dot_f32(probs.astype(jnp.bfloat16), d_out, NN)
        for at, grad in enumerate((d_query, d_keys, d_values)):
            cols = slice(base + at * DH, base + (at + 1) * DH)
            d_qkv[:, cols] = grad.astype(jnp.bfloat16)
            sums[:, cols] = jnp.sum(grad, axis=0, keepdims=True)
    acc[...] += dot_f32(d_qkv[...], wqkv[...], NT)

    @pl.when(step == steps - 1)
    def _():
        low, high, inv_std = norm_halves(*halves(info, own, other))
        inv_one[...] = inv_std
        hat_own[...] = jnp.where(first, low, high)
        left, right = acc[:, :half], acc[:, half:]
        d_own[...] = jnp.where(first, left, right)
        d_sent[...] = jnp.where(first, right, left).astype(jnp.bfloat16)
        for at, grad, part in ((0, left, low), (half, right, high)):
            columns = slice(at, at + half)
            sum_hat[:, columns] = jnp.sum(grad * part, axis=0, keepdims=True)
            sum_plain[:, columns] = jnp.sum(grad, axis=0, keepdims=True)
        left, right = left * gain1[:, :half], right * gain1[:, half:]
        plain = jnp.sum(left, axis=1, keepdims=True) + jnp.sum(right, axis=1, keepdims=True)
        hatted = jnp.sum(left * low, axis=1, keepdims=True) + jnp.sum(
            right * high, axis=1, keepdims=True
        )
        lane = lax.broadcasted_iota(jnp.int32, (rows, 128), 1)
        both = jnp.where(lane == 0, plain, jnp.where(lane == 1, hatted, 0.0))
        row_sums[...] = jnp.transpose(both)[:8]


def pair_grad_kernel(left0, left1, right0, right1, more0, more1, rest0, rest1, out, held, *, cut):
    step = pl.program_id(0)

    def load(one, two):
        held[...] = jnp.concatenate([one[...], two[...]], axis=0)

    def make(one, two):
        right = jnp.concatenate([one[...], two[...]], axis=0)
        out[...] = dot_f32(held[...], right, TN).astype(jnp.bfloat16)

    pl.when(step == 0)(lambda: load(left0, left1))
    pl.when(step == cut)(lambda: load(more0, more1))
    pl.when(step < cut)(lambda: make(right0, right1))
    pl.when(step >= cut)(lambda: make(rest0, rest1))


SCALARS = pl.BlockSpec(memory_space=pltpu.SMEM)
PARAMS = pltpu.CompilerParams(vmem_limit_bytes=48 * 1024 * 1024)


def whole(shape):
    return pl.BlockSpec(shape, lambda s: (0,) * len(shape), pipeline_mode=pl.Buffered(1))


def cols(rows, width, start=0):
    return pl.BlockSpec((rows, width), lambda s: (0, start + s))


def cost(flops, moved):
    return pl.CostEstimate(flops=flops, bytes_accessed=moved, transcendentals=0)


def shaped(*shapes):
    return [jax.ShapeDtypeStruct(shape, kind) for shape, kind in shapes]


F32, BF16 = jnp.float32, jnp.bfloat16


def forward(info, own, other, gain, shift, early, bias, score_scale):
    rows, half = own.shape
    wide, total = early.shape
    inner = total - bias.shape[1]
    heads = 2
    steps = inner // (heads * DH)
    span = heads * 3 * DH
    return pl.pallas_call(
        functools.partial(fwd_kernel, heads=heads, score_scale=score_scale),
        grid=(steps,),
        in_specs=[
            SCALARS, whole((rows, half)), whole((rows, half)), whole((1, wide)), whole((1, wide)),
            cols(wide, span), cols(1, span),
            pl.BlockSpec((wide, inner), lambda s: (0, bias.shape[1] // inner)),
        ],
        out_specs=[
            whole((rows, wide)), cols(rows, span), cols(rows, heads * DH),
            pl.BlockSpec((1, 8, rows), lambda s: (s, 0, 0)), whole((rows, wide)),
        ],
        out_shape=shaped(
            ((rows, wide), BF16), ((rows, steps * span), BF16), ((rows, inner), BF16),
            ((steps, 8, rows), F32), ((rows, wide), BF16),
        ),
        scratch_shapes=[pltpu.VMEM((steps, rows, heads * DH), BF16)],
        compiler_params=PARAMS,
        cost_estimate=cost(3_000_000_000, 3_000_000),
        name="attention_forward",
    )(info, own, other, gain, shift, early, bias, early)


def mlp_pass(info, img, own, other, cot_own, cot_other, mine, theirs, vectors, out_shift, late, b1):
    rows, half = own.shape
    wide = late.shape[0]
    hidden = b1.shape[1]
    tile = 512
    steps = hidden // tile
    proj_shift, gain, shift = vectors
    return pl.pallas_call(
        functools.partial(mlp_kernel, img=img),
        grid=(steps,),
        in_specs=[
            SCALARS, *[whole((rows, half))] * 4, *[whole((rows, wide))] * 2, *[whole((1, wide))] * 3,
            whole((1, half)), cols(wide, tile), cols(1, tile), cols(wide, tile, steps),
        ],
        out_specs=[
            whole((rows, wide)), whole((rows, wide)), cols(rows, tile), cols(rows, tile),
            cols(1, tile), whole((rows, wide)), whole((rows, 1)), whole((rows, wide)),
            whole((rows, half)), whole((rows, half)),
        ],
        out_shape=shaped(
            ((rows, wide), BF16), ((rows, wide), BF16), ((rows, hidden), BF16),
            ((rows, hidden), BF16), ((1, hidden), F32), ((rows, wide), F32), ((rows, 1), F32),
            ((rows, wide), BF16), ((rows, half), F32), ((rows, half), BF16),
        ),
        scratch_shapes=[pltpu.VMEM((rows, wide), F32), pltpu.VMEM((rows, wide), F32)],
        compiler_params=PARAMS,
        cost_estimate=cost(4_000_000_000, 8_000_000),
        name="feed_forward",
    )(info, own, other, cot_own, cot_other, mine, theirs, proj_shift, gain, shift, out_shift,
      late, b1, late)


def backward(
    info, img, own, other, cot_own, cot_other, mine, theirs, gain2, gain1, hat, inv, early, qkv,
    mixed, logsum, score_scale,
):
    rows, half = own.shape
    wide = early.shape[0]
    inner = mixed.shape[1]
    heads = 2
    steps = inner // (heads * DH)
    span = heads * 3 * DH
    return pl.pallas_call(
        functools.partial(bwd_kernel, img=img, heads=heads, score_scale=score_scale),
        grid=(steps,),
        in_specs=[
            SCALARS, *[whole((rows, half))] * 4, *[whole((rows, wide))] * 2, *[whole((1, wide))] * 2,
            whole((rows, wide)), whole((rows, 1)),
            pl.BlockSpec((wide, inner), lambda s: (0, qkv.shape[1] // inner)),
            cols(rows, span), cols(rows, heads * DH),
            pl.BlockSpec((1, 8, rows), lambda s: (s, 0, 0)), cols(wide, span),
        ],
        out_specs=[
            whole((rows, wide)), cols(rows, span), cols(1, span), whole((rows, half)),
            whole((1, wide)), whole((1, wide)), whole((1, wide)), whole((rows, half)),
            whole((rows, half)), whole((rows, half)), whole((rows, 1)), whole((8, rows)),
            whole((1, wide)), whole((1, wide)),
        ],
        out_shape=shaped(
            ((rows, wide), BF16), ((rows, 3 * inner), BF16), ((1, 3 * inner), F32),
            ((rows, half), F32), ((1, wide), F32), ((1, wide), F32), ((1, wide), F32),
            ((rows, half), F32), ((rows, half), BF16), ((rows, half), F32), ((rows, 1), F32),
            ((8, rows), F32), ((1, wide), F32), ((1, wide), F32),
        ),
        scratch_shapes=[
            pltpu.VMEM((steps, rows, heads * DH), BF16), pltpu.VMEM((rows, wide), F32)
        ],
        compiler_params=PARAMS,
        cost_estimate=cost(5_000_000_000, 8_000_000),
        name="attention_backward",
    )(info, own, other, cot_own, cot_other, mine, theirs, gain2, gain1, hat, inv, early, qkv, mixed,
      logsum, early)


def pair_grads(lefts, rights, mores, rests, tile=512):
    rows, wide = lefts[0].shape
    first, second = rights[0].shape[1] // tile, rests[0].shape[1] // tile
    left = whole((rows, wide))
    right = pl.BlockSpec((rows, tile), lambda s: (0, jnp.minimum(s, first - 1)))
    rest = pl.BlockSpec((rows, tile), lambda s: (0, jnp.maximum(s - first, 0)))
    return pl.pallas_call(
        functools.partial(pair_grad_kernel, cut=first),
        grid=(first + second,),
        in_specs=[left, left, right, right, left, left, rest, rest],
        out_specs=cols(wide, tile),
        out_shape=jax.ShapeDtypeStruct((wide, (first + second) * tile), BF16),
        scratch_shapes=[pltpu.VMEM((2 * rows, wide), BF16)],
        compiler_params=PARAMS,
        cost_estimate=cost(rows * wide * (first + second) * tile, 5_000_000),
        name="weight_gradients",
    )(*lefts, *rights, *mores, *rests)


MESH = pl.DeviceIdType.MESH


def place():
    index = lax.axis_index("wide")
    return index, lax.div(index, 4), lax.rem(lax.div(index, 2), 2), lax.rem(index, 2)


def greet(partners):
    barrier = pltpu.get_barrier_semaphore()
    count = 0
    for when, device in partners:
        def signal(device=device):
            pl.semaphore_signal(barrier, inc=1, device_id=device, device_id_type=MESH)

        if when is None:
            signal()
            count = count + 1
        else:
            pl.when(when)(signal)
            count = count + when.astype(jnp.int32)
    pl.semaphore_wait(barrier, count)


def gather_kernel(shard, *refs, deep, extra):
    rows, out, moved = refs[:extra], refs[extra], refs[extra + 1 : 2 * extra + 1]
    here_sem, send_sem, recv_sem, x_send, x_recv = refs[2 * extra + 1 :]
    index, z, y, core = place()
    across = {"narrow": 1 - lax.axis_index("narrow")}
    beside, near = index + 2 - 4 * y, index + 1 - 2 * core
    more, less = z + 1 < deep, z > 0
    greet([
        (None, across), (None, {"wide": beside}), (None, {"wide": near}),
        (more, {"wide": index + 4}), (less, {"wide": index - 4}),
    ])
    sent = []

    def build(owner, way, target, source):
        return pltpu.make_async_remote_copy(
            src_ref=source, dst_ref=out.at[owner], send_sem=send_sem.at[owner, way],
            recv_sem=recv_sem.at[owner], device_id={"wide": target}, device_id_type=MESH,
        )

    def guarded(when, step):
        if when is None:
            step()
        else:
            pl.when(when)(step)

    def send(when, owner, way, target, source=None):
        source = out.at[owner] if source is None else source
        guarded(when, lambda: build(owner, way, target, source).start())
        sent.append((when, owner, way, target, source))

    def arrive(when, owner):
        guarded(when, lambda: build(owner, 0, near, out.at[owner]).wait_recv())

    swaps = [
        pltpu.make_async_remote_copy(
            src_ref=source, dst_ref=target, send_sem=x_send.at[at], recv_sem=x_recv.at[at],
            device_id=across, device_id_type=MESH,
        )
        for at, (source, target) in enumerate(zip(rows, moved))
    ]
    send(more, index, 0, index + 4, shard)
    send(less, index, 1, index - 4, shard)
    send(None, index, 2, beside, shard)
    send(None, index, 3, near, shard)
    for copy in swaps:
        copy.start()
    here = pltpu.make_async_copy(shard, out.at[index], here_sem)
    here.start()
    for step in range(1, deep):
        for sign, way, onward in ((-1, 0, more), (1, 1, less)):
            owner = index + 4 * sign * step
            holds = z >= step if sign < 0 else z + step < deep
            arrive(holds, owner)
            send(holds & onward, owner, way, index - 4 * sign)
            send(holds, owner, 2, beside)
            send(holds, owner, 3, near)
        owner = beside
        for owner, holds in (
            [(beside, None)] if step == 1 else []
        ) + [(beside - 4 * step, z >= step), (beside + 4 * step, z + step < deep)]:
            arrive(holds, owner)
            send(holds, owner, 3, near)
    base = 1 - core
    for other in range(2 * deep):
        arrive(None, 2 * other + base)
    for copy in swaps:
        copy.wait()
    here.wait()
    for when, owner, way, target, source in sent:
        guarded(when, lambda: build(owner, way, target, source).wait_send())


def gather_early(shard, rows):
    count, extra = lax.axis_size("wide"), len(rows)
    anywhere = pl.BlockSpec(memory_space=pl.ANY)
    dma = pltpu.SemaphoreType.DMA
    out, *moved = pl.pallas_call(
        functools.partial(gather_kernel, deep=count // 4, extra=extra),
        in_specs=[anywhere] * (1 + extra),
        out_specs=[anywhere] * (1 + extra),
        out_shape=[jax.ShapeDtypeStruct((count, *shard.shape), shard.dtype)]
        + [jax.ShapeDtypeStruct(part.shape, part.dtype) for part in rows],
        scratch_shapes=[dma, dma((count, 4)), dma((count,)), dma((extra,)), dma((extra,))],
        compiler_params=pltpu.CompilerParams(collective_id=0, has_side_effects=True),
        cost_estimate=cost(15_000_000_000, 8_000_000),
        name="gather_early",
    )(shard, *rows)
    return out.reshape(count * shard.shape[0], shard.shape[1]), moved


def scatter_kernel(
    normed0, normed1, d_qkv0, d_qkv1, sent0, sent1, mixed0, mixed1, vector, out, vector_out,
    grads, right, right_more, near_in, side_out, side_in, line_out, line_in, sums,
    v_near, v_side, v_line, near_send, near_recv, side_send, side_recv, line_send, line_recv,
    v_send, v_recv, *, deep,
):
    index, z, y, core = place()
    beside, near = {"wide": index + 2 - 4 * y}, {"wide": index + 1 - 2 * core}
    more, less = z + 1 < deep, z > 0
    column = lax.rem(index, 4)
    greet([(None, beside), (None, near)] + [
        (z != at, {"wide": 4 * at + column}) for at in range(deep)
    ])

    def remote(source, target, send, recv, device):
        return pltpu.make_async_remote_copy(
            src_ref=source, dst_ref=target, send_sem=send, recv_sem=recv, device_id=device,
            device_id_type=MESH,
        )

    def add(*parts):
        return functools.reduce(lambda a, b: a + b, [part.astype(jnp.float32) for part in parts])

    order = [at for pair in zip(range(deep - 1, -1, -1), range(deep)) for at in pair][:deep]

    def to_near(at, side):
        slot = 2 * at + side
        copy = remote(
            grads.at[2 * slot + 1 - core], near_in.at[slot], near_send.at[slot],
            near_recv.at[slot], near,
        )
        return copy

    near_copies, side_copies = {}, {}
    v_copy = remote(vector, v_near, v_send.at[0], v_recv.at[0], near)
    v_copy.start()
    right[...] = jnp.concatenate([d_qkv0[...], d_qkv1[...]], axis=0)
    right_more[...] = jnp.concatenate([mixed0[...], mixed1[...]], axis=0)
    rows, split = grads.shape[1], right.shape[1]

    def make(at):
        columns = slice(4 * rows * at, 4 * rows * (at + 1))
        left = jnp.concatenate([normed0[:, columns], normed1[:, columns]], axis=0)
        more = jnp.concatenate([sent0[:, columns], sent1[:, columns]], axis=0)
        wide = dot_f32(left, right[...], TN).astype(jnp.bfloat16)
        rest = dot_f32(more, right_more[...], TN).astype(jnp.bfloat16)
        for piece in range(4):
            cut = slice(piece * rows, (piece + 1) * rows)
            grads[4 * at + piece, :, :split] = wide[cut]
            grads[4 * at + piece, :, split:] = rest[cut]

    def push(at):
        slot = 2 * at + 1 - y
        near_copies[0, at].wait_recv()
        side_out[at] = add(grads[2 * slot + core], near_in[slot]).astype(jnp.bfloat16)
        side_copies[at] = remote(
            side_out.at[at], side_in.at[at], side_send.at[at], side_recv.at[at], beside
        )
        side_copies[at].start()

    for place_in, at in enumerate(order):
        make(at)
        for part, side in ((0, 1 - y), (1, y)):
            near_copies[part, at] = to_near(at, side)
            near_copies[part, at].start()
        if place_in == 0:
            v_copy.wait()
            v_near[...] += vector[...]
            v_copy = remote(v_near, v_side, v_send.at[1], v_recv.at[1], beside)
            v_copy.start()
        else:
            push(order[place_in - 1])
    push(order[-1])
    v_copy.wait()
    v_line[z] = v_near[...] + v_side[...]
    v_pushes = [
        (z != at, remote(v_line.at[z], v_line.at[z], v_send.at[2 + at], v_recv.at[2 + z],
                         {"wide": 4 * at + column}))
        for at in range(deep)
    ]
    for when, copy in v_pushes:
        pl.when(when)(copy.start)

    def hop(at, way):
        slot = at * 2 + way
        return remote(
            line_out.at[at], line_in.at[slot], line_send.at[at], line_recv.at[slot],
            {"wide": index + (4 if way == 0 else -4)},
        )

    for at in order:
        slot = 2 * at + y
        near_copies[1, at].wait_recv()
        side_copies[at].wait_recv()
        sums[at] = add(grads[2 * slot + core], near_in[slot], side_in[at])
        for way, goes, joins in ((0, z < at, z > 0), (1, z > at, z < deep - 1)):
            @pl.when(goes & joins)
            def _(way=way):
                hop(at, way).wait_recv()
                line_out[at] = (sums[at] + line_in[2 * at + way].astype(jnp.float32)).astype(
                    jnp.bfloat16
                )
                hop(at, way).start()

            @pl.when(goes & ~joins)
            def _(way=way):
                line_out[at] = sums[at].astype(jnp.bfloat16)
                hop(at, way).start()

    for at in range(deep):
        @pl.when(z == at)
        def _():
            out[...] = sums[at]
            if at > 0:
                hop(at, 0).wait_recv()
                out[...] += line_in[2 * at].astype(jnp.float32)
            if at < deep - 1:
                hop(at, 1).wait_recv()
                out[...] += line_in[2 * at + 1].astype(jnp.float32)

        @pl.when(z != at)
        def _():
            hop(at, 0).wait_send()
            remote(v_line.at[at], v_line.at[at], v_send.at[2 + at], v_recv.at[2 + at],
                   near).wait_recv()
            remote(v_line.at[z], v_line.at[z], v_send.at[2 + at], v_recv.at[2 + z],
                   near).wait_send()
    total = v_line[0]
    for at in range(1, deep):
        total = total + v_line[at]
    vector_out[...] = total
    for copy in near_copies.values():
        copy.wait_send()
    for copy in side_copies.values():
        copy.wait_send()


def scatter_late(normed, d_qkv, sent, mixed, vector):
    count = lax.axis_size("wide")
    deep = count // 4
    tall, split = d_qkv[0].shape
    more = mixed[0].shape[1]
    rows, width = normed[0].shape[1] // count, split + more
    block = (rows, width)
    inside = pl.BlockSpec(memory_space=pltpu.VMEM)
    dma = pltpu.SemaphoreType.DMA
    return pl.pallas_call(
        functools.partial(scatter_kernel, deep=deep),
        in_specs=[inside] * 9,
        out_specs=[inside] * 2,
        out_shape=shaped((block, F32), (vector.shape, F32)),
        scratch_shapes=[
            pltpu.VMEM((count, *block), BF16), pltpu.VMEM((2 * tall, split), BF16),
            pltpu.VMEM((2 * tall, more), BF16),
            pltpu.VMEM((2 * deep, *block), BF16), pltpu.VMEM((deep, *block), BF16),
            pltpu.VMEM((deep, *block), BF16), pltpu.VMEM((deep, *block), BF16),
            pltpu.VMEM((2 * deep, *block), BF16), pltpu.VMEM((deep, *block), F32),
            pltpu.VMEM(vector.shape, F32), pltpu.VMEM(vector.shape, F32),
            pltpu.VMEM((deep, *vector.shape), F32),
            dma((2 * deep,)), dma((2 * deep,)), dma((deep,)), dma((deep,)), dma((deep,)),
            dma((2 * deep,)), dma((2 + deep,)), dma((2 + deep,)),
        ],
        compiler_params=pltpu.CompilerParams(
            collective_id=1, has_side_effects=True, vmem_limit_bytes=48 * 1024 * 1024
        ),
        cost_estimate=cost(15_000_000_000, 12_000_000),
        name="scatter_late",
    )(*normed, *d_qkv, *sent, *mixed, vector)


def shards_pair(
    inputs, counts, ln1_gain, ln1_bias, w_qkv, qv_bias, w_proj, proj_bias, ln2_gain, ln2_bias,
    w_fc1, fc1_bias, w_fc2, fc2_bias, cotangent,
):
    me = lax.axis_index("narrow")
    row_count, half = inputs.shape
    images = row_count // SEQ
    rows = -(-SEQ // ROW_TILE) * ROW_TILE
    head_count = w_qkv.shape[1] // (3 * DH)
    score_scale = 1.0 / math.sqrt(DH)
    span = range(images)
    info = jnp.stack([me.astype(jnp.int32), counts[0]])

    def slot(array, img):
        return jnp.pad(array[img * SEQ : (img + 1) * SEQ], ((0, rows - SEQ), (0, 0)))

    def own(vector):
        return lax.dynamic_slice_in_dim(vector, me * half, half, vector.ndim - 1)

    mine = [slot(inputs, i) for i in span]
    vectors = jnp.stack([ln1_gain, ln1_bias, ln2_gain, ln2_bias, proj_bias] + [proj_bias] * 3)
    late = lax.all_gather(jnp.concatenate([w_fc1, w_fc2.T], axis=1), "wide", axis=0, tiled=True)
    cot = [slot(cotangent, i) for i in span]
    early, moved = gather_early(jnp.concatenate([w_qkv, w_proj.T], axis=1), mine + cot + [vectors])
    theirs, cot_theirs = moved[:images], moved[images : 2 * images]
    vectors = jnp.concatenate(
        [jnp.where(me == 0, vectors, moved[-1]), jnp.where(me == 0, moved[-1], vectors)], axis=1
    )
    gain_one, shift_one, gain_two, shift_two, proj_shift = (vectors[i : i + 1] for i in range(5))

    bias_qv = qv_bias.reshape(head_count, 2, DH)
    bias_full = jnp.stack(
        [bias_qv[:, 0], jnp.zeros_like(bias_qv[:, 0]), bias_qv[:, 1]], axis=1
    ).reshape(1, head_count * 3 * DH)

    front = [
        forward(info, mine[i], theirs[i], gain_one, shift_one, early, bias_full, score_scale)
        for i in span
    ]
    normed1, qkv, mixed, logsum, part = zip(*front)
    part_theirs = [swap(x) for x in part]
    middle = [
        mlp_pass(
            info, i, mine[i], theirs[i], cot[i], cot_theirs[i], part[i], part_theirs[i],
            (proj_shift, gain_two, shift_two), fc2_bias.reshape(1, -1), late,
            fc1_bias.reshape(1, -1),
        )
        for i in span
    ]
    normed2, sent2, act, d_inner, d_sum, hat2, inv2, d_part, out_base, out_sent = zip(*middle)
    d_theirs = [swap(x) for x in d_part]
    out_theirs = [swap(x) for x in out_sent]
    grad_fc = pair_grads(normed2, d_inner, sent2, act)
    d_theirs[0], grad_fc = lax.optimization_barrier((d_theirs[0], grad_fc))
    grad_fc = lax.psum_scatter(grad_fc, "wide", scatter_dimension=0, tiled=True)
    ends = [
        backward(
            info, i, mine[i], theirs[i], cot[i], cot_theirs[i], d_part[i], d_theirs[i], gain_two,
            gain_one, hat2[i], inv2[i], early, qkv[i], mixed[i], logsum[i], score_scale,
        )
        for i in span
    ]
    (sent1, d_qkv, qkv_sums, mid, sum_gain, sum_bias, sum_proj, d_own, d_sent, hat_own, inv_one,
     row_sums, sum_hat, sum_plain) = zip(*ends)
    d_moved = [swap(x) for x in d_sent]
    row_sums = [x + swap(x) for x in row_sums]
    d_qkv, out_theirs = lax.optimization_barrier((d_qkv, out_theirs))

    qkv_sums = sum(qkv_sums).reshape(head_count, 3, DH)
    grad_qv = jnp.stack([qkv_sums[:, 0], qkv_sums[:, 2]], axis=1).reshape(-1)
    own_cot = sum(
        jnp.sum(jnp.where(counts[0] > i, cot[i].astype(F32), 0.0), axis=0) for i in span
    )
    first_sums = jnp.concatenate([sum(sum_hat), sum(sum_plain)], axis=0)
    first_sums = first_sums + swap(first_sums)
    joined = jnp.concatenate(
        [
            grad_qv, own(sum(sum_proj))[0], own(sum(sum_gain))[0], own(sum(sum_bias))[0],
            sum(d_sum)[0], own_cot, own(first_sums).reshape(-1),
        ]
    )
    grad_attn, joined = scatter_late(normed1, d_qkv, sent1, mixed, joined.reshape(-1, 128))
    joined = joined.reshape(-1)

    output = jnp.concatenate(
        [(out_base[i] + out_theirs[i].astype(F32)).astype(BF16)[:SEQ] for i in span], axis=0
    )
    full_width = float(2 * half)
    grads_in = []
    for i in span:
        d_norm1 = d_own[i] + d_moved[i].astype(F32)
        back = inv_one[i] * (
            d_norm1 * ln1_gain
            - row_sums[i][0][:, None] / full_width
            - hat_own[i] * (row_sums[i][1][:, None] / full_width)
        )
        grads_in.append((mid[i] + back).astype(BF16)[:SEQ])
    grad_in = jnp.concatenate(grads_in, axis=0)
    qv, ff = grad_qv.shape[0], fc1_bias.shape[0]
    edges = [0]
    for extent in (qv, half, half, half, ff, half, half, half):
        edges.append(edges[-1] + extent)
    pieces = [joined[a:b] for a, b in zip(edges[:-1], edges[1:])]
    split_attn, split_fc = w_qkv.shape[1], w_fc1.shape[1]
    return (
        output,
        grad_in,
        pieces[6],
        pieces[7],
        grad_attn[:, :split_attn],
        pieces[0],
        grad_attn[:, split_attn:].T,
        pieces[1],
        pieces[2],
        pieces[3],
        grad_fc[:, :split_fc].astype(F32),
        pieces[4],
        grad_fc[:, split_fc:].T.astype(F32),
        pieces[5],
    )


def shards(*arrays):
    if lax.axis_size("narrow") == 2:
        return shards_pair(*arrays)
    return shards_any(*arrays)


def solution(mesh):
    return jax.shard_map(
        shards,
        mesh=mesh,
        in_specs=(
            P("wide", "narrow"),
            P("wide"),
            P("narrow"),
            P("narrow"),
            P("wide", "narrow"),
            P("narrow"),
            P("narrow", "wide"),
            P("narrow"),
            P("narrow"),
            P("narrow"),
            P("wide", "narrow"),
            P("narrow"),
            P("narrow", "wide"),
            P("narrow"),
            P("wide", "narrow"),
        ),
        out_specs=(
            P("wide", "narrow"),
            P("wide", "narrow"),
            P("narrow"),
            P("narrow"),
            P("wide", "narrow"),
            P("narrow"),
            P("narrow", "wide"),
            P("narrow"),
            P("narrow"),
            P("narrow"),
            P("wide", "narrow"),
            P("narrow"),
            P("narrow", "wide"),
            P("narrow"),
        ),
        check_vma=False,
    )
```

```python
import functools
import math

import jax
import jax.numpy as jnp
from jax import lax
from jax.experimental import pallas as pl
from jax.experimental.pallas import tpu as pltpu
from jax.sharding import PartitionSpec as P

DH = 64
SEQ = 577
ROW_TILE = 16


norm_eps = 1e-06
NT = (((1,), (1,)), ((), ()))
TN = (((0,), (0,)), ((), ()))
NN = (((1,), (0,)), ((), ()))


def dot_f32(left_mat, right_mat, dims=NN):
    return lax.dot_general(left_mat, right_mat, dims, preferred_element_type=jnp.float32)


def swap(piece):
    return lax.ppermute(piece, "narrow", ((0, 1), (1, 0)))


def widen(piece, me, size):
    if size != 2:
        return lax.all_gather(piece, "narrow", axis=1, tiled=True)
    other = swap(piece)
    return jnp.concatenate(
        [jnp.where(me == 0, piece, other), jnp.where(me == 0, other, piece)], axis=1
    )


def sum_whole(partial_rows, size):
    if size != 2:
        return lax.psum(partial_rows, "narrow")
    mine = partial_rows.astype(jnp.bfloat16)
    return mine.astype(jnp.float32) + swap(mine).astype(jnp.float32)


def sum_own(left_mat, right_rows, me, size, width):
    if size != 2:
        return lax.psum_scatter(
            dot_f32(left_mat, right_rows, NT), "narrow", scatter_dimension=1, tiled=True
        )
    theirs = lax.dynamic_slice_in_dim(right_rows, (1 - me) * width, width, 0)
    ours = lax.dynamic_slice_in_dim(right_rows, me * width, width, 0)
    moved = swap(dot_f32(left_mat, theirs, NT).astype(jnp.bfloat16))
    return dot_f32(left_mat, ours, NT) + moved.astype(jnp.float32)


def normal_cdf(values_in):
    return 0.5 * (1.0 + lax.erf(values_in * (1.0 / math.sqrt(2.0))))


def gelu_exact(values_in):
    return values_in * normal_cdf(values_in)


def gelu_slope(values_in):
    return normal_cdf(values_in) + values_in * jnp.exp(-0.5 * values_in * values_in) * (
        1.0 / math.sqrt(2.0 * math.pi)
    )


def norm_forward(rows_in, gain_vec, shift_vec):
    width = float(rows_in.shape[1])
    center = jnp.sum(rows_in, axis=1, keepdims=True) / width
    spread = jnp.sum(rows_in * rows_in, axis=1, keepdims=True) / width - center * center
    inv_std = lax.rsqrt(spread + norm_eps)
    normalized = (rows_in - center) * inv_std
    return (normalized, inv_std, (normalized * gain_vec + shift_vec).astype(jnp.bfloat16))


def scores_by_key(queries, key_rows, score_scale):
    scores = dot_f32(key_rows, queries, NT) * score_scale
    key_index = lax.broadcasted_iota(jnp.int32, scores.shape, 0)
    return jnp.where(key_index < SEQ, scores, -1e30)


def attend_kernel(qkv_ref, mixed_ref, logsum_ref, *, heads, score_scale):
    for head in range(heads):
        base = head * 3 * DH
        queries = qkv_ref[:, base : base + DH]
        key_rows = qkv_ref[:, base + DH : base + 2 * DH]
        value_rows = qkv_ref[:, base + 2 * DH : base + 3 * DH]
        scores = scores_by_key(queries, key_rows, score_scale)
        top = jnp.max(scores, axis=0, keepdims=True)
        exp_scores = jnp.exp(scores - top)
        total = jnp.sum(exp_scores, axis=0, keepdims=True)
        probs = (exp_scores * (1.0 / total)).astype(jnp.bfloat16)
        mixed_ref[:, head * DH : (head + 1) * DH] = dot_f32(probs, value_rows, TN).astype(
            jnp.bfloat16
        )
        logsum_ref[0, head : head + 1, :] = top + jnp.log(total)


def attend_back_kernel(
    qkv_ref, mixed_ref, d_mixed_ref, logsum_ref, d_qkv_ref, sums_ref, *, heads, score_scale
):
    for head in range(heads):
        base = head * 3 * DH
        queries = qkv_ref[:, base : base + DH]
        key_rows = qkv_ref[:, base + DH : base + 2 * DH]
        value_rows = qkv_ref[:, base + 2 * DH : base + 3 * DH]
        mixed = mixed_ref[:, head * DH : (head + 1) * DH]
        d_mixed = d_mixed_ref[:, head * DH : (head + 1) * DH]
        products = d_mixed.astype(jnp.float32) * mixed.astype(jnp.float32)
        delta = jnp.sum(jnp.transpose(products), axis=0, keepdims=True)
        scores = scores_by_key(queries, key_rows, score_scale)
        probs = jnp.exp(scores - logsum_ref[0, head : head + 1, :])
        d_probs = dot_f32(value_rows, d_mixed, NT)
        d_scores = (probs * (d_probs - delta)).astype(jnp.bfloat16)
        d_query = dot_f32(d_scores, key_rows, TN) * score_scale
        d_keys = dot_f32(d_scores, queries, NN) * score_scale
        d_values = dot_f32(probs.astype(jnp.bfloat16), d_mixed, NN)
        for part, grad in enumerate((d_query, d_keys, d_values)):
            columns = slice(base + part * DH, base + (part + 1) * DH)
            d_qkv_ref[:, columns] = grad.astype(jnp.bfloat16)
            sums_ref[0, :, columns] = jnp.broadcast_to(
                jnp.sum(grad, axis=0, keepdims=True), (8, DH)
            )


def head_pairs(width):
    heads = 2
    return heads, width // (3 * DH * heads)


def attend(qkv_rows, slot_rows, score_scale):
    row_count, width = qkv_rows.shape
    slots = row_count // slot_rows
    heads, pairs = head_pairs(width)
    return pl.pallas_call(
        functools.partial(attend_kernel, heads=heads, score_scale=score_scale),
        grid=(slots, pairs),
        in_specs=[pl.BlockSpec((slot_rows, heads * 3 * DH), lambda s, p: (s, p))],
        out_specs=[
            pl.BlockSpec((slot_rows, heads * DH), lambda s, p: (s, p)),
            pl.BlockSpec((1, 8, slot_rows), lambda s, p: (s * pairs + p, 0, 0)),
        ],
        out_shape=[
            jax.ShapeDtypeStruct((row_count, width // 3), jnp.bfloat16),
            jax.ShapeDtypeStruct((slots * pairs, 8, slot_rows), jnp.float32),
        ],
        cost_estimate=pl.CostEstimate(
            flops=4 * slots * pairs * heads * slot_rows * slot_rows * 256,
            bytes_accessed=row_count * width * 3,
            transcendentals=slots * pairs * heads * slot_rows * slot_rows,
        ),
        name="attend",
    )(qkv_rows)


def attend_backward(qkv_rows, mixed_rows, d_mixed, logsum, slot_rows, score_scale):
    row_count, width = qkv_rows.shape
    slots = row_count // slot_rows
    heads, pairs = head_pairs(width)
    narrow_block = pl.BlockSpec((slot_rows, heads * DH), lambda s, p: (s, p))
    wide_block = pl.BlockSpec((slot_rows, heads * 3 * DH), lambda s, p: (s, p))
    return pl.pallas_call(
        functools.partial(attend_back_kernel, heads=heads, score_scale=score_scale),
        grid=(slots, pairs),
        in_specs=[
            wide_block,
            narrow_block,
            narrow_block,
            pl.BlockSpec((1, 8, slot_rows), lambda s, p: (s * pairs + p, 0, 0)),
        ],
        out_specs=[
            wide_block,
            pl.BlockSpec((1, 8, heads * 3 * DH), lambda s, p: (s, 0, p)),
        ],
        out_shape=[
            jax.ShapeDtypeStruct((row_count, width), jnp.bfloat16),
            jax.ShapeDtypeStruct((slots, 8, width), jnp.float32),
        ],
        cost_estimate=pl.CostEstimate(
            flops=10 * slots * pairs * heads * slot_rows * slot_rows * 256,
            bytes_accessed=row_count * width * 6,
            transcendentals=slots * pairs * heads * slot_rows * slot_rows,
        ),
        name="attend_back",
    )(qkv_rows, mixed_rows, d_mixed, logsum)


def shards_any(
    inputs,
    counts,
    ln1_gain,
    ln1_bias,
    w_qkv,
    qv_bias,
    w_proj,
    proj_bias,
    ln2_gain,
    ln2_bias,
    w_fc1,
    fc1_bias,
    w_fc2,
    fc2_bias,
    cotangent,
):
    size = lax.axis_size("narrow")
    me = lax.axis_index("narrow")
    row_count, width = inputs.shape
    slot_count = row_count // SEQ
    slot_rows = -(-SEQ // ROW_TILE) * ROW_TILE
    padded = slot_count * slot_rows
    head_count = w_qkv.shape[1] // (3 * DH)
    score_scale = 1.0 / math.sqrt(DH)

    def pad_rows(rows):
        rows = rows.reshape(slot_count, SEQ, rows.shape[1])
        rows = jnp.pad(rows, ((0, 0), (0, slot_rows - SEQ), (0, 0)))
        return rows.reshape(padded, rows.shape[2])

    def trim_rows(rows):
        rows = rows.reshape(slot_count, slot_rows, rows.shape[1])[:, :SEQ]
        return rows.reshape(row_count, rows.shape[2])

    def own(rows):
        return lax.dynamic_slice_in_dim(rows, me * width, width, rows.ndim - 1)

    padded_index = lax.broadcasted_iota(jnp.int32, (padded, 1), 0)
    live_rows = (
        (padded_index // slot_rows < counts[0]) & (padded_index % slot_rows < SEQ)
    ).astype(jnp.float32)

    early = lax.all_gather(
        jnp.concatenate([w_qkv, w_proj.T], axis=1), "wide", axis=0, tiled=True
    )
    wqkv_full = early[:, : w_qkv.shape[1]]
    wproj_t = early[:, w_qkv.shape[1] :]
    late = lax.all_gather(
        jnp.concatenate([w_fc1, w_fc2.T], axis=1), "wide", axis=0, tiled=True
    )
    wfc1_full = late[:, : w_fc1.shape[1]]
    wfc2_t = late[:, w_fc1.shape[1] :]

    vectors = widen(
        jnp.stack([ln1_gain, ln1_bias, ln2_gain, ln2_bias, proj_bias]), me, size
    )
    gain_one, shift_one, gain_two, shift_two, proj_shift = (vectors[i : i + 1] for i in range(5))

    inputs_whole = widen(pad_rows(inputs), me, size)
    sent2 = widen((live_rows * pad_rows(cotangent).astype(jnp.float32)).astype(jnp.bfloat16), me, size)

    resid = inputs_whole.astype(jnp.float32)
    hat_one, inv_one, normed1 = norm_forward(resid, gain_one, shift_one)
    bias_qv = qv_bias.reshape(head_count, 2, DH)
    bias_full = jnp.stack(
        [bias_qv[:, 0], jnp.zeros_like(bias_qv[:, 0]), bias_qv[:, 1]], axis=1
    ).reshape(1, head_count * 3 * DH)
    qkv_rows = (dot_f32(normed1, wqkv_full) + bias_full).astype(jnp.bfloat16)
    qkv_rows, sent2 = lax.optimization_barrier((qkv_rows, sent2))
    mixed_rows, logsum = attend(qkv_rows, slot_rows, score_scale)
    attn_out = sum_whole(dot_f32(mixed_rows, wproj_t, NT), size) + proj_shift
    resid_mid = resid + live_rows * attn_out
    hat_two, inv_two, normed2 = norm_forward(resid_mid, gain_two, shift_two)
    inner_pre = dot_f32(normed2, wfc1_full) + fc1_bias
    activation = gelu_exact(inner_pre).astype(jnp.bfloat16)

    d_inner = dot_f32(sent2, wfc2_t) * gelu_slope(inner_pre)
    d_inner_b = d_inner.astype(jnp.bfloat16)
    d_norm2 = sum_whole(dot_f32(d_inner_b, wfc1_full, NT), size)
    grad_fc = jnp.concatenate(
        [
            dot_f32(normed2, d_inner_b, TN).astype(jnp.bfloat16),
            dot_f32(sent2, activation, TN).astype(jnp.bfloat16),
        ],
        axis=1,
    )
    d_norm2, _ = lax.optimization_barrier((d_norm2, grad_fc))
    grad_fc = lax.psum_scatter(grad_fc, "wide", scatter_dimension=0, tiled=True)

    mlp_out = sum_own(activation, wfc2_t, me, size, width) + fc2_bias

    full_width = float(width * size)
    scaled = d_norm2 * gain_two
    back_two = inv_two * (
        scaled
        - jnp.sum(scaled, axis=1, keepdims=True) / full_width
        - hat_two * (jnp.sum(scaled * hat_two, axis=1, keepdims=True) / full_width)
    )
    own_norm2 = own(d_norm2)
    grad_ln2_gain = jnp.sum(own_norm2 * own(hat_two), axis=0)
    grad_ln2_bias = jnp.sum(own_norm2, axis=0)
    own_cot = pad_rows(cotangent).astype(jnp.float32)
    masked1 = live_rows * (sent2.astype(jnp.float32) + back_two)
    own_mid = own_cot + own(back_two)
    sent1 = masked1.astype(jnp.bfloat16)
    d_mixed = dot_f32(sent1, wproj_t).astype(jnp.bfloat16)
    d_qkv_b, qkv_sums = attend_backward(
        qkv_rows, mixed_rows, d_mixed, logsum, slot_rows, score_scale
    )
    d_qkv_b, mlp_out = lax.optimization_barrier((d_qkv_b, mlp_out))
    output = trim_rows((own(resid_mid) + live_rows * mlp_out).astype(jnp.bfloat16))
    grad_attn = jnp.concatenate(
        [
            dot_f32(normed1, d_qkv_b, TN).astype(jnp.bfloat16),
            dot_f32(sent1, mixed_rows, TN).astype(jnp.bfloat16),
        ],
        axis=1,
    )
    grad_attn, grad_fc = lax.optimization_barrier((grad_attn, grad_fc))
    grad_attn = lax.psum_scatter(grad_attn, "wide", scatter_dimension=0, tiled=True)
    qkv_sums = jnp.sum(qkv_sums[:, 0], axis=0).reshape(head_count, 3, DH)
    grad_qv_bias = jnp.stack([qkv_sums[:, 0], qkv_sums[:, 2]], axis=1).reshape(-1)

    part1 = dot_f32(d_qkv_b, wqkv_full, NT)
    scaled_part = part1 * gain_one
    row_sums = jnp.stack([jnp.sum(scaled_part, axis=1), jnp.sum(scaled_part * hat_one, axis=1)])
    if size == 2:
        row_sums = row_sums + swap(row_sums)
        moved = swap(
            lax.dynamic_slice_in_dim(part1, (1 - me) * width, width, 1).astype(jnp.bfloat16)
        )
        d_norm1 = own(part1) + moved.astype(jnp.float32)
    else:
        row_sums = lax.psum(row_sums, "narrow")
        d_norm1 = lax.psum_scatter(part1, "narrow", scatter_dimension=1, tiled=True)
    own_hat = own(hat_one)
    back_one = inv_one * (
        d_norm1 * ln1_gain
        - row_sums[0][:, None] / full_width
        - own_hat * (row_sums[1][:, None] / full_width)
    )
    grad_in = trim_rows((own_mid + back_one).astype(jnp.bfloat16))

    vectors_out = [
        jnp.sum(d_norm1 * own_hat, axis=0),
        jnp.sum(d_norm1, axis=0),
        grad_qv_bias,
        jnp.sum(own(masked1), axis=0),
        grad_ln2_gain,
        grad_ln2_bias,
        jnp.sum(d_inner, axis=0),
        jnp.sum(live_rows * own_cot, axis=0),
    ]
    joined = jnp.concatenate(vectors_out)
    joined = lax.psum(joined.reshape(-1, 128), "wide").reshape(-1)
    summed, at = [], 0
    for vector in vectors_out:
        summed.append(joined[at : at + vector.shape[0]])
        at += vector.shape[0]
    qkv_columns, fc_columns = w_qkv.shape[1], w_fc1.shape[1]
    grad_w_qkv = grad_attn[:, :qkv_columns].astype(jnp.float32)
    grad_w_proj = grad_attn[:, qkv_columns:].T.astype(jnp.float32)
    grad_w_fc1 = grad_fc[:, :fc_columns].astype(jnp.float32)
    grad_w_fc2 = grad_fc[:, fc_columns:].T.astype(jnp.float32)
    return (
        output,
        grad_in,
        summed[0],
        summed[1],
        grad_w_qkv,
        summed[2],
        grad_w_proj,
        summed[3],
        summed[4],
        summed[5],
        grad_w_fc1,
        summed[6],
        grad_w_fc2,
        summed[7],
    )


def row_mask(info_ref, img, rows):
    index = lax.broadcasted_iota(jnp.int32, (rows, 1), 0)
    return ((index < SEQ) & (info_ref[1] > img)).astype(jnp.float32)


def halves(info_ref, own_ref, other_ref):
    first = info_ref[0] == 0
    own, other = own_ref[...].astype(jnp.float32), other_ref[...].astype(jnp.float32)
    return jnp.where(first, own, other), jnp.where(first, other, own)


def norm_halves(low, high):
    width = float(low.shape[1] * 2)
    center = (jnp.sum(low, axis=1, keepdims=True) + jnp.sum(high, axis=1, keepdims=True)) / width
    squares = jnp.sum(low * low, axis=1, keepdims=True) + jnp.sum(high * high, axis=1, keepdims=True)
    inv_std = lax.rsqrt(squares / width - center * center + norm_eps)
    return (low - center) * inv_std, (high - center) * inv_std, inv_std


def mask_keys(scores):
    edge = SEQ // 8 * 8
    tail = scores[edge:]
    index = lax.broadcasted_iota(jnp.int32, tail.shape, 0)
    return jnp.concatenate([scores[:edge], jnp.where(index < SEQ - edge, tail, -1e30)], axis=0)


def fwd_kernel(
    info, own, other, gain, shift, wqkv, bias, wproj, *refs, heads, score_scale, moving,
):
    if moving:
        source, normed, qkv, mixed, logsum, part, target, held, send_sem, recv_sem = refs
        side = lax.axis_index("narrow")
        across = {"narrow": 1 - side}
        travel = pltpu.make_async_remote_copy(
            src_ref=source, dst_ref=target, send_sem=send_sem, recv_sem=recv_sem,
            device_id=across, device_id_type=MESH,
        )
    else:
        normed, qkv, mixed, logsum, part, held = refs
        side = info[0]
    step, steps = pl.program_id(0), held.shape[0]
    half = own.shape[1]

    @pl.when(step == 0)
    def _():
        if moving:
            greet([(None, across)])
            travel.start()
        low, high, _ = norm_halves(*halves((side,), own, other))
        for at, hat in ((0, low), (half, high)):
            cols = slice(at, at + half)
            normed[:, cols] = (hat * gain[:, cols] + shift[:, cols]).astype(jnp.bfloat16)

    block = (dot_f32(normed[...], wqkv[...]) + bias[...]).astype(jnp.bfloat16)
    qkv[...] = block
    for head in range(heads):
        base = head * 3 * DH
        queries = block[:, base : base + DH]
        key_rows = block[:, base + DH : base + 2 * DH]
        value_rows = block[:, base + 2 * DH : base + 3 * DH]
        scores = mask_keys(dot_f32(key_rows, queries * score_scale, NT))
        top = jnp.max(scores, axis=0, keepdims=True)
        exp_scores = jnp.exp(scores - top)
        total = jnp.sum(exp_scores, axis=0, keepdims=True)
        probs = (exp_scores * (1.0 / total)).astype(jnp.bfloat16)
        made = jnp.transpose(dot_f32(value_rows, probs, TN)).astype(jnp.bfloat16)
        mixed[:, head * DH : (head + 1) * DH] = made
        logsum[0, head : head + 1, :] = top + jnp.log(total)
    held[step] = mixed[...]

    @pl.when(step == steps - 1)
    def _():
        whole = jnp.concatenate([held[at] for at in range(steps)], axis=1)
        part[...] = dot_f32(whole, wproj[...], NT).astype(jnp.bfloat16)
        if moving:
            travel.wait()


def mlp_kernel(
    info, own, other, cot_own, cot_other, mine, theirs, proj_shift, gain, shift, out_shift,
    w1, b1, w2, normed, sent, act, d_inner, d_sum, hat, inv, d_part, out_base, out_sent,
    d_acc, m_acc, *, img,
):
    step, steps = pl.program_id(0), pl.num_programs(0)
    rows, half = own.shape
    first = info[0] == 0

    @pl.when(step == 0)
    def _():
        live = row_mask(info, img, rows)
        low, high = halves(info, own, other)
        attn = mine[...].astype(jnp.float32) + theirs[...].astype(jnp.float32) + proj_shift[...]
        low = low + live * attn[:, :half]
        high = high + live * attn[:, half:]
        out_base[...] = jnp.where(first, low, high)
        low, high, inv_std = norm_halves(low, high)
        inv[...] = inv_std
        cot = halves(info, cot_own, cot_other)
        for at, part, grad in ((0, low, cot[0]), (half, high, cot[1])):
            cols = slice(at, at + half)
            hat[:, cols] = part
            normed[:, cols] = (part * gain[:, cols] + shift[:, cols]).astype(jnp.bfloat16)
            sent[:, cols] = (live * grad).astype(jnp.bfloat16)
        d_acc[...] = jnp.zeros_like(d_acc)
        m_acc[...] = jnp.zeros_like(m_acc)

    inner = dot_f32(normed[...], w1[...]) + b1[...]
    cdf = normal_cdf(inner)
    made = (inner * cdf).astype(jnp.bfloat16)
    act[...] = made
    slope = cdf + inner * jnp.exp(-0.5 * inner * inner) * (1.0 / math.sqrt(2.0 * math.pi))
    grad = dot_f32(sent[...], w2[...]) * slope
    d_sum[...] = jnp.sum(grad, axis=0, keepdims=True)
    grad = grad.astype(jnp.bfloat16)
    d_inner[...] = grad
    d_acc[...] += dot_f32(grad, w1[...], NT)
    m_acc[...] += dot_f32(made, w2[...], NT)

    @pl.when(step == steps - 1)
    def _():
        d_part[...] = d_acc[...].astype(jnp.bfloat16)
        low, high = m_acc[:, :half], m_acc[:, half:]
        live = row_mask(info, img, rows)
        out_base[...] += live * (jnp.where(first, low, high) + out_shift[...])
        out_sent[...] = (live * jnp.where(first, high, low)).astype(jnp.bfloat16)


def bwd_kernel(
    info, own, other, cot_own, cot_other, mine, theirs, gain2, gain1, hat, inv, wproj, qkv, mixed,
    logsum, wqkv, sent, d_qkv, sums, mid, sum_gain, sum_bias, sum_proj, d_own, d_sent, hat_own,
    inv_one, row_sums, sum_hat, sum_plain, d_mixed, acc, *, img, heads, score_scale,
):
    step, steps = pl.program_id(0), pl.num_programs(0)
    rows, half = own.shape
    full_width = float(2 * half)
    first = info[0] == 0

    @pl.when(step == 0)
    def _():
        live = row_mask(info, img, rows)
        grad = mine[...].astype(jnp.float32) + theirs[...].astype(jnp.float32)
        scaled = grad * gain2[...]
        back = inv[...] * (
            scaled
            - jnp.sum(scaled, axis=1, keepdims=True) / full_width
            - hat[...] * (jnp.sum(scaled * hat[...], axis=1, keepdims=True) / full_width)
        )
        sum_gain[...] = jnp.sum(grad * hat[...], axis=0, keepdims=True)
        sum_bias[...] = jnp.sum(grad, axis=0, keepdims=True)
        low, high = halves(info, cot_own, cot_other)
        low, high = low + back[:, :half], high + back[:, half:]
        mid[...] = jnp.where(first, low, high)
        for at, part in ((0, low), (half, high)):
            cols = slice(at, at + half)
            masked = live * part
            sum_proj[:, cols] = jnp.sum(masked, axis=0, keepdims=True)
            sent[:, cols] = masked.astype(jnp.bfloat16)
        made = dot_f32(sent[...], wproj[...]).astype(jnp.bfloat16)
        for at in range(d_mixed.shape[0]):
            d_mixed[at] = made[:, at * heads * DH : (at + 1) * heads * DH]
        acc[...] = jnp.zeros_like(acc)

    for head in range(heads):
        base = head * 3 * DH
        queries = qkv[:, base : base + DH]
        key_rows = qkv[:, base + DH : base + 2 * DH]
        value_rows = qkv[:, base + 2 * DH : base + 3 * DH]
        out = mixed[:, head * DH : (head + 1) * DH]
        d_out = d_mixed[step, :, head * DH : (head + 1) * DH]
        products = d_out.astype(jnp.float32) * out.astype(jnp.float32)
        delta = jnp.sum(jnp.transpose(products), axis=0, keepdims=True)
        scores = mask_keys(dot_f32(key_rows, queries * score_scale, NT))
        probs = jnp.exp(scores - logsum[0, head : head + 1, :])
        d_probs = dot_f32(value_rows, d_out, NT)
        d_scores = (probs * (d_probs - delta)).astype(jnp.bfloat16)
        d_query = jnp.transpose(dot_f32(key_rows, d_scores, TN)) * score_scale
        d_keys = dot_f32(d_scores, queries, NN) * score_scale
        d_values = dot_f32(probs.astype(jnp.bfloat16), d_out, NN)
        for at, grad in enumerate((d_query, d_keys, d_values)):
            cols = slice(base + at * DH, base + (at + 1) * DH)
            d_qkv[:, cols] = grad.astype(jnp.bfloat16)
            sums[:, cols] = jnp.sum(grad, axis=0, keepdims=True)
    acc[...] += dot_f32(d_qkv[...], wqkv[...], NT)

    @pl.when(step == steps - 1)
    def _():
        low, high, inv_std = norm_halves(*halves(info, own, other))
        inv_one[...] = inv_std
        hat_own[...] = jnp.where(first, low, high)
        left, right = acc[:, :half], acc[:, half:]
        d_own[...] = jnp.where(first, left, right)
        d_sent[...] = jnp.where(first, right, left).astype(jnp.bfloat16)
        for at, grad, part in ((0, left, low), (half, right, high)):
            columns = slice(at, at + half)
            sum_hat[:, columns] = jnp.sum(grad * part, axis=0, keepdims=True)
            sum_plain[:, columns] = jnp.sum(grad, axis=0, keepdims=True)
        left, right = left * gain1[:, :half], right * gain1[:, half:]
        plain = jnp.sum(left, axis=1, keepdims=True) + jnp.sum(right, axis=1, keepdims=True)
        hatted = jnp.sum(left * low, axis=1, keepdims=True) + jnp.sum(
            right * high, axis=1, keepdims=True
        )
        lane = lax.broadcasted_iota(jnp.int32, (rows, 128), 1)
        both = jnp.where(lane == 0, plain, jnp.where(lane == 1, hatted, 0.0))
        row_sums[...] = jnp.transpose(both)[:8]


def pair_grad_kernel(left0, left1, right0, right1, more0, more1, rest0, rest1, out, held, *, cut):
    step = pl.program_id(0)

    def load(one, two):
        held[...] = jnp.concatenate([one[...], two[...]], axis=0)

    def make(one, two):
        right = jnp.concatenate([one[...], two[...]], axis=0)
        out[...] = dot_f32(held[...], right, TN).astype(jnp.bfloat16)

    pl.when(step == 0)(lambda: load(left0, left1))
    pl.when(step == cut)(lambda: load(more0, more1))
    pl.when(step < cut)(lambda: make(right0, right1))
    pl.when(step >= cut)(lambda: make(rest0, rest1))


SCALARS = pl.BlockSpec(memory_space=pltpu.SMEM)
PARAMS = pltpu.CompilerParams(vmem_limit_bytes=48 * 1024 * 1024)
CARRYING = pltpu.CompilerParams(
    vmem_limit_bytes=48 * 1024 * 1024, collective_id=2, has_side_effects=True
)


def whole(shape):
    return pl.BlockSpec(shape, lambda s: (0,) * len(shape), pipeline_mode=pl.Buffered(1))


def cols(rows, width, start=0):
    return pl.BlockSpec((rows, width), lambda s: (0, start + s))


def cost(flops, moved):
    return pl.CostEstimate(flops=flops, bytes_accessed=moved, transcendentals=0)


def shaped(*shapes):
    return [jax.ShapeDtypeStruct(shape, kind) for shape, kind in shapes]


F32, BF16 = jnp.float32, jnp.bfloat16


def forward(info, own, other, gain, shift, early, bias, score_scale, moving=None):
    rows, half = own.shape
    wide, total = early.shape
    inner = total - bias.shape[1]
    heads = 2
    steps = inner // (heads * DH)
    span = heads * 3 * DH
    carried = [] if moving is None else [moving]
    anywhere = [pl.BlockSpec(memory_space=pl.ANY)] * len(carried)
    return pl.pallas_call(
        functools.partial(fwd_kernel, heads=heads, score_scale=score_scale, moving=bool(carried)),
        grid=(steps,),
        in_specs=[
            SCALARS, whole((rows, half)), whole((rows, half)), whole((1, wide)), whole((1, wide)),
            cols(wide, span), cols(1, span),
            pl.BlockSpec((wide, inner), lambda s: (0, bias.shape[1] // inner)),
            *anywhere,
        ],
        out_specs=[
            whole((rows, wide)), cols(rows, span), cols(rows, heads * DH),
            pl.BlockSpec((1, 8, rows), lambda s: (s, 0, 0)), whole((rows, wide)), *anywhere,
        ],
        out_shape=shaped(
            ((rows, wide), BF16), ((rows, steps * span), BF16), ((rows, inner), BF16),
            ((steps, 8, rows), F32), ((rows, wide), BF16),
            *[(array.shape, array.dtype) for array in carried],
        ),
        scratch_shapes=[pltpu.VMEM((steps, rows, heads * DH), BF16)]
        + [pltpu.SemaphoreType.DMA] * (2 * len(carried)),
        compiler_params=CARRYING if carried else PARAMS,
        cost_estimate=cost(3_000_000_000, 3_000_000),
        name="attention_carrying" if carried else "attention_forward",
    )(info, own, other, gain, shift, early, bias, early, *carried)


def mlp_pass(info, img, own, other, cot_own, cot_other, mine, theirs, vectors, out_shift, late, b1):
    rows, half = own.shape
    wide = late.shape[0]
    hidden = b1.shape[1]
    tile = 512
    steps = hidden // tile
    proj_shift, gain, shift = vectors
    return pl.pallas_call(
        functools.partial(mlp_kernel, img=img),
        grid=(steps,),
        in_specs=[
            SCALARS, *[whole((rows, half))] * 4, *[whole((rows, wide))] * 2, *[whole((1, wide))] * 3,
            whole((1, half)), cols(wide, tile), cols(1, tile), cols(wide, tile, steps),
        ],
        out_specs=[
            whole((rows, wide)), whole((rows, wide)), cols(rows, tile), cols(rows, tile),
            cols(1, tile), whole((rows, wide)), whole((rows, 1)), whole((rows, wide)),
            whole((rows, half)), whole((rows, half)),
        ],
        out_shape=shaped(
            ((rows, wide), BF16), ((rows, wide), BF16), ((rows, hidden), BF16),
            ((rows, hidden), BF16), ((1, hidden), F32), ((rows, wide), F32), ((rows, 1), F32),
            ((rows, wide), BF16), ((rows, half), F32), ((rows, half), BF16),
        ),
        scratch_shapes=[pltpu.VMEM((rows, wide), F32), pltpu.VMEM((rows, wide), F32)],
        compiler_params=PARAMS,
        cost_estimate=cost(4_000_000_000, 8_000_000),
        name="feed_forward",
    )(info, own, other, cot_own, cot_other, mine, theirs, proj_shift, gain, shift, out_shift,
      late, b1, late)


def backward(
    info, img, own, other, cot_own, cot_other, mine, theirs, gain2, gain1, hat, inv, early, qkv,
    mixed, logsum, score_scale,
):
    rows, half = own.shape
    wide = early.shape[0]
    inner = mixed.shape[1]
    heads = 2
    steps = inner // (heads * DH)
    span = heads * 3 * DH
    return pl.pallas_call(
        functools.partial(bwd_kernel, img=img, heads=heads, score_scale=score_scale),
        grid=(steps,),
        in_specs=[
            SCALARS, *[whole((rows, half))] * 4, *[whole((rows, wide))] * 2, *[whole((1, wide))] * 2,
            whole((rows, wide)), whole((rows, 1)),
            pl.BlockSpec((wide, inner), lambda s: (0, qkv.shape[1] // inner)),
            cols(rows, span), cols(rows, heads * DH),
            pl.BlockSpec((1, 8, rows), lambda s: (s, 0, 0)), cols(wide, span),
        ],
        out_specs=[
            whole((rows, wide)), cols(rows, span), cols(1, span), whole((rows, half)),
            whole((1, wide)), whole((1, wide)), whole((1, wide)), whole((rows, half)),
            whole((rows, half)), whole((rows, half)), whole((rows, 1)), whole((8, rows)),
            whole((1, wide)), whole((1, wide)),
        ],
        out_shape=shaped(
            ((rows, wide), BF16), ((rows, 3 * inner), BF16), ((1, 3 * inner), F32),
            ((rows, half), F32), ((1, wide), F32), ((1, wide), F32), ((1, wide), F32),
            ((rows, half), F32), ((rows, half), BF16), ((rows, half), F32), ((rows, 1), F32),
            ((8, rows), F32), ((1, wide), F32), ((1, wide), F32),
        ),
        scratch_shapes=[
            pltpu.VMEM((steps, rows, heads * DH), BF16), pltpu.VMEM((rows, wide), F32)
        ],
        compiler_params=PARAMS,
        cost_estimate=cost(5_000_000_000, 8_000_000),
        name="attention_backward",
    )(info, own, other, cot_own, cot_other, mine, theirs, gain2, gain1, hat, inv, early, qkv, mixed,
      logsum, early)


def pair_grads(lefts, rights, mores, rests, tile=512):
    rows, wide = lefts[0].shape
    first, second = rights[0].shape[1] // tile, rests[0].shape[1] // tile
    left = whole((rows, wide))
    right = pl.BlockSpec((rows, tile), lambda s: (0, jnp.minimum(s, first - 1)))
    rest = pl.BlockSpec((rows, tile), lambda s: (0, jnp.maximum(s - first, 0)))
    return pl.pallas_call(
        functools.partial(pair_grad_kernel, cut=first),
        grid=(first + second,),
        in_specs=[left, left, right, right, left, left, rest, rest],
        out_specs=cols(wide, tile),
        out_shape=jax.ShapeDtypeStruct((wide, (first + second) * tile), BF16),
        scratch_shapes=[pltpu.VMEM((2 * rows, wide), BF16)],
        compiler_params=PARAMS,
        cost_estimate=cost(rows * wide * (first + second) * tile, 5_000_000),
        name="weight_gradients",
    )(*lefts, *rights, *mores, *rests)


MESH = pl.DeviceIdType.MESH


def place():
    index = lax.axis_index("wide")
    return index, lax.div(index, 4), lax.rem(lax.div(index, 2), 2), lax.rem(index, 2)


def greet(partners):
    barrier = pltpu.get_barrier_semaphore()
    count = 0
    for when, device in partners:
        def signal(device=device):
            pl.semaphore_signal(barrier, inc=1, device_id=device, device_id_type=MESH)

        if when is None:
            signal()
            count = count + 1
        else:
            pl.when(when)(signal)
            count = count + when.astype(jnp.int32)
    pl.semaphore_wait(barrier, count)


def gather_kernel(shard, *refs, deep, extra):
    rows, out, moved = refs[:extra], refs[extra], refs[extra + 1 : 2 * extra + 1]
    here_sem, send_sem, recv_sem, x_send, x_recv = refs[2 * extra + 1 :]
    index, z, y, core = place()
    across = {"narrow": 1 - lax.axis_index("narrow")}
    beside, near = index + 2 - 4 * y, index + 1 - 2 * core
    more, less = z + 1 < deep, z > 0
    greet([
        (None, across), (None, {"wide": beside}), (None, {"wide": near}),
        (more, {"wide": index + 4}), (less, {"wide": index - 4}),
    ])
    sent = []

    def build(owner, way, target, source):
        return pltpu.make_async_remote_copy(
            src_ref=source, dst_ref=out.at[owner], send_sem=send_sem.at[owner, way],
            recv_sem=recv_sem.at[owner], device_id={"wide": target}, device_id_type=MESH,
        )

    def guarded(when, step):
        if when is None:
            step()
        else:
            pl.when(when)(step)

    def send(when, owner, way, target, source=None):
        source = out.at[owner] if source is None else source
        guarded(when, lambda: build(owner, way, target, source).start())
        sent.append((when, owner, way, target, source))

    def arrive(when, owner):
        guarded(when, lambda: build(owner, 0, near, out.at[owner]).wait_recv())

    swaps = [
        pltpu.make_async_remote_copy(
            src_ref=source, dst_ref=target, send_sem=x_send.at[at], recv_sem=x_recv.at[at],
            device_id=across, device_id_type=MESH,
        )
        for at, (source, target) in enumerate(zip(rows, moved))
    ]
    send(more, index, 0, index + 4, shard)
    send(less, index, 1, index - 4, shard)
    send(None, index, 2, beside, shard)
    send(None, index, 3, near, shard)
    for copy in swaps:
        copy.start()
    here = pltpu.make_async_copy(shard, out.at[index], here_sem)
    here.start()
    for step in range(1, deep):
        for sign, way, onward in ((-1, 0, more), (1, 1, less)):
            owner = index + 4 * sign * step
            holds = z >= step if sign < 0 else z + step < deep
            arrive(holds, owner)
            send(holds & onward, owner, way, index - 4 * sign)
            send(holds, owner, 2, beside)
            send(holds, owner, 3, near)
        owner = beside
        for owner, holds in (
            [(beside, None)] if step == 1 else []
        ) + [(beside - 4 * step, z >= step), (beside + 4 * step, z + step < deep)]:
            arrive(holds, owner)
            send(holds, owner, 3, near)
    base = 1 - core
    for other in range(2 * deep):
        arrive(None, 2 * other + base)
    for copy in swaps:
        copy.wait()
    here.wait()
    for when, owner, way, target, source in sent:
        guarded(when, lambda: build(owner, way, target, source).wait_send())


def gather_early(shard, rows):
    count, extra = lax.axis_size("wide"), len(rows)
    anywhere = pl.BlockSpec(memory_space=pl.ANY)
    dma = pltpu.SemaphoreType.DMA
    out, *moved = pl.pallas_call(
        functools.partial(gather_kernel, deep=count // 4, extra=extra),
        in_specs=[anywhere] * (1 + extra),
        out_specs=[anywhere] * (1 + extra),
        out_shape=[jax.ShapeDtypeStruct((count, *shard.shape), shard.dtype)]
        + [jax.ShapeDtypeStruct(part.shape, part.dtype) for part in rows],
        scratch_shapes=[dma, dma((count, 4)), dma((count,)), dma((extra,)), dma((extra,))],
        compiler_params=pltpu.CompilerParams(collective_id=0, has_side_effects=True),
        cost_estimate=cost(15_000_000_000, 8_000_000),
        name="gather_early",
    )(shard, *rows)
    return out.reshape(count * shard.shape[0], shard.shape[1]), moved


def scatter_kernel(
    normed0, normed1, d_qkv0, d_qkv1, sent0, sent1, mixed0, mixed1, vector, out, vector_out,
    grads, right, right_more, near_in, side_out, side_in, line_out, line_in, sums,
    v_near, v_side, v_line, near_send, near_recv, side_send, side_recv, line_send, line_recv,
    v_send, v_recv, *, deep,
):
    index, z, y, core = place()
    beside, near = {"wide": index + 2 - 4 * y}, {"wide": index + 1 - 2 * core}
    more, less = z + 1 < deep, z > 0
    column = lax.rem(index, 4)
    greet([(None, beside), (None, near)] + [
        (z != at, {"wide": 4 * at + column}) for at in range(deep)
    ])

    def remote(source, target, send, recv, device):
        return pltpu.make_async_remote_copy(
            src_ref=source, dst_ref=target, send_sem=send, recv_sem=recv, device_id=device,
            device_id_type=MESH,
        )

    def add(*parts):
        return functools.reduce(lambda a, b: a + b, [part.astype(jnp.float32) for part in parts])

    order = [at for pair in zip(range(deep - 1, -1, -1), range(deep)) for at in pair][:deep]

    def to_near(at, side):
        slot = 2 * at + side
        copy = remote(
            grads.at[2 * slot + 1 - core], near_in.at[slot], near_send.at[slot],
            near_recv.at[slot], near,
        )
        return copy

    near_copies, side_copies = {}, {}
    v_copy = remote(vector, v_near, v_send.at[0], v_recv.at[0], near)
    v_copy.start()
    right[...] = jnp.concatenate([d_qkv0[...], d_qkv1[...]], axis=0)
    right_more[...] = jnp.concatenate([mixed0[...], mixed1[...]], axis=0)
    rows, split = grads.shape[1], right.shape[1]

    def make(at):
        columns = slice(4 * rows * at, 4 * rows * (at + 1))
        left = jnp.concatenate([normed0[:, columns], normed1[:, columns]], axis=0)
        more = jnp.concatenate([sent0[:, columns], sent1[:, columns]], axis=0)
        wide = dot_f32(left, right[...], TN).astype(jnp.bfloat16)
        rest = dot_f32(more, right_more[...], TN).astype(jnp.bfloat16)
        for piece in range(4):
            cut = slice(piece * rows, (piece + 1) * rows)
            grads[4 * at + piece, :, :split] = wide[cut]
            grads[4 * at + piece, :, split:] = rest[cut]

    def push(at):
        slot = 2 * at + 1 - y
        near_copies[0, at].wait_recv()
        side_out[at] = add(grads[2 * slot + core], near_in[slot]).astype(jnp.bfloat16)
        side_copies[at] = remote(
            side_out.at[at], side_in.at[at], side_send.at[at], side_recv.at[at], beside
        )
        side_copies[at].start()

    for place_in, at in enumerate(order):
        make(at)
        for part, side in ((0, 1 - y), (1, y)):
            near_copies[part, at] = to_near(at, side)
            near_copies[part, at].start()
        if place_in == 0:
            v_copy.wait()
            v_near[...] += vector[...]
            v_copy = remote(v_near, v_side, v_send.at[1], v_recv.at[1], beside)
            v_copy.start()
        else:
            push(order[place_in - 1])
    push(order[-1])
    v_copy.wait()
    v_line[z] = v_near[...] + v_side[...]
    v_pushes = [
        (z != at, remote(v_line.at[z], v_line.at[z], v_send.at[2 + at], v_recv.at[2 + z],
                         {"wide": 4 * at + column}))
        for at in range(deep)
    ]
    for when, copy in v_pushes:
        pl.when(when)(copy.start)

    def hop(at, way):
        slot = at * 2 + way
        return remote(
            line_out.at[at], line_in.at[slot], line_send.at[at], line_recv.at[slot],
            {"wide": index + (4 if way == 0 else -4)},
        )

    for at in order:
        slot = 2 * at + y
        near_copies[1, at].wait_recv()
        side_copies[at].wait_recv()
        sums[at] = add(grads[2 * slot + core], near_in[slot], side_in[at])
        for way, goes, joins in ((0, z < at, z > 0), (1, z > at, z < deep - 1)):
            @pl.when(goes & joins)
            def _(way=way):
                hop(at, way).wait_recv()
                line_out[at] = (sums[at] + line_in[2 * at + way].astype(jnp.float32)).astype(
                    jnp.bfloat16
                )
                hop(at, way).start()

            @pl.when(goes & ~joins)
            def _(way=way):
                line_out[at] = sums[at].astype(jnp.bfloat16)
                hop(at, way).start()

    for at in range(deep):
        @pl.when(z == at)
        def _():
            out[...] = sums[at]
            if at > 0:
                hop(at, 0).wait_recv()
                out[...] += line_in[2 * at].astype(jnp.float32)
            if at < deep - 1:
                hop(at, 1).wait_recv()
                out[...] += line_in[2 * at + 1].astype(jnp.float32)

        @pl.when(z != at)
        def _():
            hop(at, 0).wait_send()
            remote(v_line.at[at], v_line.at[at], v_send.at[2 + at], v_recv.at[2 + at],
                   near).wait_recv()
            remote(v_line.at[z], v_line.at[z], v_send.at[2 + at], v_recv.at[2 + z],
                   near).wait_send()
    total = v_line[0]
    for at in range(1, deep):
        total = total + v_line[at]
    vector_out[...] = total
    for copy in near_copies.values():
        copy.wait_send()
    for copy in side_copies.values():
        copy.wait_send()


def scatter_late(normed, d_qkv, sent, mixed, vector):
    count = lax.axis_size("wide")
    deep = count // 4
    tall, split = d_qkv[0].shape
    more = mixed[0].shape[1]
    rows, width = normed[0].shape[1] // count, split + more
    block = (rows, width)
    inside = pl.BlockSpec(memory_space=pltpu.VMEM)
    dma = pltpu.SemaphoreType.DMA
    return pl.pallas_call(
        functools.partial(scatter_kernel, deep=deep),
        in_specs=[inside] * 9,
        out_specs=[inside] * 2,
        out_shape=shaped((block, F32), (vector.shape, F32)),
        scratch_shapes=[
            pltpu.VMEM((count, *block), BF16), pltpu.VMEM((2 * tall, split), BF16),
            pltpu.VMEM((2 * tall, more), BF16),
            pltpu.VMEM((2 * deep, *block), BF16), pltpu.VMEM((deep, *block), BF16),
            pltpu.VMEM((deep, *block), BF16), pltpu.VMEM((deep, *block), BF16),
            pltpu.VMEM((2 * deep, *block), BF16), pltpu.VMEM((deep, *block), F32),
            pltpu.VMEM(vector.shape, F32), pltpu.VMEM(vector.shape, F32),
            pltpu.VMEM((deep, *vector.shape), F32),
            dma((2 * deep,)), dma((2 * deep,)), dma((deep,)), dma((deep,)), dma((deep,)),
            dma((2 * deep,)), dma((2 + deep,)), dma((2 + deep,)),
        ],
        compiler_params=pltpu.CompilerParams(
            collective_id=1, has_side_effects=True, vmem_limit_bytes=48 * 1024 * 1024
        ),
        cost_estimate=cost(15_000_000_000, 12_000_000),
        name="scatter_late",
    )(*normed, *d_qkv, *sent, *mixed, vector)


def shards_pair(
    inputs, counts, ln1_gain, ln1_bias, w_qkv, qv_bias, w_proj, proj_bias, ln2_gain, ln2_bias,
    w_fc1, fc1_bias, w_fc2, fc2_bias, cotangent,
):
    me = lax.axis_index("narrow")
    row_count, half = inputs.shape
    images = row_count // SEQ
    rows = -(-SEQ // ROW_TILE) * ROW_TILE
    head_count = w_qkv.shape[1] // (3 * DH)
    score_scale = 1.0 / math.sqrt(DH)
    span = range(images)
    info = jnp.stack([me.astype(jnp.int32), counts[0]])

    def slot(array, img):
        return jnp.pad(array[img * SEQ : (img + 1) * SEQ], ((0, rows - SEQ), (0, 0)))

    def own(vector):
        return lax.dynamic_slice_in_dim(vector, me * half, half, vector.ndim - 1)

    mine = [slot(inputs, i) for i in span]
    vectors = jnp.stack([ln1_gain, ln1_bias, ln2_gain, ln2_bias, proj_bias] + [proj_bias] * 3)
    late = lax.all_gather(jnp.concatenate([w_fc1, w_fc2.T], axis=1), "wide", axis=0, tiled=True)
    cot = [slot(cotangent, i) for i in span]
    early, moved = gather_early(jnp.concatenate([w_qkv, w_proj.T], axis=1), mine + cot[:-1] + [vectors])
    theirs, cot_theirs = moved[:images], moved[images:-1]
    vectors = jnp.concatenate(
        [jnp.where(me == 0, vectors, moved[-1]), jnp.where(me == 0, moved[-1], vectors)], axis=1
    )
    gain_one, shift_one, gain_two, shift_two, proj_shift = (vectors[i : i + 1] for i in range(5))

    bias_qv = qv_bias.reshape(head_count, 2, DH)
    bias_full = jnp.stack(
        [bias_qv[:, 0], jnp.zeros_like(bias_qv[:, 0]), bias_qv[:, 1]], axis=1
    ).reshape(1, head_count * 3 * DH)

    *ahead, last = forward(
        info, mine[0], theirs[0], gain_one, shift_one, early, bias_full, score_scale, cot[-1]
    )
    cot_theirs = cot_theirs + [last]
    front = [ahead] + [
        forward(info, mine[i], theirs[i], gain_one, shift_one, early, bias_full, score_scale)
        for i in span[1:]
    ]
    normed1, qkv, mixed, logsum, part = zip(*front)
    part_theirs = [swap(x) for x in part]
    middle = [
        mlp_pass(
            info, i, mine[i], theirs[i], cot[i], cot_theirs[i], part[i], part_theirs[i],
            (proj_shift, gain_two, shift_two), fc2_bias.reshape(1, -1), late,
            fc1_bias.reshape(1, -1),
        )
        for i in span
    ]
    normed2, sent2, act, d_inner, d_sum, hat2, inv2, d_part, out_base, out_sent = zip(*middle)
    d_theirs = [swap(x) for x in d_part]
    out_theirs = [swap(x) for x in out_sent]
    grad_fc = pair_grads(normed2, d_inner, sent2, act)
    d_theirs[0], grad_fc = lax.optimization_barrier((d_theirs[0], grad_fc))
    grad_fc = lax.psum_scatter(grad_fc, "wide", scatter_dimension=0, tiled=True)
    ends = [
        backward(
            info, i, mine[i], theirs[i], cot[i], cot_theirs[i], d_part[i], d_theirs[i], gain_two,
            gain_one, hat2[i], inv2[i], early, qkv[i], mixed[i], logsum[i], score_scale,
        )
        for i in span
    ]
    (sent1, d_qkv, qkv_sums, mid, sum_gain, sum_bias, sum_proj, d_own, d_sent, hat_own, inv_one,
     row_sums, sum_hat, sum_plain) = zip(*ends)
    d_moved = [swap(x) for x in d_sent]
    row_sums = [x + swap(x) for x in row_sums]
    d_qkv, out_theirs = lax.optimization_barrier((d_qkv, out_theirs))

    qkv_sums = sum(qkv_sums).reshape(head_count, 3, DH)
    grad_qv = jnp.stack([qkv_sums[:, 0], qkv_sums[:, 2]], axis=1).reshape(-1)
    own_cot = sum(
        jnp.sum(jnp.where(counts[0] > i, cot[i].astype(F32), 0.0), axis=0) for i in span
    )
    first_sums = jnp.concatenate([sum(sum_hat), sum(sum_plain)], axis=0)
    first_sums = first_sums + swap(first_sums)
    joined = jnp.concatenate(
        [
            grad_qv, own(sum(sum_proj))[0], own(sum(sum_gain))[0], own(sum(sum_bias))[0],
            sum(d_sum)[0], own_cot, own(first_sums).reshape(-1),
        ]
    )
    grad_attn, joined = scatter_late(normed1, d_qkv, sent1, mixed, joined.reshape(-1, 128))
    joined = joined.reshape(-1)

    output = jnp.concatenate(
        [(out_base[i] + out_theirs[i].astype(F32)).astype(BF16)[:SEQ] for i in span], axis=0
    )
    full_width = float(2 * half)
    grads_in = []
    for i in span:
        d_norm1 = d_own[i] + d_moved[i].astype(F32)
        back = inv_one[i] * (
            d_norm1 * ln1_gain
            - row_sums[i][0][:, None] / full_width
            - hat_own[i] * (row_sums[i][1][:, None] / full_width)
        )
        grads_in.append((mid[i] + back).astype(BF16)[:SEQ])
    grad_in = jnp.concatenate(grads_in, axis=0)
    qv, ff = grad_qv.shape[0], fc1_bias.shape[0]
    edges = [0]
    for extent in (qv, half, half, half, ff, half, half, half):
        edges.append(edges[-1] + extent)
    pieces = [joined[a:b] for a, b in zip(edges[:-1], edges[1:])]
    split_attn, split_fc = w_qkv.shape[1], w_fc1.shape[1]
    return (
        output,
        grad_in,
        pieces[6],
        pieces[7],
        grad_attn[:, :split_attn],
        pieces[0],
        grad_attn[:, split_attn:].T,
        pieces[1],
        pieces[2],
        pieces[3],
        grad_fc[:, :split_fc].astype(F32),
        pieces[4],
        grad_fc[:, split_fc:].T.astype(F32),
        pieces[5],
    )


def shards(*arrays):
    if lax.axis_size("narrow") == 2:
        return shards_pair(*arrays)
    return shards_any(*arrays)


def solution(mesh):
    return jax.shard_map(
        shards,
        mesh=mesh,
        in_specs=(
            P("wide", "narrow"),
            P("wide"),
            P("narrow"),
            P("narrow"),
            P("wide", "narrow"),
            P("narrow"),
            P("narrow", "wide"),
            P("narrow"),
            P("narrow"),
            P("narrow"),
            P("wide", "narrow"),
            P("narrow"),
            P("narrow", "wide"),
            P("narrow"),
            P("wide", "narrow"),
        ),
        out_specs=(
            P("wide", "narrow"),
            P("wide", "narrow"),
            P("narrow"),
            P("narrow"),
            P("wide", "narrow"),
            P("narrow"),
            P("narrow", "wide"),
            P("narrow"),
            P("narrow"),
            P("narrow"),
            P("wide", "narrow"),
            P("narrow"),
            P("narrow", "wide"),
            P("narrow"),
        ),
        check_vma=False,
    )
```
